32 devices in a mesh: dp: 8 (over z, y), fsdp: 4 (over x, core).
Axes of the slice: x: 2, y: 2, z: 4, core: 2. Of those that a mesh axis runs over, the one named last changes fastest.
Arguments:
- tokens: bfloat16 [8192, 1024], P(('dp', 'fsdp')), may hold values from -6 to 6
- cotangent: bfloat16 [8192, 1024], P(('dp', 'fsdp')), may hold values from -6 to 6
- master: float32 [12597248], P(('dp', 'fsdp')), may hold values from -4 to 4
- first_moment: float32 [12597248], P(('dp', 'fsdp')), may hold values from -2.5 to 2.5
- second_moment: float32 [12597248], P(('dp', 'fsdp')), may hold values from 0.33 to 1.3
- average: float32 [12597248], P(('dp', 'fsdp')), may hold values from -0.5 to 0.5
- timestep: int32 [8], P('dp'), may hold values from 1 to 5000
- block_length: int32 [8], P('dp'), may hold values from 10 to 50, as said below
- block_start: int32 [8], P('dp'), may hold values from 0 to 974
Outputs:
- block_out: bfloat16 [8192, 1024], P(('dp', 'fsdp'))
- input_grad: float32 [8192, 1024], P(('dp', 'fsdp'))
- grad_norm: float32 [], replicated
- vector_grad: float32 [14336], P('fsdp')
- new_first: float32 [12597248], P(('dp', 'fsdp'))
- new_second: float32 [12597248], P(('dp', 'fsdp'))
- new_master: float32 [12597248], P(('dp', 'fsdp'))
- new_average: float32 [12597248], P(('dp', 'fsdp'))
The draws below stay inside these ranges and needn't reach their ends.
Inputs may be any that keep to these rules, and one draw needn't show every extreme that they name: `block_length`: each is 10, 25 or 50; some sequence has 50 and some 10.
All inputs are finite; a program needn't handle non-finite values.
Results may differ from the reference program's by a relative error of at most 0.01225.
The reference program's roundings to bfloat16 on the way count: a program that leaves them out, or rounds other values in their place, can miss the bound.
Values may be sent and summed in bfloat16 or wider, within the bound.
No kernel may reach another device: no remote copies, remote signals or barrier semaphores. Data moves between devices by JAX's collectives and lax.ppermute only.
A program may use at most 192 MiB of HBM per device.

```python
import math
import jax
import jax.numpy as jnp
from jax import lax

D = 1024
H = 16
DH = 64
FF = 4096
STEP = 10
SEQ = 1024
SEQS = 8
TOKENS = 8192
VEC = 14336
PARAMS = 12597248
N_DP = 8
N_FSDP = 4


def param_layout():
    root_d = 1.0 / math.sqrt(D)
    root_ff = 1.0 / math.sqrt(FF)
    return [(D * D, 1.5 * root_d, 0.0), (D * D, 1.5 * root_d, 0.0), (D * D, root_d, 0.0), (D * D, 4.0 * root_d, 0.0), (D * FF, root_d, 0.0), (FF * D, root_ff, 0.0), (D, 0.2, 0.0), (D, 0.2, 0.0), (D, 0.2, 0.0), (D, 0.2, 0.0), (FF, 0.2, 0.0), (D, 0.1, 1.0), (D, 0.2, 0.0), (D, 0.1, 1.0), (D, 0.2, 0.0), (D, 1.0, 0.0), (D, 0.5, 0.0)]


def blocked_table(which):
    layout = param_layout()
    block = jnp.concatenate([jnp.full((amount // N_FSDP,), entry[which], jnp.float32) for amount, *entry in [(a, s, c) for a, s, c in layout]])
    table = jnp.tile(block[None, :], (N_FSDP, 1))
    return table.reshape(N_FSDP, N_DP, -1).transpose(1, 0, 2).reshape(-1)


def param_values(noise_draw):
    return blocked_table(1) + blocked_table(0) * noise_draw


def noise_for(inner_key):
    return jax.random.truncated_normal(inner_key, -4.0, 4.0, (PARAMS,), jnp.float32)


def draw_master(key, part):
    return param_values(noise_for(jax.random.fold_in(key, 11)))


def draw_average(key, part):
    filled = 1.0 - 0.99 ** (STEP - 1)
    return filled * param_values(noise_for(jax.random.fold_in(key, 23)))


def draw_block_length(key, part):
    length_table = jnp.array([10, 25, 50], dtype=jnp.int32)
    pick_index = jax.random.randint(jax.random.fold_in(key, 37), (SEQS,), 0, 3)
    lengths = length_table[pick_index]
    return lengths.at[0].set(50).at[1].set(10)


def set_ends(drawn, key, least, top_value):
    spot = [jax.random.randint(jax.random.fold_in(key, axis), (), 0, length) for axis, length in enumerate(drawn.shape)]
    widest = drawn.shape.index(max(drawn.shape))
    beside = spot[:widest] + [(spot[widest] + 1) % drawn.shape[widest]] + spot[widest + 1:]
    return drawn.at[tuple(spot)].set(least).at[tuple(beside)].set(top_value)


def block_scale(rng, extent, split, least, top_value):
    factor_of = 1.0
    for dim, parts in split:
        heights = jax.random.uniform(jax.random.fold_in(jax.random.fold_in(rng, 6), dim), (parts,), jnp.float32, least / len(split), top_value / len(split))
        factor_of = factor_of * jnp.repeat(jnp.exp(heights), extent[dim] // parts).reshape((-1,) + (1,) * (len(extent) - 1 - dim))
    return factor_of


def gaussian(key, shape, deviation, reach, cuts=(), kind=jnp.bfloat16):
    drawn = jax.random.normal(key, shape, jnp.float32) * deviation
    if len(cuts) > 0:
        drawn = block_scale(key, shape, cuts, -0.22, 0.18) * drawn
    return jnp.clip(drawn, min=-reach, max=reach).astype(kind)


def setup_inputs(seed: int = 0) -> dict:
    splits = jax.random.split(jax.random.key(seed), 10)
    return {
        "tokens": gaussian(splits[0], (TOKENS, D), 1.0, 6.0, ((0, 32),)),
        "cotangent": gaussian(splits[1], (TOKENS, D), 1.0, 6.0, ((0, 32),)),
        "master": draw_master(jax.random.fold_in(splits[9], 71), 0),
        "first_moment": gaussian(splits[3], (PARAMS,), 0.44, 2.5, ((0, 32),), jnp.float32),
        "second_moment": jnp.clip(jnp.exp(math.log(1.3) - 1.3710268 * jax.random.uniform(splits[4], (PARAMS,), jnp.float32) ** block_scale(splits[4], (PARAMS,), ((0, 32),), -0.2, 0.2)), 0.33, 1.3),
        "average": draw_average(jax.random.fold_in(splits[9], 71), 0),
        "timestep": set_ends(jax.random.randint(splits[6], (SEQS,), 1, 5001), jax.random.fold_in(splits[6], 1), 1, 5000).astype(jnp.int32),
        "block_length": draw_block_length(jax.random.fold_in(splits[9], 71), 0),
        "block_start": set_ends(jax.random.randint(splits[8], (SEQS,), 0, SEQ - 49), jax.random.fold_in(splits[8], 1), 0, (SEQ - 49) - 1).astype(jnp.int32),
    }


@jax.custom_vjp
def low(v):
    return lax.optimization_barrier(v.astype(jnp.bfloat16)).astype(jnp.float32)

@jax.custom_vjp
def low_back(v):
    return v

def low_keep(v):
    return (low(v), None)

def low_pass(kept, grad):
    return (grad,)

def back_keep(v):
    return (v, None)

def back_low(kept, grad):
    return (low(grad),)
low.defvjp(low_keep, low_pass)
low_back.defvjp(back_keep, back_low)
NORM_EPS = 1e-05

def matmul(left, right):
    return jnp.dot(left, right, precision=lax.Precision.HIGHEST, preferred_element_type=jnp.float32)

def layer_norm(resid, gain, shift):
    average = lax.optimization_barrier(jnp.mean(resid, axis=-1, keepdims=True))
    centred = resid - average
    variance = lax.optimization_barrier(jnp.mean(centred * centred, axis=-1, keepdims=True))
    return centred * lax.rsqrt(variance + NORM_EPS) * gain + shift

def unpack(flat_params, dp_count, fsdp_count):
    shapes = [(D, D)] * 4 + [(D, FF), (FF, D)] + [(1, D)] * 4 + [(1, FF)] + [(1, D)] * 6
    blocks = flat_params.reshape(dp_count, fsdp_count, -1).transpose(1, 0, 2).reshape(fsdp_count, -1)
    pieces = []
    offset = 0
    for rows, cols in shapes:
        width = rows * (cols // fsdp_count)
        part = blocks[:, offset:offset + width].reshape(fsdp_count, rows, cols // fsdp_count)
        whole = part.transpose(1, 0, 2).reshape(rows, cols)
        pieces.append(whole.reshape(-1) if rows == 1 else whole)
        offset += width
    return pieces

def split_heads(values):
    return values.reshape(values.shape[0], H, DH).transpose(1, 0, 2)

def merge_heads(values):
    return values.transpose(1, 0, 2).reshape(values.shape[1], H * DH)

def one_head(head_item):
    query_h, key_h, value_h = head_item
    scores = low_back(matmul(query_h, key_h.T) * DH ** (-0.5))
    probabilities = jax.nn.softmax(scores, axis=-1)
    return matmul(low(probabilities), value_h)

def forward(inputs, master_flat, timestep, length, start):
    w_query, w_key, w_value, w_out, w_up, w_down, b_query, b_value, b_out, b_down, b_up, gain_attn, shift_attn, gain_ffn, shift_ffn, w_time, b_time = unpack(low(master_flat), N_DP, N_FSDP)
    position = jnp.arange(SEQ, dtype=jnp.int32)
    inside = ((position >= start) & (position < start + length)).astype(jnp.float32)[:, None]
    time_frac = timestep.astype(jnp.float32) / 5000.0
    stream = inputs + inside * (time_frac * w_time + b_time)
    stream_low = low(stream)
    queries = low(low_back(matmul(stream_low, w_query) + b_query))
    keys = low(low_back(matmul(stream_low, w_key)))
    values = low(low_back(matmul(stream_low, w_value) + b_value))
    heads = lax.map(jax.checkpoint(one_head), (split_heads(queries), split_heads(keys), split_heads(values)))
    heads_low = low(low_back(merge_heads(heads)))
    attn = low_back(matmul(heads_low, w_out) + b_out)
    resid_attn = stream + attn
    normed = layer_norm(resid_attn, gain_attn, shift_attn)
    normed_low = low(normed)
    pre_act = low_back(matmul(normed_low, w_up) + b_up)
    hidden = low(jax.nn.gelu(pre_act, approximate=False))
    ffn = low_back(matmul(hidden, w_down) + b_down)
    resid_ffn = normed + ffn
    return layer_norm(resid_ffn, gain_ffn, shift_ffn)

def reference(tokens, cotangent, master, first_moment, second_moment, average, timestep, block_length, block_start):
    inputs = tokens.astype(jnp.float32).reshape(SEQS, SEQ, D)
    cot_all = cotangent.astype(jnp.float32).reshape(SEQS, SEQ, D)

    def per_sequence(grad_total, seq_item):
        input_seq, cot_seq, step_seq, length_seq, start_seq = seq_item

        def apply_layer(input_arg, master_arg):
            return forward(input_arg, master_arg, step_seq, length_seq, start_seq)
        output_seq, pullback = jax.vjp(apply_layer, input_seq, master)
        input_grad_seq, master_grad = pullback(cot_seq)
        return (grad_total + master_grad, (output_seq.astype(jnp.bfloat16), input_grad_seq))
    gradient, (outputs, input_grads) = lax.scan(per_sequence, jnp.zeros((PARAMS,), jnp.float32), (inputs, cot_all, timestep, block_length, block_start))
    owner_blocks = gradient.reshape(N_DP, N_FSDP, -1).transpose(1, 0, 2).reshape(N_FSDP, -1)
    vector_grad = owner_blocks[:, (PARAMS - VEC) // N_FSDP:].reshape(-1)
    grad_norm = jnp.sqrt(jnp.sum(gradient * gradient))
    clip_limit = 4.0 * math.sqrt(PARAMS)
    clipped = gradient * (clip_limit / jnp.maximum(grad_norm, clip_limit))
    new_first = 0.9 * first_moment + 0.1 * clipped
    new_second = 0.98 * second_moment + 0.02 * clipped * clipped
    first_hat = new_first / (1.0 - 0.9 ** STEP)
    second_hat = new_second / (1.0 - 0.98 ** STEP)
    new_master = master - 0.02 * (first_hat / (jnp.sqrt(second_hat) + 1e-06) + 0.01 * master)
    new_average = 0.99 * average + 0.01 * new_master
    return (outputs.reshape(TOKENS, D), input_grads.reshape(TOKENS, D), grad_norm, vector_grad, new_first, new_second, new_master, new_average)
```

```python
from functools import partial
import math

import jax
import jax.numpy as jnp
from jax import lax
from jax.experimental import pallas as pl
from jax.experimental.pallas import tpu as pltpu
from jax.sharding import PartitionSpec as P

D = 1024
H = 16
DH = 64
FF = 4096
STEP = 10
PARAMS = 12597248
NORM_EPS = 1e-05

SHARD = PARAMS // 32
PIECE = 1600
LANE_ROWS = 3080
PAD = 128
TAIL = 1536
REGIONS = (
    ("q", 0, 1024, 256),
    ("k", 262144, 1024, 256),
    ("v", 524288, 1024, 256),
    ("o", 786432, 1024, 256),
    ("up", 1048576, 1024, 1024),
    ("down", 2097152, 4096, 256),
    ("vec", 3145728, 16, 256),
)


def segments(shard):
    low, high = shard * SHARD, (shard + 1) * SHARD
    found, offset = [], 0
    for name, start, rows, width in REGIONS:
        size = 3584 if name == "vec" else rows * width
        first, last = max(low, start), min(high, start + size)
        if first >= last:
            continue
        row_a = (first - start) // width // 16 * 16
        row_b = min(rows, -(-(-(-(last - start) // width)) // 16) * 16)
        found.append((name, row_a, row_b, offset, width // 128, start // 128))
        offset += (row_b - row_a) * (width // 256)
    return found


def lane_start(shard):
    return shard * SHARD // 128


SEGMENTS = [segments(shard) for shard in range(8)]
SLOT = ((0, 3, 2, 1), (1, 0, 3, 2), (1, 3, 0, 2), (1, 2, 3, 0))


def dot(left, right):
    return jnp.dot(left, right, preferred_element_type=jnp.float32)


def dot_last(left, right):
    return lax.dot_general(
        left, right, (((1,), (1,)), ((), ())), preferred_element_type=jnp.float32
    )


def dot_first(left, right):
    return lax.dot_general(
        left, right, (((0,), (0,)), ((), ())), preferred_element_type=jnp.float32
    )


def low(values):
    return values.astype(jnp.bfloat16)


def wide(values):
    return values.astype(jnp.float32)


VMEM = pl.BlockSpec(memory_space=pltpu.VMEM)
SMEM = pl.BlockSpec(memory_space=pltpu.SMEM)
ANY = pl.BlockSpec(memory_space=pl.ANY)


def struct(shape, kind=jnp.bfloat16):
    return jax.ShapeDtypeStruct(shape, kind)


def chunks(rows, most=128):
    return [(a, min(most, rows - a)) for a in range(0, rows, most)]


def pack_kernel(place, flat, piece, rolled, rows):
    shard = place[0]
    rows[0:PAD, :] = jnp.zeros((PAD, 128), jnp.float32)
    rows[PAD + LANE_ROWS : PAD + LANE_ROWS + PAD, :] = jnp.zeros((PAD, 128), jnp.float32)
    rolled[0:8, :] = jnp.zeros((8, 128), jnp.float32)

    @pl.when(shard % 2 == 0)
    def _():
        for a, n in chunks(LANE_ROWS):
            rows[PAD + a : PAD + a + n, :] = flat[a : a + n, :]

    @pl.when(shard % 2 == 1)
    def _():
        for a, n in chunks(LANE_ROWS):
            rolled[8 + a : 8 + a + n, :] = pltpu.roll(flat[a : a + n, :], 64, 1)
        for a, n in chunks(LANE_ROWS):
            lane = lax.broadcasted_iota(jnp.int32, (n, 128), 1)
            rows[PAD + a : PAD + a + n, :] = jnp.where(
                lane < 64, rolled[7 + a : 7 + a + n, :], rolled[8 + a : 8 + a + n, :]
            )

    for case in range(8):

        @pl.when(shard == case)
        def _(case=case):
            for _, row_a, row_b, offset, step, first in SEGMENTS[case]:
                count = row_b - row_a
                base = PAD + first + step * row_a - lane_start(case)
                for t in range(step):
                    out = offset + t // 2 * count
                    lanes = slice(t % 2 * 128, t % 2 * 128 + 128)
                    for a, n in chunks(count):
                        piece[out + a : out + a + n, lanes] = low(
                            rows[pl.ds(base + t + step * a, n, stride=step), :]
                        )


def pack(place, flat):
    return pl.pallas_call(
        pack_kernel,
        out_shape=struct((PIECE, 256)),
        in_specs=[SMEM, VMEM],
        out_specs=VMEM,
        scratch_shapes=[
            pltpu.VMEM((8 + LANE_ROWS, 128), jnp.float32),
            pltpu.VMEM((PAD + LANE_ROWS + PAD, 128), jnp.float32),
        ],
        compiler_params=pltpu.CompilerParams(vmem_limit_bytes=24 << 20),
        name="pack",
    )(place, flat)


def unpack_kernel(place, piece, extra, flat, square, rows):
    shard = place[0]
    for case in range(8):

        @pl.when(shard == case)
        def _(case=case):
            for name, row_a, row_b, offset, step, first in SEGMENTS[case]:
                count = row_b - row_a
                base = PAD + first + step * row_a - lane_start(case)
                for t in range(step):
                    source = offset + t // 2 * count
                    lanes = slice(t % 2 * 128, t % 2 * 128 + 128)
                    for a, n in chunks(count):
                        if name == "vec":
                            value = extra[0:16, lanes]
                        elif name == "o" and case == 1:
                            value = extra[16:32, lanes]
                        else:
                            value = wide(piece[source + a : source + a + n, lanes])
                        rows[pl.ds(base + t + step * a, n, stride=step), :] = value

    square[...] = jnp.zeros_like(square)
    for odd in range(2):

        @pl.when(shard % 2 == odd)
        def _(odd=odd):
            total = jnp.zeros((8, 128), jnp.float32)
            for a, n in chunks(LANE_ROWS):
                value = rows[PAD + a : PAD + a + n, :]
                lane = lax.broadcasted_iota(jnp.int32, (n, 128), 1)
                if odd:
                    after = rows[PAD + a + 1 : PAD + a + 1 + n, :]
                    value = jnp.where(
                        lane < 64, pltpu.roll(value, 64, 1), pltpu.roll(after, 64, 1)
                    )
                if (a + n) * 128 > SHARD:
                    row = lax.broadcasted_iota(jnp.int32, (n, 128), 0) + a
                    value = jnp.where(row * 128 + lane < SHARD, value, 0.0)
                flat[a : a + n, :] = value
                total += jnp.sum((value * value).reshape(n // 8, 8, 128), axis=0)
            square[...] = total


def unpack(place, piece, extra):
    return pl.pallas_call(
        unpack_kernel,
        out_shape=(struct((LANE_ROWS, 128), jnp.float32), struct((8, 128), jnp.float32)),
        in_specs=[SMEM, VMEM, VMEM],
        out_specs=(VMEM, VMEM),
        scratch_shapes=[pltpu.VMEM((PAD + LANE_ROWS + PAD, 128), jnp.float32)],
        compiler_params=pltpu.CompilerParams(vmem_limit_bytes=24 << 20),
        name="unpack",
    )(place, piece, extra)


def column_sum(values):
    return jnp.sum(values, axis=0, keepdims=True)


def inside_column(place, relative):
    rows = lax.broadcasted_iota(jnp.int32, (256, 1), 0)
    position = rows + (place[3] ^ relative) * 256
    return ((position >= place[4]) & (position < place[4] + place[5])).astype(jnp.float32)


def attend_kernel(
    place, t0, t1, t2, t3, embed, bias, s_own, s_other, b_own, b_other,
    stream_out, weight_out, q_out, k_out, v_out, h0, h1, h2, h3, lse_out,
    q_heads, k_heads, v_heads, o_heads, edge, sem,
):
    def copies(first, second):
        return [
            pltpu.make_async_copy(first.at[0:1024, :], weight_out.at[0], sem.at[0]),
            pltpu.make_async_copy(first.at[1024:1552, :], weight_out.at[1, 0:528, :], sem.at[1]),
            pltpu.make_async_copy(second.at[16:512, :], weight_out.at[1, 528:1024, :], sem.at[2]),
            pltpu.make_async_copy(second.at[0:16, :], edge, sem.at[3]),
            pltpu.make_async_copy(second.at[512:1536, :], weight_out.at[2], sem.at[4]),
        ]

    for bottom in range(2):
        for y in range(2):
            own, other = (s_own, s_other) if bottom else (b_own, b_other)
            pair = (other, own) if y else (own, other)

            @pl.when(((place[1] == 0) == bool(bottom)) & (place[2] == y))
            def _(pair=pair):
                for copy in copies(*pair):
                    copy.start()

    for r, tokens in enumerate((t0, t1, t2, t3)):
        stream_out[r] = low(wide(tokens[...]) + inside_column(place, r) * embed[...])
    lanes = lax.broadcasted_iota(jnp.int32, (1024, 128), 1)
    v_heads[...] = jnp.broadcast_to((lanes >= 64).astype(jnp.bfloat16), (4, 1024, 128))
    for copy in copies(s_own, s_other):
        copy.wait()
    weight_out[1, 512:528, :] = weight_out[1, 512:528, :] + edge[...]
    for r in range(4):
        rows = slice(r * 256, r * 256 + 256)
        stream = stream_out[r]
        query = low(dot(stream, weight_out[0]) + bias[0:1, :])
        key = low(dot(stream, weight_out[1]))
        value = low(dot(stream, weight_out[2]) + bias[1:2, :])
        q_out[rows, :] = query
        k_out[rows, :] = key
        v_out[rows, :] = value
        for h in range(4):
            cols = slice(h * 64, h * 64 + 64)
            q_heads[h, rows, :] = query[:, cols] * 0.125
            k_heads[h, rows, :] = key[:, cols]
            v_heads[h, rows, 0:64] = value[:, cols]
    lse_out[...] = jnp.zeros_like(lse_out)

    def step(n, _):
        h, r = n // 4, n % 4
        rows = pl.ds(pl.multiple_of(r * 256, 256), 256)
        scores = dot_last(q_heads[h, rows, :], k_heads[h])
        highest = jnp.max(scores, axis=1, keepdims=True)
        weights = low(jnp.exp(scores - highest))
        result = dot(weights, v_heads[h])
        total = result[:, 64:65]
        o_heads[h, rows, :] = low(result[:, 0:64] / total)
        lane = lax.broadcasted_iota(jnp.int32, (256, 128), 1)
        lse_out[rows, :] = jnp.where(lane == h, highest + jnp.log(total), lse_out[rows, :])
        return 0

    lax.fori_loop(0, 16, step, 0)
    for r, out in enumerate((h0, h1, h2, h3)):
        for h in range(4):
            out[:, h * 64 : h * 64 + 64] = o_heads[h, r * 256 : r * 256 + 256, :]


def attend(place, tokens, embed, bias, pieces):
    square = struct((1024, 256))
    block = struct((256, 256))
    return pl.pallas_call(
        attend_kernel,
        out_shape=(
            struct((4, 256, 1024)), struct((3, 1024, 256)), square, square, square,
            block, block, block, block, struct((1024, 128), jnp.float32),
        ),
        in_specs=[SMEM] + [VMEM] * 6 + [ANY] * 4,
        out_specs=(VMEM,) * 10,
        scratch_shapes=[
            pltpu.VMEM((4, 1024, 64), jnp.bfloat16),
            pltpu.VMEM((4, 1024, 64), jnp.bfloat16),
            pltpu.VMEM((4, 1024, 128), jnp.bfloat16),
            pltpu.VMEM((4, 1024, 64), jnp.bfloat16),
            pltpu.VMEM((16, 256), jnp.bfloat16),
            pltpu.SemaphoreType.DMA((5,)),
        ],
        compiler_params=pltpu.CompilerParams(vmem_limit_bytes=40 << 20),
        name="attend",
    )(place, *tokens, embed, bias, *pieces)


def attend_back_kernel(
    place, q_in, k_in, v_in, lse, weight, g0, g1, g2, g3,
    q_grad, k_grad, v_grad, kept, sent, sums,
    q_heads, k_heads, v_heads, g_heads, dq_heads, dk_heads, dv_heads,
):
    for r, grad in enumerate((g0, g1, g2, g3)):
        rows = slice(r * 256, r * 256 + 256)
        for h in range(4):
            cols = slice(h * 64, h * 64 + 64)
            q_heads[h, rows, :] = q_in[rows, cols] * 0.125
            k_heads[h, rows, :] = k_in[rows, cols]
            v_heads[h, rows, :] = v_in[rows, cols]
            g_heads[h, rows, :] = grad[:, cols]

    def step(n, _):
        h, r = n // 4, n % 4
        rows = pl.ds(pl.multiple_of(r * 256, 256), 256)
        query, grad = q_heads[h, rows, :], g_heads[h, rows, :]
        scores = dot_last(query, k_heads[h])
        lane = lax.broadcasted_iota(jnp.int32, (256, 128), 1)
        logsum = jnp.sum(jnp.where(lane == h, lse[rows, :], 0.0), axis=1, keepdims=True)
        probs = jnp.exp(scores - logsum)
        weighted = probs * dot_last(grad, v_heads[h])
        inner = jnp.sum(weighted, axis=1, keepdims=True)
        score_grad = low(weighted - probs * inner)
        dq_heads[h, rows, :] = low(dot(score_grad, k_heads[h]) * 0.125)
        dk_heads[h] += dot_first(query, score_grad)
        dv_heads[h] += dot_first(grad, low(probs))
        return 0

    dk_heads[...] = jnp.zeros_like(dk_heads)
    dv_heads[...] = jnp.zeros_like(dv_heads)
    lax.fori_loop(0, 16, step, 0)
    for h in range(4):
        cols = slice(h * 64, h * 64 + 64)
        q_grad[:, cols] = dq_heads[h]
        k_grad[:, cols] = low(dk_heads[h].T)
        v_grad[:, cols] = low(dv_heads[h].T)
    sums[...] = jnp.zeros_like(sums)
    sums[1:2, 0:256] = column_sum(wide(q_grad[...]))
    sums[2:3, 0:256] = column_sum(wide(v_grad[...]))
    for r in range(4):
        rows = slice(r * 256, r * 256 + 256)
        part = (
            dot_last(q_grad[rows, :], weight[0])
            + dot_last(k_grad[rows, :], weight[1])
            + dot_last(v_grad[rows, :], weight[2])
        )
        sums[0:1, :] += column_sum(inside_column(place, r) * part)
        if r % 2:
            sent[r // 2] = low(part)
        else:
            kept[r // 2] = part


def attend_back(place, query, key, value, lse, weight, grads):
    square = struct((1024, 256))
    return pl.pallas_call(
        attend_back_kernel,
        out_shape=(
            square, square, square, struct((2, 256, D), jnp.float32), struct((2, 256, D)),
            struct((8, D), jnp.float32),
        ),
        in_specs=[SMEM] + [VMEM] * 9,
        out_specs=(VMEM,) * 6,
        scratch_shapes=[pltpu.VMEM((4, 1024, 64), jnp.bfloat16)] * 5
        + [pltpu.VMEM((4, 64, 1024), jnp.float32)] * 2,
        compiler_params=pltpu.CompilerParams(vmem_limit_bytes=40 << 20),
        name="attend_back",
    )(place, query, key, value, lse, weight, *grads)


def row_mean(values):
    return jnp.sum(values, axis=1, keepdims=True) * (1.0 / D)


def normalise(resid):
    centred = resid - row_mean(resid)
    scale = lax.rsqrt(row_mean(centred * centred) + NORM_EPS)
    return centred * scale, scale


def normalise_back(grad, gain, xhat, scale):
    scaled = grad * gain
    return (scaled - row_mean(scaled) - xhat * row_mean(scaled * xhat)) * scale


def layer_kernel(
    place, h0, h1, h2, h3, tokens, cotangent, embed, vectors, bias_up, out_head, *refs
):
    pieces = refs[:32]
    (block_out, resid_grad, g0, g1, g2, g3, sums, sums_up, head_grad) = refs[32:41]
    grads_own, grads_other = refs[41:44], refs[44:47]
    (w_out, w_up, w_down, edge_up, edge_down, hidden, slope, grad_up, grad_down,
     grad_out, acc, sem, sem_out) = refs[47:]

    def fetch(z, y):
        made = {"out": [], "up": [], "down": []}
        for k in range(1, 4):
            for ry in range(2):
                case = 2 * k + (y ^ ry)
                for r in range(4):
                    rx, rc = r // 2, r % 2
                    source = pieces[rc * 16 + rx * 8 + ry * 4 + SLOT[z][k]]
                    column = place[3] ^ r
                    for name, row_a, row_b, offset, step, _ in SEGMENTS[case]:
                        count = row_b - row_a
                        if name == "o":
                            made["out"].append((source.at[offset : offset + count, :], w_out.at[column]))
                        elif name == "up":
                            block = source.at[offset : offset + 4 * count, :].reshape(4, count, 256)
                            target = w_up.at[pl.ds(column * 4, 4)]
                            skip = 0
                            if row_a:
                                skip = 16
                                made["up"].append(
                                    (block.at[:, 0:16, :], edge_up.at[case - 3, pl.ds(column * 4, 4)])
                                )
                            made["up"].append(
                                (block.at[:, skip:count, :], target.at[:, row_a + skip : row_b, :])
                            )
                        elif name == "down":
                            skip = 0
                            if row_a:
                                skip = 16
                                made["down"].append(
                                    (source.at[offset : offset + 16, :], edge_down.at[case - 6, column])
                                )
                            made["down"].append(
                                (source.at[offset + skip : offset + count, :],
                                 w_down.at[column, row_a + skip : row_b, :])
                            )
        return made

    order = ("out", "up", "down")
    for z in range(4):
        for y in range(2):

            @pl.when((place[1] == z) & (place[2] == y))
            def _(z=z, y=y):
                made = fetch(z, y)
                for n, name in enumerate(order):
                    for source, target in made[name]:
                        pltpu.make_async_copy(source, target, sem.at[n]).start()

    def arrived(refs, n):
        for ref in refs:
            pltpu.make_async_copy(ref, ref, sem.at[n]).wait()

    here = inside_column(place, 0)
    stream = wide(tokens[...]) + here * embed[...]
    arrived([w_out], 0)
    w_out[:, 0:16, :] = w_out[:, 0:16, :] + out_head[...]
    heads = (h0, h1, h2, h3)
    for n in range(4):
        total = jnp.zeros((256, 256), jnp.float32)
        for r in range(4):
            rows = pl.ds(pl.multiple_of((place[3] ^ r) * 256, 256), 256)
            total += dot(heads[r][...], w_out[n, rows, :])
        acc[:, n * 256 : n * 256 + 256] = total
    bias_out, bias_down, gain_a, shift_a, gain_f, shift_f = (vectors[n : n + 1, :] for n in range(6))
    xhat_a, scale_a = normalise(stream + acc[...] + bias_out)
    normed = xhat_a * gain_a + shift_a
    normed_low = low(normed)

    arrived([w_up] + [edge_up], 1)
    for n, row in enumerate((128, 512, 896)):
        w_up[:, row : row + 16, :] = w_up[:, row : row + 16, :] + edge_up[n]

    def up(g, _):
        pre = dot(normed_low, w_up[g]) + bias_up[pl.ds(g, 1), :]
        inner = 0.5 * (1.0 + lax.erf(pre * (1.0 / math.sqrt(2.0))))
        hidden[g] = low(pre * inner)
        slope[g] = inner + pre * (jnp.exp(-0.5 * pre * pre) * (1.0 / math.sqrt(2.0 * math.pi)))
        return 0

    lax.fori_loop(0, 16, up, 0)
    arrived([w_down] + [edge_down], 2)
    for n, row in enumerate((1024, 2560)):
        w_down[:, row : row + 16, :] = w_down[:, row : row + 16, :] + edge_down[n]
    acc[...] = normed + bias_down

    def down(g, _):
        rows = pl.ds(pl.multiple_of(g * 256, 256), 256)
        for n in range(4):
            cols = slice(n * 256, n * 256 + 256)
            acc[:, cols] += dot(hidden[g], w_down[n, rows, :])
        return 0

    lax.fori_loop(0, 16, down, 0)
    xhat_f, scale_f = normalise(acc[...])
    block_out[...] = low(xhat_f * gain_f + shift_f)

    out_grad = wide(cotangent[...])
    sums[4:5, :] = column_sum(out_grad * xhat_f)
    sums[5:6, :] = column_sum(out_grad)
    acc[...] = normalise_back(out_grad, gain_f, xhat_f, scale_f)
    ffn_grad = low(acc[...])
    sums[1:2, :] = column_sum(wide(ffn_grad))
    normed_t = normed_low.T

    def back_step(g, _):
        rows = pl.ds(pl.multiple_of(g * 256, 256), 256)
        total = jnp.zeros((256, 256), jnp.float32)
        for n in range(4):
            total += dot_last(ffn_grad[:, n * 256 : n * 256 + 256], w_down[n, rows, :])
        pre_grad = low(total * slope[g])
        sums_up[pl.ds(g, 1), :] = column_sum(wide(pre_grad))
        acc[...] += dot_last(pre_grad, w_up[g])
        grad_up[g] = low(dot(normed_t, pre_grad))
        part = low(dot_first(hidden[g], ffn_grad))
        for n in range(4):
            grad_down[n, rows, :] = part[:, n * 256 : n * 256 + 256]
        return 0

    lax.fori_loop(0, 16, back_step, 0)

    def send(case, name, source, column):
        made = []
        for seg, row_a, row_b, offset, _, _ in SEGMENTS[case]:
            count = row_b - row_a
            if seg == name:
                made.append((row_a, row_b, offset, count))
        return made

    started = []
    for r in range(4):
        rx, rc = r // 2, r % 2
        column = place[3] ^ r
        targets = grads_other if rc else grads_own
        for case in range(2, 8):
            ry = place[2] ^ (case % 2)
            piece = targets[case // 2 - 1].at[ry, rx]
            for row_a, row_b, offset, count in send(case, "up", grad_up, column):
                started.append(
                    (grad_up.at[pl.ds(column * 4, 4), row_a:row_b, :],
                     piece.at[offset : offset + 4 * count, :].reshape(4, count, 256))
                )
            for row_a, row_b, offset, count in send(case, "down", grad_down, column):
                started.append(
                    (grad_down.at[column, row_a:row_b, :], piece.at[offset : offset + count, :])
                )
    for source, target in started:
        pltpu.make_async_copy(source, target, sem_out.at[0]).start()

    normed_grad = acc[...]
    sums[2:3, :] = column_sum(normed_grad * xhat_a)
    sums[3:4, :] = column_sum(normed_grad)
    attn_wide = normalise_back(normed_grad, gain_a, xhat_a, scale_a)
    resid_grad[...] = attn_wide
    sums[6:7, :] = column_sum(here * attn_wide)
    attn_grad = low(attn_wide)
    sums[0:1, :] = column_sum(wide(attn_grad))
    sums[7:8, :] = jnp.zeros((1, D), jnp.float32)
    for r, out in enumerate((g0, g1, g2, g3)):
        rows = pl.ds(pl.multiple_of((place[3] ^ r) * 256, 256), 256)
        total = jnp.zeros((256, 256), jnp.float32)
        for n in range(4):
            total += dot_last(attn_grad[:, n * 256 : n * 256 + 256], w_out[n, rows, :])
        out[...] = low(total)
        part = dot_first(heads[r][...], attn_grad)
        for n in range(4):
            grad_out[n, rows, :] = low(part[:, n * 256 : n * 256 + 256])
    head_grad[...] = wide(grad_out[:, 0:16, :])
    last = []
    for r in range(4):
        rx, rc = r // 2, r % 2
        column = place[3] ^ r
        targets = grads_other if rc else grads_own
        piece = targets[0].at[place[2], rx]
        last.append((grad_out.at[column], piece.at[0:1024, :]))
    for source, target in last:
        pltpu.make_async_copy(source, target, sem_out.at[1]).start()
    for source, target in started:
        pltpu.make_async_copy(source, target, sem_out.at[0]).wait()
    for source, target in last:
        pltpu.make_async_copy(source, target, sem_out.at[1]).wait()


def layer(place, heads, tokens, cotangent, embed, vectors, bias_up, out_head, pieces):
    grads = struct((2, 2, PIECE, 256))
    block = struct((256, 256))
    return pl.pallas_call(
        layer_kernel,
        out_shape=(
            struct((256, D)), struct((256, D), jnp.float32), block, block, block, block,
            struct((8, D), jnp.float32), struct((16, 256), jnp.float32),
            struct((4, 16, 256), jnp.float32),
        ) + (grads,) * 6,
        in_specs=[SMEM] + [VMEM] * 10 + [ANY] * 32,
        out_specs=(VMEM,) * 9 + (ANY,) * 6,
        scratch_shapes=[
            pltpu.VMEM((4, 1024, 256), jnp.bfloat16),
            pltpu.VMEM((16, 1024, 256), jnp.bfloat16),
            pltpu.VMEM((4, 4096, 256), jnp.bfloat16),
            pltpu.VMEM((3, 16, 16, 256), jnp.bfloat16),
            pltpu.VMEM((2, 4, 16, 256), jnp.bfloat16),
            pltpu.VMEM((16, 256, 256), jnp.bfloat16),
            pltpu.VMEM((16, 256, 256), jnp.float32),
            pltpu.VMEM((16, 1024, 256), jnp.bfloat16),
            pltpu.VMEM((4, 4096, 256), jnp.bfloat16),
            pltpu.VMEM((4, 1024, 256), jnp.bfloat16),
            pltpu.VMEM((256, D), jnp.float32),
            pltpu.SemaphoreType.DMA((3,)),
            pltpu.SemaphoreType.DMA((2,)),
        ],
        compiler_params=pltpu.CompilerParams(vmem_limit_bytes=60 << 20),
        name="layer",
    )(place, *heads, tokens, cotangent, embed, vectors, bias_up, out_head, *pieces)


def product(left, right):
    return jnp.dot(left, right, preferred_element_type=jnp.float32)


def product_inner(left, right):
    return lax.dot_general(
        left, right, (((0,), (0,)), ((), ())), preferred_element_type=jnp.float32
    )


def layer_norm(resid, gain, shift):
    average = jnp.mean(resid, axis=-1, keepdims=True)
    centred = resid - average
    variance = jnp.mean(centred * centred, axis=-1, keepdims=True)
    return centred * lax.rsqrt(variance + NORM_EPS) * gain + shift


def unpack_all(flat_params, dp_count, fsdp_count):
    shapes = [(D, D)] * 4 + [(D, FF), (FF, D)] + [(1, D)] * 4 + [(1, FF)] + [(1, D)] * 6
    blocks = (
        flat_params.reshape(dp_count, fsdp_count, -1).transpose(1, 0, 2).reshape(fsdp_count, -1)
    )
    pieces = []
    offset = 0
    for rows, cols in shapes:
        width = rows * (cols // fsdp_count)
        part = blocks[:, offset : offset + width].reshape(fsdp_count, rows, cols // fsdp_count)
        whole = part.transpose(1, 0, 2).reshape(rows, cols)
        pieces.append(whole.reshape(-1) if rows == 1 else whole)
        offset += width
    return pieces


def split_heads(values):
    return values.reshape(values.shape[0], H, DH).transpose(1, 0, 2)


def merge_heads(values):
    return values.transpose(1, 0, 2).reshape(values.shape[1], H * DH)


def head_forward(head_item):
    query_h, key_h, value_h = head_item
    scores = product(query_h, key_h.T) * DH ** (-0.5)
    highest = jnp.max(scores, axis=1, keepdims=True)
    weights = jnp.exp(scores - highest)
    totals = jnp.sum(weights, axis=1, keepdims=True)
    probabilities = weights / totals
    result = product(probabilities.astype(jnp.bfloat16), value_h)
    return (result, (highest + jnp.log(totals))[:, 0])


def head_query_back(head_item):
    query_h, key_h, value_h, grad_h, logsum = head_item
    score_scale = DH ** (-0.5)
    scores = product(query_h, key_h.T) * score_scale
    probabilities = jnp.exp(scores - logsum[:, None])
    prob_grad = product(grad_h, value_h.T)
    inner_sum = jnp.sum(probabilities * prob_grad, axis=1)
    score_grad = (probabilities * (prob_grad - inner_sum[:, None])).astype(jnp.bfloat16)
    query_grad = product(score_grad, key_h) * score_scale
    return (query_grad, inner_sum)


def head_key_back(head_item):
    key_h, value_h, query_all, grad_all, logsum_all, inner_all = head_item
    score_scale = DH ** (-0.5)
    scores_t = product(key_h, query_all.T) * score_scale
    probs_t = jnp.exp(scores_t - logsum_all[None, :])
    prob_grad_t = product(value_h, grad_all.T)
    score_grad_t = (probs_t * (prob_grad_t - inner_all[None, :])).astype(jnp.bfloat16)
    key_grad = product(score_grad_t, query_all) * score_scale
    value_grad = product(probs_t.astype(jnp.bfloat16), grad_all)
    return (key_grad, value_grad)


def body(
    tokens,
    cotangent,
    master,
    first_moment,
    second_moment,
    average,
    timestep,
    block_length,
    block_start,
):
    dp_count = lax.axis_size("dp")
    fsdp_count = lax.axis_size("fsdp")
    master_low = master.astype(jnp.bfloat16)
    flat_params = lax.all_gather(master_low, ("dp", "fsdp"), axis=0, tiled=True)
    (
        w_query,
        w_key,
        w_value,
        w_out,
        w_up,
        w_down,
        b_query,
        b_value,
        b_out,
        b_down,
        b_up,
        gain_attn,
        shift_attn,
        gain_ffn,
        shift_ffn,
        w_time,
        b_time,
    ) = unpack_all(flat_params, dp_count, fsdp_count)
    gain_a = gain_attn.astype(jnp.float32)
    shift_a = shift_attn.astype(jnp.float32)
    gain_f = gain_ffn.astype(jnp.float32)
    shift_f = shift_ffn.astype(jnp.float32)
    row_count = tokens.shape[0]
    position = lax.axis_index("fsdp") * row_count + jnp.arange(row_count, dtype=jnp.int32)
    block_first = block_start[0]
    inside = ((position >= block_first) & (position < block_first + block_length[0])).astype(
        jnp.float32
    )[:, None]
    time_frac = timestep[0].astype(jnp.float32) / 5000.0
    time_embed = time_frac * w_time.astype(jnp.float32) + b_time.astype(jnp.float32)
    stream = tokens.astype(jnp.float32) + inside * time_embed
    stream_low = stream.astype(jnp.bfloat16)
    queries = (product(stream_low, w_query) + b_query.astype(jnp.float32)).astype(jnp.bfloat16)
    keys_local = product(stream_low, w_key).astype(jnp.bfloat16)
    values_local = (product(stream_low, w_value) + b_value.astype(jnp.float32)).astype(jnp.bfloat16)
    keys_all, values_all = (
        lax.all_gather(keys_local, "fsdp", axis=0, tiled=True),
        lax.all_gather(values_local, "fsdp", axis=0, tiled=True),
    )
    query_heads = split_heads(queries)
    key_heads = split_heads(keys_all)
    value_heads = split_heads(values_all)
    head_out, logsum = lax.map(head_forward, (query_heads, key_heads, value_heads))
    heads_low = merge_heads(head_out).astype(jnp.bfloat16)
    resid_attn = stream + product(heads_low, w_out) + b_out.astype(jnp.float32)
    normed = layer_norm(resid_attn, gain_a, shift_a)
    normed_low = normed.astype(jnp.bfloat16)
    pre_act = product(normed_low, w_up) + b_up.astype(jnp.float32)
    hidden = jax.nn.gelu(pre_act, approximate=False).astype(jnp.bfloat16)
    resid_ffn = normed + product(hidden, w_down) + b_down.astype(jnp.float32)
    block_out = layer_norm(resid_ffn, gain_f, shift_f).astype(jnp.bfloat16)
    stream_all, heads_all, normed_all, hidden_all = (
        lax.all_gather(stream_low, "fsdp", axis=0, tiled=True),
        lax.all_gather(heads_low, "fsdp", axis=0, tiled=True),
        lax.all_gather(normed_low, "fsdp", axis=0, tiled=True),
        lax.all_gather(hidden, "fsdp", axis=0, tiled=True),
    )
    back_params = lax.all_gather(master_low, ("dp", "fsdp"), axis=0, tiled=True)
    back_pieces = unpack_all(back_params, dp_count, fsdp_count)
    w_query_back, w_key_back, w_value_back, w_out_back, w_up_back, w_down_back = back_pieces[:6]
    out_grad = cotangent.astype(jnp.float32)
    _, pull_ffn = jax.vjp(layer_norm, resid_ffn, gain_f, shift_f)
    resid_ffn_grad, grad_gain_ffn, grad_shift_ffn = pull_ffn(out_grad)
    ffn_grad = resid_ffn_grad.astype(jnp.bfloat16)
    hidden_grad = product(ffn_grad, w_down_back.T)
    _, pull_gelu = jax.vjp(partial(jax.nn.gelu, approximate=False), pre_act)
    pre_grad = pull_gelu(hidden_grad)[0].astype(jnp.bfloat16)
    normed_grad = resid_ffn_grad + product(pre_grad, w_up_back.T)
    _, pull_attn = jax.vjp(layer_norm, resid_attn, gain_a, shift_a)
    resid_attn_grad, grad_gain_attn, grad_shift_attn = pull_attn(normed_grad)
    attn_grad = resid_attn_grad.astype(jnp.bfloat16)
    heads_grad = product(attn_grad, w_out_back.T).astype(jnp.bfloat16)
    query_parts, inner_sum = lax.map(
        head_query_back, (query_heads, key_heads, value_heads, split_heads(heads_grad), logsum)
    )
    query_grad = merge_heads(query_parts).astype(jnp.bfloat16)
    queries_all, heads_grad_all = (
        lax.all_gather(queries, "fsdp", axis=0, tiled=True),
        lax.all_gather(heads_grad, "fsdp", axis=0, tiled=True),
    )
    logsum_all, inner_all = (
        lax.all_gather(logsum, "fsdp", axis=1, tiled=True),
        lax.all_gather(inner_sum, "fsdp", axis=1, tiled=True),
    )
    key_parts, value_parts = lax.map(
        head_key_back,
        (
            split_heads(keys_local),
            split_heads(values_local),
            split_heads(queries_all),
            split_heads(heads_grad_all),
            logsum_all,
            inner_all,
        ),
    )
    key_grad = merge_heads(key_parts).astype(jnp.bfloat16)
    value_grad = merge_heads(value_parts).astype(jnp.bfloat16)
    stream_grad = (
        resid_attn_grad
        + product(query_grad, w_query_back.T)
        + product(key_grad, w_key_back.T)
        + product(value_grad, w_value_back.T)
    )
    grad_b_time = jnp.sum(inside * stream_grad, axis=0)
    grad_w_time = time_frac * grad_b_time
    query_cols, key_cols, value_cols, attn_cols, ffn_cols, pre_cols = (
        lax.all_to_all(query_grad, "fsdp", split_axis=1, concat_axis=0, tiled=True),
        lax.all_to_all(key_grad, "fsdp", split_axis=1, concat_axis=0, tiled=True),
        lax.all_to_all(value_grad, "fsdp", split_axis=1, concat_axis=0, tiled=True),
        lax.all_to_all(attn_grad, "fsdp", split_axis=1, concat_axis=0, tiled=True),
        lax.all_to_all(ffn_grad, "fsdp", split_axis=1, concat_axis=0, tiled=True),
        lax.all_to_all(pre_grad, "fsdp", split_axis=1, concat_axis=0, tiled=True),
    )
    grad_w_query = product_inner(stream_all, query_cols)
    grad_w_key = product_inner(stream_all, key_cols)
    grad_w_value = product_inner(stream_all, value_cols)
    grad_w_out = product_inner(heads_all, attn_cols)
    grad_w_up = product_inner(normed_all, pre_cols)
    grad_w_down = product_inner(hidden_all, ffn_cols)
    grad_b_query = jnp.sum(query_cols.astype(jnp.float32), axis=0)
    grad_b_value = jnp.sum(value_cols.astype(jnp.float32), axis=0)
    grad_b_out = jnp.sum(attn_cols.astype(jnp.float32), axis=0)
    grad_b_down = jnp.sum(ffn_cols.astype(jnp.float32), axis=0)
    grad_b_up = jnp.sum(pre_cols.astype(jnp.float32), axis=0)
    vector_terms = jnp.stack(
        [grad_gain_attn, grad_shift_attn, grad_gain_ffn, grad_shift_ffn, grad_w_time, grad_b_time]
    )
    vector_part = lax.psum_scatter(vector_terms, "fsdp", scatter_dimension=1, tiled=True)
    vector_block = jnp.concatenate(
        [grad_b_query, grad_b_value, grad_b_out, grad_b_down, grad_b_up, vector_part.reshape(-1)]
    )
    grad_block = jnp.concatenate(
        [
            piece.reshape(-1)
            for piece in (
                grad_w_query,
                grad_w_key,
                grad_w_value,
                grad_w_out,
                grad_w_up,
                grad_w_down,
            )
        ]
        + [vector_block]
    )
    grad_shard = lax.psum_scatter(grad_block, "dp", scatter_dimension=0, tiled=True)
    vector_grad = lax.psum(vector_block, "dp")
    square_sum = lax.psum(jnp.sum(grad_shard * grad_shard), ("dp", "fsdp"))
    grad_norm = jnp.sqrt(square_sum)
    clip_limit = 4.0 * math.sqrt(PARAMS)
    clipped = grad_shard * (clip_limit / jnp.maximum(grad_norm, clip_limit))
    new_first = 0.9 * first_moment + 0.1 * clipped
    new_second = 0.98 * second_moment + 0.02 * clipped * clipped
    first_hat = new_first / (1.0 - 0.9**STEP)
    second_hat = new_second / (1.0 - 0.98**STEP)
    new_master = master - 0.02 * (first_hat / (jnp.sqrt(second_hat) + 1e-06) + 0.01 * master)
    new_average = 0.99 * average + 0.01 * new_master
    return (
        block_out,
        stream_grad,
        grad_norm,
        vector_grad,
        new_first,
        new_second,
        new_master,
        new_average,
    )


AXES = ("dp", "fsdp")


def send(values, route):
    pairs = []
    for n in range(32):
        there = route(n // 8, n // 4 % 2, n // 2 % 2, n % 2)
        if there is not None:
            z, y, x, c = there
            pairs.append((n, z * 8 + y * 4 + x * 2 + c))
    return lax.ppermute(values, AXES, pairs)


def to_core(z, y, x, c):
    return z, y, x, 1 - c


def to_x(z, y, x, c):
    return z, y, 1 - x, c


def to_y(z, y, x, c):
    return z, 1 - y, x, c


def to_near(z, y, x, c):
    return z ^ 1, y, x, c


def to_far(z, y, x, c):
    return z ^ 2, y, x, c


def only(route, planes):
    return lambda z, y, x, c: route(z, y, x, c) if z in planes else None


EVERY = (to_core, to_x, to_y, to_near, to_far)


def total(values):
    for route in EVERY:
        values = values + send(values, route)
    return values


def gather_pieces(own, z):
    outer = (z == 0) | (z == 3)
    got_1 = send(own, only(to_far, (0, 3)))
    pass_1 = jnp.where(outer, own, got_1)
    got_2 = send(pass_1, to_near)
    got_3 = send(own, only(to_far, (1, 2)))
    pass_2 = jnp.where(outer, got_3, own)
    got_4 = send(pass_2, to_near)
    slot_b = jnp.where(z == 2, got_1, got_2)
    slot_v = jnp.where(z == 1, got_1, jnp.where(z == 2, got_2, got_3))
    slots = [own, slot_b, slot_v, got_4]
    planes = [(1, 2, 3), (0,), (0, 1, 2, 3), (0, 1, 2, 3)]
    own_y = [send(piece, to_y) for piece in slots]
    over_x = [send(piece, only(to_x, p)) for piece, p in zip(slots, planes)]
    over_xy = [
        send(over_x[n], only(to_y, planes[n])) if n == 2 else send(own_y[n], only(to_x, planes[n]))
        for n in range(4)
    ]
    mine = slots + own_y + over_x + over_xy
    core = [send(piece, only(to_core, planes[n % 4])) for n, piece in enumerate(mine)]
    return slots, own_y, mine + core


def add(left, right):
    return wide(left) + wide(right)


def block_body(
    tokens,
    cotangent,
    master,
    first_moment,
    second_moment,
    average,
    timestep,
    block_length,
    block_start,
):
    shard = lax.axis_index("dp")
    j = lax.axis_index("fsdp")
    z, y = shard // 2, shard % 2
    place = jnp.stack([shard, z, y, j, block_start[0], block_length[0]]).astype(jnp.int32)
    flat = jnp.pad(master, (0, LANE_ROWS * 128 - SHARD)).reshape(LANE_ROWS, 128)
    own = pack(place, flat)
    tokens_c = send(tokens, to_core)
    tokens_x = send(tokens, to_x)
    tokens_xc = send(tokens_x, to_core)

    tail = own[TAIL : TAIL + 16]
    zero = jnp.zeros_like(tail)
    shared = jnp.concatenate([jnp.where(shard == 7, tail, zero), jnp.where(shard == 1, tail, zero)])
    here = (jnp.arange(4) == j)[:, None, None]
    shared = total(jnp.where(here, shared[None], jnp.zeros_like(shared)[None]))
    vec = wide(shared[:, :16])
    out_head = shared[:, 16:]
    vec_own = lax.dynamic_index_in_dim(vec, j, 0, keepdims=False)
    time_frac = timestep[0].astype(jnp.float32) / 5000.0
    full = vec.transpose(1, 0, 2).reshape(16, D)
    embed = time_frac * full[12:13] + full[13:14]
    vectors = jnp.concatenate([full[2:4], full[8:12], jnp.zeros((2, D), jnp.float32)])
    bias_up = vec[:, 4:8].reshape(16, 256)

    slots, slots_y, pieces = gather_pieces(own, z)

    (stream, weight, query, key, value, h0, h1, h2, h3, lse) = attend(
        place,
        (tokens, tokens_c, tokens_x, tokens_xc),
        embed,
        vec_own[0:8],
        (slots[0], slots_y[0], slots[1], slots_y[1]),
    )

    def to_relative(r):
        return lambda z, y, x, c: (z, y, x ^ (r // 2), c ^ (r % 2))

    def exchange(blocks):
        return [blocks[0]] + [send(blocks[r], to_relative(r)) for r in range(1, 4)]

    (block_out, resid_grad, g0, g1, g2, g3, sums, sums_up, head_grad, *grads) = layer(
        place, exchange((h0, h1, h2, h3)), tokens, cotangent, embed, vectors, bias_up, out_head, pieces
    )
    grads_own, grads_other = grads[:3], grads[3:]

    (q_grad, k_grad, v_grad, kept, sent, sums_qkv) = attend_back(
        place, query, key, value, lse, weight, exchange((g0, g1, g2, g3))
    )

    part = {}
    for k in (3, 2, 1):
        both = low(add(grads_own[k - 1], send(grads_other[k - 1], to_core)))
        if k == 1:
            both = low(add(both[0], send(both[1], to_y)))
            part[k] = low(add(both[0], send(both[1], to_x)))
        else:
            both = low(add(both[:, 0], send(both[:, 1], to_x)))
            part[k] = low(add(both[0], send(both[1], to_y)))
    even = z % 2 == 0
    outer = (z == 0) | (z == 3)
    inner_part = add(
        jnp.where(even, part[2], part[1]), send(jnp.where(even, part[1], part[2]), to_near)
    )
    inner_sum = add(inner_part, send(low(inner_part), only(to_far, (0, 3))))

    rows = stream.reshape(1024, D)
    w_grads = [low(product_inner(rows, grad)) for grad in (q_grad, k_grad, v_grad)]
    rest = jnp.zeros((PIECE - 1552, 256), jnp.bfloat16)
    piece_0 = jnp.concatenate([w_grads[0], w_grads[1][:528], rest])
    piece_1 = jnp.concatenate([w_grads[1][512:], w_grads[2], rest, rest[:16]])
    low_row = y == 0
    part[0] = low(
        add(
            jnp.where(low_row, piece_0, piece_1),
            send(jnp.where(low_row, piece_1, piece_0), to_y),
        )
    )
    outer_part = add(
        jnp.where(even, part[0], part[3]), send(jnp.where(even, part[3], part[0]), to_near)
    )
    outer_sum = add(outer_part, send(low(outer_part), only(to_far, (1, 2))))

    from_core = send(sent, to_core)
    input_grad = (
        resid_grad
        + kept[0]
        + wide(from_core[0])
        + wide(send(low(kept[1] + wide(from_core[1])), to_x))
    )

    time_grad = sums[6] + sums_qkv[0]
    vec_grad = jnp.concatenate(
        [
            jnp.where(here, sums_qkv[1:3, :256][None], 0.0),
            sums[0:2].reshape(2, 4, 256).transpose(1, 0, 2),
            sums_up.reshape(4, 4, 256),
            sums[2:6].reshape(4, 4, 256).transpose(1, 0, 2),
            (time_frac * time_grad).reshape(4, 1, 256),
            time_grad.reshape(4, 1, 256),
            jnp.zeros((4, 2, 256), jnp.float32),
            head_grad,
        ],
        axis=1,
    )
    extra = lax.dynamic_index_in_dim(total(vec_grad), j, 0, keepdims=False)
    vector_grad = extra[:14].reshape(-1)

    grad_flat, square = unpack(place, jnp.where(outer, outer_sum, inner_sum), extra)
    grad_shard = grad_flat.reshape(-1)[:SHARD]
    grad_norm = jnp.sqrt(jnp.sum(total(square)))
    clip_limit = 4.0 * math.sqrt(PARAMS)
    clipped = grad_shard * (clip_limit / jnp.maximum(grad_norm, clip_limit))
    new_first = 0.9 * first_moment + 0.1 * clipped
    new_second = 0.98 * second_moment + 0.02 * clipped * clipped
    first_hat = new_first / (1.0 - 0.9**STEP)
    second_hat = new_second / (1.0 - 0.98**STEP)
    new_master = master - 0.02 * (first_hat / (jnp.sqrt(second_hat) + 1e-06) + 0.01 * master)
    new_average = 0.99 * average + 0.01 * new_master
    return (
        block_out,
        input_grad,
        grad_norm,
        vector_grad,
        new_first,
        new_second,
        new_master,
        new_average,
    )


def solution(mesh):
    return jax.shard_map(
        block_body if mesh.shape["dp"] == 8 and mesh.shape["fsdp"] == 4 else body,
        mesh=mesh,
        in_specs=(
            P(("dp", "fsdp"), None),
            P(("dp", "fsdp"), None),
            P(("dp", "fsdp")),
            P(("dp", "fsdp")),
            P(("dp", "fsdp")),
            P(("dp", "fsdp")),
            P("dp"),
            P("dp"),
            P("dp"),
        ),
        out_specs=(
            P(("dp", "fsdp"), None),
            P(("dp", "fsdp"), None),
            P(),
            P("fsdp"),
            P(("dp", "fsdp")),
            P(("dp", "fsdp")),
            P(("dp", "fsdp")),
            P(("dp", "fsdp")),
        ),
        check_vma=False,
    )
```

```python
from functools import partial
import math

import jax
import jax.numpy as jnp
from jax import lax
from jax.experimental import pallas as pl
from jax.experimental.pallas import tpu as pltpu
from jax.sharding import PartitionSpec as P

D = 1024
H = 16
DH = 64
FF = 4096
STEP = 10
PARAMS = 12597248
NORM_EPS = 1e-05

SHARD = PARAMS // 32
PIECE = 1600
LANE_ROWS = 3080
PAD = 128
TAIL = 1536
REGIONS = (
    ("q", 0, 1024, 256),
    ("k", 262144, 1024, 256),
    ("v", 524288, 1024, 256),
    ("o", 786432, 1024, 256),
    ("up", 1048576, 1024, 1024),
    ("down", 2097152, 4096, 256),
    ("vec", 3145728, 16, 256),
)


def segments(shard):
    low, high = shard * SHARD, (shard + 1) * SHARD
    found, offset = [], 0
    for name, start, rows, width in REGIONS:
        size = 3584 if name == "vec" else rows * width
        first, last = max(low, start), min(high, start + size)
        if first >= last:
            continue
        row_a = (first - start) // width // 16 * 16
        row_b = min(rows, -(-(-(-(last - start) // width)) // 16) * 16)
        found.append((name, row_a, row_b, offset, width // 128, start // 128))
        offset += (row_b - row_a) * (width // 256)
    return found


def lane_start(shard):
    return shard * SHARD // 128


SEGMENTS = [segments(shard) for shard in range(8)]
SLOT = ((0, 1, 3, 2), (2, 0, 3, 1), (1, 3, 0, 2), (2, 3, 1, 0))


def buffers(z):
    x_a, y_b = 9, 11
    over_x = [7, 8, x_a, 13]
    both = [y_b if z == 2 else x_a, y_b, 12, 14]
    return [0, 1, 2, 3, 4, 5, 6, 10, *over_x, *both]


BUFFER = [buffers(z) for z in range(4)]


def dot(left, right):
    return jnp.dot(left, right, preferred_element_type=jnp.float32)


def dot_last(left, right):
    return lax.dot_general(
        left, right, (((1,), (1,)), ((), ())), preferred_element_type=jnp.float32
    )


def dot_first(left, right):
    return lax.dot_general(
        left, right, (((0,), (0,)), ((), ())), preferred_element_type=jnp.float32
    )


def low(values):
    return values.astype(jnp.bfloat16)


def wide(values):
    return values.astype(jnp.float32)


VMEM = pl.BlockSpec(memory_space=pltpu.VMEM)
SMEM = pl.BlockSpec(memory_space=pltpu.SMEM)
ANY = pl.BlockSpec(memory_space=pl.ANY)


def struct(shape, kind=jnp.bfloat16):
    return jax.ShapeDtypeStruct(shape, kind)


def chunks(rows, most=128):
    return [(a, min(most, rows - a)) for a in range(0, rows, most)]


def pack_kernel(place, flat, tails, piece, rolled, rows):
    shard = place[0]
    rows[0:PAD, :] = jnp.zeros((PAD, 128), jnp.float32)
    rows[PAD + LANE_ROWS : PAD + LANE_ROWS + PAD, :] = jnp.zeros((PAD, 128), jnp.float32)
    rolled[0:8, :] = jnp.zeros((8, 128), jnp.float32)

    @pl.when(shard % 2 == 0)
    def _():
        for a, n in chunks(LANE_ROWS):
            rows[PAD + a : PAD + a + n, :] = flat[a : a + n, :]

    @pl.when(shard % 2 == 1)
    def _():
        for a, n in chunks(LANE_ROWS):
            rolled[8 + a : 8 + a + n, :] = pltpu.roll(flat[a : a + n, :], 64, 1)
        for a, n in chunks(LANE_ROWS):
            lane = lax.broadcasted_iota(jnp.int32, (n, 128), 1)
            rows[PAD + a : PAD + a + n, :] = jnp.where(
                lane < 64, rolled[7 + a : 7 + a + n, :], rolled[8 + a : 8 + a + n, :]
            )

    for case in range(8):

        @pl.when(shard == case)
        def _(case=case):
            for _, row_a, row_b, offset, step, first in SEGMENTS[case]:
                if offset == TAIL:
                    piece[TAIL:PIECE, :] = tails[...]
                    continue
                count = row_b - row_a
                base = PAD + first + step * row_a - lane_start(case)
                for t in range(step):
                    out = offset + t // 2 * count
                    lanes = slice(t % 2 * 128, t % 2 * 128 + 128)
                    for a, n in chunks(count):
                        piece[out + a : out + a + n, lanes] = low(
                            rows[pl.ds(base + t + step * a, n, stride=step), :]
                        )


def pack(place, flat, tails):
    return pl.pallas_call(
        pack_kernel,
        out_shape=struct((PIECE, 256)),
        in_specs=[SMEM, VMEM, VMEM],
        out_specs=VMEM,
        scratch_shapes=[
            pltpu.VMEM((8 + LANE_ROWS, 128), jnp.float32),
            pltpu.VMEM((PAD + LANE_ROWS + PAD, 128), jnp.float32),
        ],
        compiler_params=pltpu.CompilerParams(vmem_limit_bytes=24 << 20),
        name="pack",
    )(place, flat, tails)


def unpack_kernel(place, inner, inner_last, outer, outer_last, flat, square, rows, left, right, sem):
    shard = place[0]
    is_inner = (place[1] == 1) | (place[1] == 2)

    def fetch(first, second):
        copies = [
            pltpu.make_async_copy(first, left, sem.at[0]),
            pltpu.make_async_copy(second, right, sem.at[1]),
        ]
        for copy in copies:
            copy.start()
        for copy in copies:
            copy.wait()

    @pl.when(is_inner)
    def _():
        fetch(inner, inner_last)

    @pl.when(jnp.logical_not(is_inner))
    def _():
        fetch(outer, outer_last)

    for case in range(8):

        @pl.when(shard == case)
        def _(case=case):
            for _, row_a, row_b, offset, step, first in SEGMENTS[case]:
                count = row_b - row_a
                base = PAD + first + step * row_a - lane_start(case)
                for t in range(step):
                    source = offset + t // 2 * count
                    lanes = slice(t % 2 * 128, t % 2 * 128 + 128)
                    for a, n in chunks(count):
                        spot = slice(source + a, source + a + n)
                        value = wide(left[spot, lanes]) + wide(right[spot, lanes])
                        if offset == TAIL:
                            value = jnp.zeros((n, 128), jnp.float32)
                        rows[pl.ds(base + t + step * a, n, stride=step), :] = value

    square[...] = jnp.zeros_like(square)
    for odd in range(2):

        @pl.when(shard % 2 == odd)
        def _(odd=odd):
            total = jnp.zeros((8, 128), jnp.float32)
            for a, n in chunks(LANE_ROWS):
                value = rows[PAD + a : PAD + a + n, :]
                lane = lax.broadcasted_iota(jnp.int32, (n, 128), 1)
                if odd:
                    after = rows[PAD + a + 1 : PAD + a + 1 + n, :]
                    value = jnp.where(
                        lane < 64, pltpu.roll(value, 64, 1), pltpu.roll(after, 64, 1)
                    )
                if (a + n) * 128 > SHARD:
                    row = lax.broadcasted_iota(jnp.int32, (n, 128), 0) + a
                    value = jnp.where(row * 128 + lane < SHARD, value, 0.0)
                flat[a : a + n, :] = value
                total += jnp.sum((value * value).reshape(n // 8, 8, 128), axis=0)
            square[...] = total


def unpack(place, *pieces):
    return pl.pallas_call(
        unpack_kernel,
        out_shape=(struct((LANE_ROWS, 128), jnp.float32), struct((8, 128), jnp.float32)),
        in_specs=[SMEM] + [ANY] * 4,
        out_specs=(VMEM, VMEM),
        scratch_shapes=[
            pltpu.VMEM((PAD + LANE_ROWS + PAD, 128), jnp.float32),
            pltpu.VMEM((PIECE, 256), jnp.bfloat16),
            pltpu.VMEM((PIECE, 256), jnp.bfloat16),
            pltpu.SemaphoreType.DMA((2,)),
        ],
        compiler_params=pltpu.CompilerParams(vmem_limit_bytes=60 << 20),
        name="unpack",
    )(place, *pieces)


def combine_kernel(split, place, *refs):
    kept, sent = refs[-2:]
    first = sum(wide(ref[...]) for ref in refs[:split])
    second = sum(wide(ref[...]) for ref in refs[split:-2])
    even = place[1] % 2 == 0
    kept[...] = low(jnp.where(even, first, second))
    sent[...] = low(jnp.where(even, second, first))


def combine(place, first, second):
    blocks = 5
    size = PIECE // blocks

    def spec(piece):
        if piece.ndim == 4:
            return pl.BlockSpec((None, None, size, 256), lambda n: (0, 0, n, 0))
        return pl.BlockSpec((size, 256), lambda n: (n, 0))

    pieces = [*first, *second]
    return pl.pallas_call(
        partial(combine_kernel, len(first)),
        grid=(blocks,),
        out_shape=(struct((PIECE, 256)), struct((PIECE, 256))),
        in_specs=[SMEM] + [spec(piece) for piece in pieces],
        out_specs=(pl.BlockSpec((size, 256), lambda n: (n, 0)),) * 2,
        compiler_params=pltpu.CompilerParams(vmem_limit_bytes=60 << 20),
        name="combine",
    )(place, *pieces)


def column_sum(values):
    return jnp.sum(values, axis=0, keepdims=True)


def inside_column(place, relative):
    rows = lax.broadcasted_iota(jnp.int32, (256, 1), 0)
    position = rows + (place[3] ^ relative) * 256
    return ((position >= place[4]) & (position < place[4] + place[5])).astype(jnp.float32)


def attend_kernel(
    place, embed, bias, t0, t1, t2, t3, p0, p1, p2, p3, p4, p5, p6, p7, p8,
    stream_out, weight_out, q_out, k_out, v_out, h0, h1, h2, h3, lse_out, stack,
    tokens, staged, q_heads, k_heads, v_heads, o_heads, edge, sem, sem_tokens, sem_in, sem_out,
):
    fetches = [
        pltpu.make_async_copy(ref, tokens.at[r], sem_tokens.at[r])
        for r, ref in enumerate((t0, t1, t2, t3))
    ]
    for copy in fetches:
        copy.start()

    def copies(first, second):
        return [
            pltpu.make_async_copy(first.at[0:1024, :], weight_out.at[0], sem.at[0]),
            pltpu.make_async_copy(first.at[1024:1552, :], weight_out.at[1, 0:528, :], sem.at[1]),
            pltpu.make_async_copy(second.at[16:512, :], weight_out.at[1, 528:1024, :], sem.at[2]),
            pltpu.make_async_copy(second.at[0:16, :], edge, sem.at[3]),
            pltpu.make_async_copy(second.at[512:1536, :], weight_out.at[2], sem.at[4]),
        ]

    held = ((p0, p1), (p2, p3), (p4, p5))
    for z in range(4):
        for y in range(2):
            own, other = held[SLOT[z][0]]
            pair = (other, own) if y else (own, other)

            @pl.when((place[1] == z) & (place[2] == y))
            def _(pair=pair):
                for copy in copies(*pair):
                    copy.start()

    held_in = [
        pltpu.make_async_copy(ref, staged.at[n], sem_in.at[n])
        for n, ref in enumerate((p0, p2, p4, p6, p1, p3, p5, p7, p8))
    ]
    held_out = [pltpu.make_async_copy(staged.at[n], stack.at[n], sem_out.at[n]) for n in range(9)]
    for copy in held_in:
        copy.start()
    for r, copy in enumerate(fetches):
        copy.wait()
        stream_out[r] = low(wide(tokens[r]) + inside_column(place, r) * embed[...])
    lanes = lax.broadcasted_iota(jnp.int32, (1024, 128), 1)
    v_heads[...] = jnp.broadcast_to((lanes >= 64).astype(jnp.bfloat16), (4, 1024, 128))
    for copy in copies(p0, p1):
        copy.wait()
    weight_out[1, 512:528, :] = weight_out[1, 512:528, :] + edge[...]
    for r in range(4):
        rows = slice(r * 256, r * 256 + 256)
        stream = stream_out[r]
        query = low(dot(stream, weight_out[0]) + bias[0:1, :])
        key = low(dot(stream, weight_out[1]))
        value = low(dot(stream, weight_out[2]) + bias[1:2, :])
        q_out[rows, :] = query
        k_out[rows, :] = key
        v_out[rows, :] = value
        for h in range(4):
            cols = slice(h * 64, h * 64 + 64)
            q_heads[h, rows, :] = query[:, cols] * 0.125
            k_heads[h, rows, :] = key[:, cols]
            v_heads[h, rows, 0:64] = value[:, cols]
    lse_out[...] = jnp.zeros_like(lse_out)
    for before, copy in zip(held_in, held_out):
        before.wait()
        copy.start()

    def step(n, _):
        h, r = n // 4, n % 4
        rows = pl.ds(pl.multiple_of(r * 256, 256), 256)
        scores = dot_last(q_heads[h, rows, :], k_heads[h])
        highest = jnp.max(scores, axis=1, keepdims=True)
        weights = low(jnp.exp(scores - highest))
        result = dot(weights, v_heads[h])
        total = result[:, 64:65]
        o_heads[h, rows, :] = low(result[:, 0:64] / total)
        lane = lax.broadcasted_iota(jnp.int32, (256, 128), 1)
        lse_out[rows, :] = jnp.where(lane == h, highest + jnp.log(total), lse_out[rows, :])
        return 0

    lax.fori_loop(0, 16, step, 0)
    for r, out in enumerate((h0, h1, h2, h3)):
        for h in range(4):
            out[:, h * 64 : h * 64 + 64] = o_heads[h, r * 256 : r * 256 + 256, :]
    for copy in held_out:
        copy.wait()


def attend(place, tokens, embed, bias, pieces):
    square = struct((1024, 256))
    block = struct((256, 256))
    return pl.pallas_call(
        attend_kernel,
        out_shape=(
            struct((4, 256, 1024)), struct((3, 1024, 256)), square, square, square,
            block, block, block, block, struct((1024, 128), jnp.float32), struct((9, PIECE, 256)),
        ),
        in_specs=[SMEM] + [VMEM] * 2 + [ANY] * 13,
        out_specs=(VMEM,) * 10 + (ANY,),
        scratch_shapes=[
            pltpu.VMEM((4, 256, 1024), jnp.bfloat16),
            pltpu.VMEM((9, PIECE, 256), jnp.bfloat16),
            pltpu.VMEM((4, 1024, 64), jnp.bfloat16),
            pltpu.VMEM((4, 1024, 64), jnp.bfloat16),
            pltpu.VMEM((4, 1024, 128), jnp.bfloat16),
            pltpu.VMEM((4, 1024, 64), jnp.bfloat16),
            pltpu.VMEM((16, 256), jnp.bfloat16),
            pltpu.SemaphoreType.DMA((5,)),
            pltpu.SemaphoreType.DMA((4,)),
            pltpu.SemaphoreType.DMA((9,)),
            pltpu.SemaphoreType.DMA((9,)),
        ],
        compiler_params=pltpu.CompilerParams(vmem_limit_bytes=48 << 20),
        cost_estimate=pl.CostEstimate(
            flops=16_000_000_000, bytes_accessed=24_000_000, transcendentals=4_194_304
        ),
        name="attend",
    )(place, embed, bias, *tokens, *pieces)


def attend_back_kernel(
    place, q_in, k_in, v_in, lse, weight, g0, g1, g2, g3,
    q_grad, k_grad, v_grad, kept, sent, sums,
    q_heads, k_heads, v_heads, g_heads, dq_heads, dk_heads, dv_heads,
):
    for r, grad in enumerate((g0, g1, g2, g3)):
        rows = slice(r * 256, r * 256 + 256)
        for h in range(4):
            cols = slice(h * 64, h * 64 + 64)
            q_heads[h, rows, :] = q_in[rows, cols] * 0.125
            k_heads[h, rows, :] = k_in[rows, cols]
            v_heads[h, rows, :] = v_in[rows, cols]
            g_heads[h, rows, :] = grad[:, cols]

    def step(n, _):
        h, r = n // 4, n % 4
        rows = pl.ds(pl.multiple_of(r * 256, 256), 256)
        query, grad = q_heads[h, rows, :], g_heads[h, rows, :]
        scores = dot_last(query, k_heads[h])
        lane = lax.broadcasted_iota(jnp.int32, (256, 128), 1)
        logsum = jnp.sum(jnp.where(lane == h, lse[rows, :], 0.0), axis=1, keepdims=True)
        probs = jnp.exp(scores - logsum)
        weighted = probs * dot_last(grad, v_heads[h])
        inner = jnp.sum(weighted, axis=1, keepdims=True)
        score_grad = low(weighted - probs * inner)
        dq_heads[h, rows, :] = low(dot(score_grad, k_heads[h]) * 0.125)
        dk_heads[h] += dot_first(query, score_grad)
        dv_heads[h] += dot_first(grad, low(probs))
        return 0

    dk_heads[...] = jnp.zeros_like(dk_heads)
    dv_heads[...] = jnp.zeros_like(dv_heads)
    lax.fori_loop(0, 16, step, 0)
    for h in range(4):
        cols = slice(h * 64, h * 64 + 64)
        q_grad[:, cols] = dq_heads[h]
        k_grad[:, cols] = low(dk_heads[h].T)
        v_grad[:, cols] = low(dv_heads[h].T)
    sums[...] = jnp.zeros_like(sums)
    sums[1:2, 0:256] = column_sum(wide(q_grad[...]))
    sums[2:3, 0:256] = column_sum(wide(v_grad[...]))
    for r in range(4):
        rows = slice(r * 256, r * 256 + 256)
        part = (
            dot_last(q_grad[rows, :], weight[0])
            + dot_last(k_grad[rows, :], weight[1])
            + dot_last(v_grad[rows, :], weight[2])
        )
        sums[0:1, :] += column_sum(inside_column(place, r) * part)
        if r % 2:
            sent[r // 2] = low(part)
        else:
            kept[r // 2] = part


def attend_back(place, query, key, value, lse, weight, grads):
    square = struct((1024, 256))
    return pl.pallas_call(
        attend_back_kernel,
        out_shape=(
            square, square, square, struct((2, 256, D), jnp.float32), struct((2, 256, D)),
            struct((8, D), jnp.float32),
        ),
        in_specs=[SMEM] + [VMEM] * 9,
        out_specs=(VMEM,) * 6,
        scratch_shapes=[pltpu.VMEM((4, 1024, 64), jnp.bfloat16)] * 5
        + [pltpu.VMEM((4, 64, 1024), jnp.float32)] * 2,
        compiler_params=pltpu.CompilerParams(vmem_limit_bytes=40 << 20),
        cost_estimate=pl.CostEstimate(
            flops=20_000_000_000, bytes_accessed=12_000_000, transcendentals=4_194_304
        ),
        name="attend_back",
    )(place, query, key, value, lse, weight, *grads)


def row_mean(values):
    return jnp.sum(values, axis=1, keepdims=True) * (1.0 / D)


def normalise(resid):
    centred = resid - row_mean(resid)
    scale = lax.rsqrt(row_mean(centred * centred) + NORM_EPS)
    return centred * scale, scale


def normalise_back(grad, gain, xhat, scale):
    scaled = grad * gain
    return (scaled - row_mean(scaled) - xhat * row_mean(scaled * xhat)) * scale


def target_piece(targets, k, ry, rx):
    return targets[k - 1].at[ry, rx] if k == 1 else targets[k - 1].at[rx, ry]


def layer_kernel(
    place, h0, h1, h2, h3, tokens, cotangent, embed, vectors, bias_up, out_head, *refs
):
    stack = refs[15]
    pieces = (refs[:15], [stack.at[n] for n in range(9)] + list(refs[16:22]))
    refs = refs[22:]
    (block_out, resid_grad, g0, g1, g2, g3, sums, sums_up, head_grad) = refs[:9]
    grads_own, grads_other = refs[9:12], refs[12:15]
    (w_out, w_up, w_down, edge_up, edge_down, hidden, slope, grad_up, grad_down,
     grad_out, acc, sem, sem_out) = refs[15:]

    def fetch(z, y):
        made = {"out": [], "up": [], "down": []}
        for k in range(1, 4):
            for ry in range(2):
                case = 2 * k + (y ^ ry)
                for r in range(4):
                    rx, rc = r // 2, r % 2
                    source = pieces[rc][BUFFER[z][rx * 8 + ry * 4 + SLOT[z][k]]]
                    column = place[3] ^ r
                    for name, row_a, row_b, offset, step, _ in SEGMENTS[case]:
                        count = row_b - row_a
                        if name == "o":
                            made["out"].append((source.at[offset : offset + count, :], w_out.at[column]))
                        elif name == "up":
                            block = source.at[offset : offset + 4 * count, :].reshape(4, count, 256)
                            target = w_up.at[pl.ds(column * 4, 4)]
                            skip = 0
                            if row_a:
                                skip = 16
                                made["up"].append(
                                    (block.at[:, 0:16, :], edge_up.at[case - 3, pl.ds(column * 4, 4)])
                                )
                            made["up"].append(
                                (block.at[:, skip:count, :], target.at[:, row_a + skip : row_b, :])
                            )
                        elif name == "down":
                            skip = 0
                            if row_a:
                                skip = 16
                                made["down"].append(
                                    (source.at[offset : offset + 16, :], edge_down.at[case - 6, column])
                                )
                            made["down"].append(
                                (source.at[offset + skip : offset + count, :],
                                 w_down.at[column, row_a + skip : row_b, :])
                            )
        return made

    order = ("out", "up", "down")
    for z in range(4):
        for y in range(2):

            @pl.when((place[1] == z) & (place[2] == y))
            def _(z=z, y=y):
                made = fetch(z, y)
                for n, name in enumerate(order):
                    for source, target in made[name]:
                        pltpu.make_async_copy(source, target, sem.at[n]).start()

    def arrived(refs, n):
        for ref in refs:
            pltpu.make_async_copy(ref, ref, sem.at[n]).wait()

    here = inside_column(place, 0)
    stream = wide(tokens[...]) + here * embed[...]
    arrived([w_out], 0)
    w_out[:, 0:16, :] = w_out[:, 0:16, :] + out_head[...]
    heads = (h0, h1, h2, h3)
    for n in range(4):
        total = jnp.zeros((256, 256), jnp.float32)
        for r in range(4):
            rows = pl.ds(pl.multiple_of((place[3] ^ r) * 256, 256), 256)
            total += dot(heads[r][...], w_out[n, rows, :])
        acc[:, n * 256 : n * 256 + 256] = total
    bias_out, bias_down, gain_a, shift_a, gain_f, shift_f = (vectors[n : n + 1, :] for n in range(6))
    xhat_a, scale_a = normalise(stream + acc[...] + bias_out)
    normed = xhat_a * gain_a + shift_a
    normed_low = low(normed)

    arrived([w_up] + [edge_up], 1)
    for n, row in enumerate((128, 512, 896)):
        w_up[:, row : row + 16, :] = w_up[:, row : row + 16, :] + edge_up[n]

    def up(g, _):
        pre = dot(normed_low, w_up[g]) + bias_up[pl.ds(g, 1), :]
        inner = 0.5 * (1.0 + lax.erf(pre * (1.0 / math.sqrt(2.0))))
        hidden[g] = low(pre * inner)
        slope[g] = inner + pre * (jnp.exp(-0.5 * pre * pre) * (1.0 / math.sqrt(2.0 * math.pi)))
        return 0

    lax.fori_loop(0, 16, up, 0)
    arrived([w_down] + [edge_down], 2)
    for n, row in enumerate((1024, 2560)):
        w_down[:, row : row + 16, :] = w_down[:, row : row + 16, :] + edge_down[n]
    acc[...] = normed + bias_down

    def down(g, _):
        rows = pl.ds(pl.multiple_of(g * 256, 256), 256)
        for n in range(4):
            cols = slice(n * 256, n * 256 + 256)
            acc[:, cols] += dot(hidden[g], w_down[n, rows, :])
        return 0

    lax.fori_loop(0, 16, down, 0)
    xhat_f, scale_f = normalise(acc[...])
    block_out[...] = low(xhat_f * gain_f + shift_f)

    out_grad = wide(cotangent[...])
    sums[4:5, :] = column_sum(out_grad * xhat_f)
    sums[5:6, :] = column_sum(out_grad)
    acc[...] = normalise_back(out_grad, gain_f, xhat_f, scale_f)
    ffn_grad = low(acc[...])
    sums[1:2, :] = column_sum(wide(ffn_grad))
    normed_t = normed_low.T

    def back_step(g, _):
        rows = pl.ds(pl.multiple_of(g * 256, 256), 256)
        total = jnp.zeros((256, 256), jnp.float32)
        for n in range(4):
            total += dot_last(ffn_grad[:, n * 256 : n * 256 + 256], w_down[n, rows, :])
        pre_grad = low(total * slope[g])
        sums_up[pl.ds(g, 1), :] = column_sum(wide(pre_grad))
        acc[...] += dot_last(pre_grad, w_up[g])
        grad_up[g] = low(dot(normed_t, pre_grad))
        part = low(dot_first(hidden[g], ffn_grad))
        for n in range(4):
            grad_down[n, rows, :] = part[:, n * 256 : n * 256 + 256]
        return 0

    lax.fori_loop(0, 16, back_step, 0)

    def send(case, name, source, column):
        made = []
        for seg, row_a, row_b, offset, _, _ in SEGMENTS[case]:
            count = row_b - row_a
            if seg == name:
                made.append((row_a, row_b, offset, count))
        return made

    started = []
    for r in range(4):
        rx, rc = r // 2, r % 2
        column = place[3] ^ r
        targets = grads_other if rc else grads_own
        for case in range(2, 8):
            ry = place[2] ^ (case % 2)
            piece = target_piece(targets, case // 2, ry, rx)
            for row_a, row_b, offset, count in send(case, "up", grad_up, column):
                started.append(
                    (grad_up.at[pl.ds(column * 4, 4), row_a:row_b, :],
                     piece.at[offset : offset + 4 * count, :].reshape(4, count, 256))
                )
            for row_a, row_b, offset, count in send(case, "down", grad_down, column):
                started.append(
                    (grad_down.at[column, row_a:row_b, :], piece.at[offset : offset + count, :])
                )
    for source, target in started:
        pltpu.make_async_copy(source, target, sem_out.at[0]).start()

    normed_grad = acc[...]
    sums[2:3, :] = column_sum(normed_grad * xhat_a)
    sums[3:4, :] = column_sum(normed_grad)
    attn_wide = normalise_back(normed_grad, gain_a, xhat_a, scale_a)
    resid_grad[...] = attn_wide
    sums[6:7, :] = column_sum(here * attn_wide)
    attn_grad = low(attn_wide)
    sums[0:1, :] = column_sum(wide(attn_grad))
    sums[7:8, :] = jnp.zeros((1, D), jnp.float32)
    for r, out in enumerate((g0, g1, g2, g3)):
        rows = pl.ds(pl.multiple_of((place[3] ^ r) * 256, 256), 256)
        total = jnp.zeros((256, 256), jnp.float32)
        for n in range(4):
            total += dot_last(attn_grad[:, n * 256 : n * 256 + 256], w_out[n, rows, :])
        out[...] = low(total)
        part = dot_first(heads[r][...], attn_grad)
        for n in range(4):
            grad_out[n, rows, :] = low(part[:, n * 256 : n * 256 + 256])
    head_grad[...] = wide(grad_out[:, 0:16, :])
    last = []
    for r in range(4):
        rx, rc = r // 2, r % 2
        column = place[3] ^ r
        targets = grads_other if rc else grads_own
        piece = target_piece(targets, 1, place[2], rx)
        last.append((grad_out.at[column], piece.at[0:1024, :]))
    for source, target in last:
        pltpu.make_async_copy(source, target, sem_out.at[1]).start()
    for source, target in started:
        pltpu.make_async_copy(source, target, sem_out.at[0]).wait()
    for source, target in last:
        pltpu.make_async_copy(source, target, sem_out.at[1]).wait()


def layer(place, heads, tokens, cotangent, embed, vectors, bias_up, out_head, pieces):
    grads = struct((2, 2, PIECE, 256))
    block = struct((256, 256))
    return pl.pallas_call(
        layer_kernel,
        out_shape=(
            struct((256, D)), struct((256, D), jnp.float32), block, block, block, block,
            struct((8, D), jnp.float32), struct((16, 256), jnp.float32),
            struct((4, 16, 256), jnp.float32),
        ) + (grads,) * 6,
        in_specs=[SMEM] + [VMEM] * 10 + [ANY] * 22,
        out_specs=(VMEM,) * 9 + (ANY,) * 6,
        scratch_shapes=[
            pltpu.VMEM((4, 1024, 256), jnp.bfloat16),
            pltpu.VMEM((16, 1024, 256), jnp.bfloat16),
            pltpu.VMEM((4, 4096, 256), jnp.bfloat16),
            pltpu.VMEM((3, 16, 16, 256), jnp.bfloat16),
            pltpu.VMEM((2, 4, 16, 256), jnp.bfloat16),
            pltpu.VMEM((16, 256, 256), jnp.bfloat16),
            pltpu.VMEM((16, 256, 256), jnp.float32),
            pltpu.VMEM((16, 1024, 256), jnp.bfloat16),
            pltpu.VMEM((4, 4096, 256), jnp.bfloat16),
            pltpu.VMEM((4, 1024, 256), jnp.bfloat16),
            pltpu.VMEM((256, D), jnp.float32),
            pltpu.SemaphoreType.DMA((3,)),
            pltpu.SemaphoreType.DMA((2,)),
        ],
        compiler_params=pltpu.CompilerParams(vmem_limit_bytes=60 << 20),
        cost_estimate=pl.CostEstimate(
            flops=15_000_000_000, bytes_accessed=40_000_000, transcendentals=2_097_152
        ),
        name="layer",
    )(place, *heads, tokens, cotangent, embed, vectors, bias_up, out_head, *pieces)


def product(left, right):
    return jnp.dot(left, right, preferred_element_type=jnp.float32)


def product_inner(left, right):
    return lax.dot_general(
        left, right, (((0,), (0,)), ((), ())), preferred_element_type=jnp.float32
    )


def layer_norm(resid, gain, shift):
    average = jnp.mean(resid, axis=-1, keepdims=True)
    centred = resid - average
    variance = jnp.mean(centred * centred, axis=-1, keepdims=True)
    return centred * lax.rsqrt(variance + NORM_EPS) * gain + shift


def unpack_all(flat_params, dp_count, fsdp_count):
    shapes = [(D, D)] * 4 + [(D, FF), (FF, D)] + [(1, D)] * 4 + [(1, FF)] + [(1, D)] * 6
    blocks = (
        flat_params.reshape(dp_count, fsdp_count, -1).transpose(1, 0, 2).reshape(fsdp_count, -1)
    )
    pieces = []
    offset = 0
    for rows, cols in shapes:
        width = rows * (cols // fsdp_count)
        part = blocks[:, offset : offset + width].reshape(fsdp_count, rows, cols // fsdp_count)
        whole = part.transpose(1, 0, 2).reshape(rows, cols)
        pieces.append(whole.reshape(-1) if rows == 1 else whole)
        offset += width
    return pieces


def split_heads(values):
    return values.reshape(values.shape[0], H, DH).transpose(1, 0, 2)


def merge_heads(values):
    return values.transpose(1, 0, 2).reshape(values.shape[1], H * DH)


def head_forward(head_item):
    query_h, key_h, value_h = head_item
    scores = product(query_h, key_h.T) * DH ** (-0.5)
    highest = jnp.max(scores, axis=1, keepdims=True)
    weights = jnp.exp(scores - highest)
    totals = jnp.sum(weights, axis=1, keepdims=True)
    probabilities = weights / totals
    result = product(probabilities.astype(jnp.bfloat16), value_h)
    return (result, (highest + jnp.log(totals))[:, 0])


def head_query_back(head_item):
    query_h, key_h, value_h, grad_h, logsum = head_item
    score_scale = DH ** (-0.5)
    scores = product(query_h, key_h.T) * score_scale
    probabilities = jnp.exp(scores - logsum[:, None])
    prob_grad = product(grad_h, value_h.T)
    inner_sum = jnp.sum(probabilities * prob_grad, axis=1)
    score_grad = (probabilities * (prob_grad - inner_sum[:, None])).astype(jnp.bfloat16)
    query_grad = product(score_grad, key_h) * score_scale
    return (query_grad, inner_sum)


def head_key_back(head_item):
    key_h, value_h, query_all, grad_all, logsum_all, inner_all = head_item
    score_scale = DH ** (-0.5)
    scores_t = product(key_h, query_all.T) * score_scale
    probs_t = jnp.exp(scores_t - logsum_all[None, :])
    prob_grad_t = product(value_h, grad_all.T)
    score_grad_t = (probs_t * (prob_grad_t - inner_all[None, :])).astype(jnp.bfloat16)
    key_grad = product(score_grad_t, query_all) * score_scale
    value_grad = product(probs_t.astype(jnp.bfloat16), grad_all)
    return (key_grad, value_grad)


def body(
    tokens,
    cotangent,
    master,
    first_moment,
    second_moment,
    average,
    timestep,
    block_length,
    block_start,
):
    dp_count = lax.axis_size("dp")
    fsdp_count = lax.axis_size("fsdp")
    master_low = master.astype(jnp.bfloat16)
    flat_params = lax.all_gather(master_low, ("dp", "fsdp"), axis=0, tiled=True)
    (
        w_query,
        w_key,
        w_value,
        w_out,
        w_up,
        w_down,
        b_query,
        b_value,
        b_out,
        b_down,
        b_up,
        gain_attn,
        shift_attn,
        gain_ffn,
        shift_ffn,
        w_time,
        b_time,
    ) = unpack_all(flat_params, dp_count, fsdp_count)
    gain_a = gain_attn.astype(jnp.float32)
    shift_a = shift_attn.astype(jnp.float32)
    gain_f = gain_ffn.astype(jnp.float32)
    shift_f = shift_ffn.astype(jnp.float32)
    row_count = tokens.shape[0]
    position = lax.axis_index("fsdp") * row_count + jnp.arange(row_count, dtype=jnp.int32)
    block_first = block_start[0]
    inside = ((position >= block_first) & (position < block_first + block_length[0])).astype(
        jnp.float32
    )[:, None]
    time_frac = timestep[0].astype(jnp.float32) / 5000.0
    time_embed = time_frac * w_time.astype(jnp.float32) + b_time.astype(jnp.float32)
    stream = tokens.astype(jnp.float32) + inside * time_embed
    stream_low = stream.astype(jnp.bfloat16)
    queries = (product(stream_low, w_query) + b_query.astype(jnp.float32)).astype(jnp.bfloat16)
    keys_local = product(stream_low, w_key).astype(jnp.bfloat16)
    values_local = (product(stream_low, w_value) + b_value.astype(jnp.float32)).astype(jnp.bfloat16)
    keys_all, values_all = (
        lax.all_gather(keys_local, "fsdp", axis=0, tiled=True),
        lax.all_gather(values_local, "fsdp", axis=0, tiled=True),
    )
    query_heads = split_heads(queries)
    key_heads = split_heads(keys_all)
    value_heads = split_heads(values_all)
    head_out, logsum = lax.map(head_forward, (query_heads, key_heads, value_heads))
    heads_low = merge_heads(head_out).astype(jnp.bfloat16)
    resid_attn = stream + product(heads_low, w_out) + b_out.astype(jnp.float32)
    normed = layer_norm(resid_attn, gain_a, shift_a)
    normed_low = normed.astype(jnp.bfloat16)
    pre_act = product(normed_low, w_up) + b_up.astype(jnp.float32)
    hidden = jax.nn.gelu(pre_act, approximate=False).astype(jnp.bfloat16)
    resid_ffn = normed + product(hidden, w_down) + b_down.astype(jnp.float32)
    block_out = layer_norm(resid_ffn, gain_f, shift_f).astype(jnp.bfloat16)
    stream_all, heads_all, normed_all, hidden_all = (
        lax.all_gather(stream_low, "fsdp", axis=0, tiled=True),
        lax.all_gather(heads_low, "fsdp", axis=0, tiled=True),
        lax.all_gather(normed_low, "fsdp", axis=0, tiled=True),
        lax.all_gather(hidden, "fsdp", axis=0, tiled=True),
    )
    back_params = lax.all_gather(master_low, ("dp", "fsdp"), axis=0, tiled=True)
    back_pieces = unpack_all(back_params, dp_count, fsdp_count)
    w_query_back, w_key_back, w_value_back, w_out_back, w_up_back, w_down_back = back_pieces[:6]
    out_grad = cotangent.astype(jnp.float32)
    _, pull_ffn = jax.vjp(layer_norm, resid_ffn, gain_f, shift_f)
    resid_ffn_grad, grad_gain_ffn, grad_shift_ffn = pull_ffn(out_grad)
    ffn_grad = resid_ffn_grad.astype(jnp.bfloat16)
    hidden_grad = product(ffn_grad, w_down_back.T)
    _, pull_gelu = jax.vjp(partial(jax.nn.gelu, approximate=False), pre_act)
    pre_grad = pull_gelu(hidden_grad)[0].astype(jnp.bfloat16)
    normed_grad = resid_ffn_grad + product(pre_grad, w_up_back.T)
    _, pull_attn = jax.vjp(layer_norm, resid_attn, gain_a, shift_a)
    resid_attn_grad, grad_gain_attn, grad_shift_attn = pull_attn(normed_grad)
    attn_grad = resid_attn_grad.astype(jnp.bfloat16)
    heads_grad = product(attn_grad, w_out_back.T).astype(jnp.bfloat16)
    query_parts, inner_sum = lax.map(
        head_query_back, (query_heads, key_heads, value_heads, split_heads(heads_grad), logsum)
    )
    query_grad = merge_heads(query_parts).astype(jnp.bfloat16)
    queries_all, heads_grad_all = (
        lax.all_gather(queries, "fsdp", axis=0, tiled=True),
        lax.all_gather(heads_grad, "fsdp", axis=0, tiled=True),
    )
    logsum_all, inner_all = (
        lax.all_gather(logsum, "fsdp", axis=1, tiled=True),
        lax.all_gather(inner_sum, "fsdp", axis=1, tiled=True),
    )
    key_parts, value_parts = lax.map(
        head_key_back,
        (
            split_heads(keys_local),
            split_heads(values_local),
            split_heads(queries_all),
            split_heads(heads_grad_all),
            logsum_all,
            inner_all,
        ),
    )
    key_grad = merge_heads(key_parts).astype(jnp.bfloat16)
    value_grad = merge_heads(value_parts).astype(jnp.bfloat16)
    stream_grad = (
        resid_attn_grad
        + product(query_grad, w_query_back.T)
        + product(key_grad, w_key_back.T)
        + product(value_grad, w_value_back.T)
    )
    grad_b_time = jnp.sum(inside * stream_grad, axis=0)
    grad_w_time = time_frac * grad_b_time
    query_cols, key_cols, value_cols, attn_cols, ffn_cols, pre_cols = (
        lax.all_to_all(query_grad, "fsdp", split_axis=1, concat_axis=0, tiled=True),
        lax.all_to_all(key_grad, "fsdp", split_axis=1, concat_axis=0, tiled=True),
        lax.all_to_all(value_grad, "fsdp", split_axis=1, concat_axis=0, tiled=True),
        lax.all_to_all(attn_grad, "fsdp", split_axis=1, concat_axis=0, tiled=True),
        lax.all_to_all(ffn_grad, "fsdp", split_axis=1, concat_axis=0, tiled=True),
        lax.all_to_all(pre_grad, "fsdp", split_axis=1, concat_axis=0, tiled=True),
    )
    grad_w_query = product_inner(stream_all, query_cols)
    grad_w_key = product_inner(stream_all, key_cols)
    grad_w_value = product_inner(stream_all, value_cols)
    grad_w_out = product_inner(heads_all, attn_cols)
    grad_w_up = product_inner(normed_all, pre_cols)
    grad_w_down = product_inner(hidden_all, ffn_cols)
    grad_b_query = jnp.sum(query_cols.astype(jnp.float32), axis=0)
    grad_b_value = jnp.sum(value_cols.astype(jnp.float32), axis=0)
    grad_b_out = jnp.sum(attn_cols.astype(jnp.float32), axis=0)
    grad_b_down = jnp.sum(ffn_cols.astype(jnp.float32), axis=0)
    grad_b_up = jnp.sum(pre_cols.astype(jnp.float32), axis=0)
    vector_terms = jnp.stack(
        [grad_gain_attn, grad_shift_attn, grad_gain_ffn, grad_shift_ffn, grad_w_time, grad_b_time]
    )
    vector_part = lax.psum_scatter(vector_terms, "fsdp", scatter_dimension=1, tiled=True)
    vector_block = jnp.concatenate(
        [grad_b_query, grad_b_value, grad_b_out, grad_b_down, grad_b_up, vector_part.reshape(-1)]
    )
    grad_block = jnp.concatenate(
        [
            piece.reshape(-1)
            for piece in (
                grad_w_query,
                grad_w_key,
                grad_w_value,
                grad_w_out,
                grad_w_up,
                grad_w_down,
            )
        ]
        + [vector_block]
    )
    grad_shard = lax.psum_scatter(grad_block, "dp", scatter_dimension=0, tiled=True)
    vector_grad = lax.psum(vector_block, "dp")
    square_sum = lax.psum(jnp.sum(grad_shard * grad_shard), ("dp", "fsdp"))
    grad_norm = jnp.sqrt(square_sum)
    clip_limit = 4.0 * math.sqrt(PARAMS)
    clipped = grad_shard * (clip_limit / jnp.maximum(grad_norm, clip_limit))
    new_first = 0.9 * first_moment + 0.1 * clipped
    new_second = 0.98 * second_moment + 0.02 * clipped * clipped
    first_hat = new_first / (1.0 - 0.9**STEP)
    second_hat = new_second / (1.0 - 0.98**STEP)
    new_master = master - 0.02 * (first_hat / (jnp.sqrt(second_hat) + 1e-06) + 0.01 * master)
    new_average = 0.99 * average + 0.01 * new_master
    return (
        block_out,
        stream_grad,
        grad_norm,
        vector_grad,
        new_first,
        new_second,
        new_master,
        new_average,
    )


AXES = ("dp", "fsdp")


def send(values, route, name="move"):
    pairs = []
    for n in range(32):
        there = route(n // 8, n // 4 % 2, n // 2 % 2, n % 2)
        if there is not None:
            z, y, x, c = there
            pairs.append((n, z * 8 + y * 4 + x * 2 + c))
    with jax.named_scope(name):
        return lax.ppermute(values, AXES, pairs)


def to_core(z, y, x, c):
    return z, y, x, 1 - c


def to_x(z, y, x, c):
    return z, y, 1 - x, c


def to_y(z, y, x, c):
    return z, 1 - y, x, c


def to_near(z, y, x, c):
    return z ^ 1, y, x, c


def to_far(z, y, x, c):
    return z ^ 2, y, x, c


def only(route, planes):
    return lambda z, y, x, c: route(z, y, x, c) if z in planes else None


EVERY = (to_core, to_x, to_y, to_near, to_far)


def total(values, name):
    for route in EVERY:
        values = values + send(values, route, name)
    return values


def after(values, *earlier):
    return lax.optimization_barrier((values, *earlier))[0]


PLANES = ((1, 2, 3), (0, 1, 3), (0, 2), (0, 1, 2, 3))


def gather_pieces(own, z, y, tokens, run_attend):
    def across(name, values, n):
        return send(values, only(to_x, PLANES[n]), name)

    outer = (z == 0) | (z == 3)
    first = send(own, lambda z, y, x, c: ((2, 0, 3, 1)[z], y, x, c), "first")
    y0 = send(own, to_y, "y0")
    x0 = across("x0", own, 0)
    tokens_c = send(tokens, to_core, "tok_c")
    second = send(jnp.where(outer, own, first), to_near, "second")
    crossed = send(
        after(own, first), lambda z, y, x, c: (3 - z, y, x, c) if z in (1, 2) else None, "crossed"
    )
    y1 = send(after(first, y0, x0), to_y, "y1")
    x1 = across("x1", after(first, x0), 1)
    tokens_x = send(after(tokens, first, x0), to_x, "tok_x")
    third = send(after(crossed, second), only(to_near, (1, 2)), "third")
    y2 = send(after(second, y1), to_y, "y2")
    x_a = send(after(jnp.where(z % 2 == 0, second, y0), x1), to_x, "xa")
    last = jnp.where(outer, third, crossed)
    tokens_xc = send(after(tokens_x, third), to_core, "tok_xc")
    y3 = send(after(last, y2), to_y, "y3")
    y_b = send(after(jnp.where(z == 2, x0, x1), y2), to_y, "yb")
    yx2 = across("yx2", after(y2, last), 2)
    x3 = across("x3", after(last, y2), 3)
    tail_0, tail_1, tail_2 = (
        jnp.where(y == 1, mine[TAIL:], other[TAIL:])
        for mine, other in ((own, y0), (first, y1), (second, y2))
    )
    attended = run_attend(
        after(last, y2), (own, y0, first, y1, second, y2, last, x0, x1),
        (tokens, tokens_c, tokens_x, tokens_xc),
        jnp.where(z == 3, tail_0, jnp.where(z == 1, tail_1, tail_2)),
        jnp.where(z == 0, tail_0, jnp.where(z == 2, tail_1, tail_2)),
    )
    attended = lax.optimization_barrier((*attended, x_a, y3, yx2))[: len(attended)]
    stack = send(attended[-1], to_core, "stack")
    yx3 = across("yx3", after(y3, attended[-1]), 3)
    later = [
        send(after(piece, attended[-1]), only(to_core, planes), name)
        for piece, planes, name in (
            (x_a, (0, 1, 2, 3), "cxa"), (y3, (0, 1, 2, 3), "cy3"), (y_b, (0, 1, 2, 3), "cyb"),
            (yx2, PLANES[2], "cyx2"), (x3, (0, 1, 2, 3), "cx3"), (yx3, (0, 1, 2, 3), "cyx3"),
        )
    ]
    mine = [own, first, second, last, y0, y1, y2, x0, x1, x_a, y3, y_b, yx2, x3, yx3]
    return attended[:-1], [*mine, stack, *later]


def add(left, right):
    return wide(left) + wide(right)


def block_body(
    tokens,
    cotangent,
    master,
    first_moment,
    second_moment,
    average,
    timestep,
    block_length,
    block_start,
):
    shard = lax.axis_index("dp")
    j = lax.axis_index("fsdp")
    z, y = shard // 2, shard % 2
    place = jnp.stack([shard, z, y, j, block_start[0], block_length[0]]).astype(jnp.int32)
    flat = jnp.pad(master, (0, LANE_ROWS * 128 - SHARD)).reshape(LANE_ROWS, 128)
    vec_rows = jnp.pad(master[SHARD - 3584 :].reshape(14, 256), ((0, 2), (0, 0)))
    head_rows = jnp.pad(master[SHARD - 896 :], (0, 3200)).reshape(16, 256)
    tail = low(jnp.where(shard == 7, vec_rows, head_rows))
    tail_x = send(tail, to_x, "tail_x")
    tail_c = send(jnp.concatenate([tail, tail_x]), to_core, "tail_c")
    own = pack(place, flat, jnp.concatenate([tail, tail_c[:16], tail_x, tail_c[16:]]))
    here = (jnp.arange(4) == j)[:, None, None]
    time_frac = timestep[0].astype(jnp.float32) / 5000.0
    vectors = {}

    def absolute(relative):
        blocks = relative.reshape(4, 16, 256)
        blocks = jnp.where(j % 2 == 1, jnp.concatenate([blocks[1:2], blocks[0:1], blocks[3:4], blocks[2:3]]), blocks)
        return jnp.where(j // 2 == 1, jnp.concatenate([blocks[2:4], blocks[0:2]]), blocks)

    def run_attend(ready, held, all_tokens, vec_tail, head_tail):
        vec = wide(absolute(vec_tail))
        full = vec.transpose(1, 0, 2).reshape(16, D)
        vec_own = wide(vec_tail[:16])
        vectors["embed"] = time_frac * full[12:13] + full[13:14]
        vectors["rows"] = jnp.concatenate([full[2:4], full[8:12], jnp.zeros((2, D), jnp.float32)])
        vectors["up"] = vec[:, 4:8].reshape(16, 256)
        vectors["head"] = absolute(head_tail)
        return attend(after(place, ready), all_tokens, vectors["embed"], vec_own[0:8], held)

    attended, pieces = gather_pieces(own, z, y, tokens, run_attend)
    stream, weight, query, key, value, h0, h1, h2, h3, lse = attended

    def to_relative(r):
        return lambda z, y, x, c: (z, y, x ^ (r // 2), c ^ (r % 2))

    def exchange(blocks, name):
        return [blocks[0]] + [send(blocks[r], to_relative(r), name) for r in range(1, 4)]

    (block_out, resid_grad, g0, g1, g2, g3, sums, sums_up, head_grad, *grads) = layer(
        place, exchange((h0, h1, h2, h3), "heads"), tokens, cotangent, vectors["embed"],
        vectors["rows"], vectors["up"], vectors["head"], pieces,
    )
    grads_own, grads_other = grads[:3], grads[3:]

    moved = {k: send(grads_other[k - 1], to_core, f"rc{k}") for k in (2, 1)}
    moved[3] = send(after(grads_other[2], moved[2], moved[1]), to_core, "rc3")

    def over_cores(k, a, b):
        return add(grads_own[k - 1][a, b], moved[k][a, b])

    grad_heads = exchange((g0, g1, g2, g3), "heads_grad")
    starts = {
        name: after(low(over_cores(k, 1, b)), *grad_heads)
        for name, k, b in (("d1", 1, 1), ("d2", 2, 1), ("e1", 1, 0), ("e2", 2, 0))
    }
    d1 = send(starts["d1"], to_y, "d1")
    d2 = send(starts["d2"], to_x, "d2")
    e1 = send(starts["e1"], to_y, "e1")
    e2 = send(starts["e2"], to_x, "e2")

    (q_grad, k_grad, v_grad, kept, sent, sums_qkv) = attend_back(
        after(place, *starts.values()),
        query, key, value, lse, weight, grad_heads,
    )

    q_grad, k_grad, v_grad, kept, sent, sums_qkv, d1, d2 = lax.optimization_barrier(
        (q_grad, k_grad, v_grad, kept, sent, sums_qkv, d1, d2)
    )
    f1 = send(low(over_cores(1, 0, 1) + wide(d1)), to_x, "f1")
    f2 = send(low(over_cores(2, 0, 1) + wide(d2)), to_y, "f2")
    d3 = send(after(low(over_cores(3, 1, 1)), e1, e2), to_x, "d3")
    e3 = send(after(low(over_cores(3, 1, 0)), f1), to_x, "e3")

    rows = stream.reshape(1024, D)
    w_grads = [low(product_inner(rows, grad)) for grad in (q_grad, k_grad, v_grad)]
    rest = jnp.zeros((PIECE - 1552, 256), jnp.bfloat16)
    piece_0 = jnp.concatenate([w_grads[0], w_grads[1][:528], rest])
    piece_1 = jnp.concatenate([w_grads[1][512:], w_grads[2], rest, rest[:16]])
    low_row = y == 0
    ry0 = send(after(jnp.where(low_row, piece_1, piece_0), e1), to_y, "ry0")
    f3 = send(low(over_cores(3, 0, 1) + wide(after(d3, ry0))), to_y, "f3")

    kept_1, sent_1 = combine(
        place, (grads_own[1], moved[2], e2, f2), (grads_own[0], moved[1], e1, f1)
    )
    inner_part = low(add(kept_1, send(sent_1, to_near, "rz_inner1")))
    inner_last = send(inner_part, only(to_far, (0, 3)), "rz_inner2")
    kept_0, sent_0 = combine(
        place, (jnp.where(low_row, piece_0, piece_1), ry0), (grads_own[2], moved[3], e3, f3)
    )
    outer_part = low(add(kept_0, send(sent_0, to_near, "rz_outer1")))
    outer_last = send(outer_part, only(to_far, (1, 2)), "rz_outer2")

    from_core = send(sent, to_core, "in_c")
    in_x = send(after(low(kept[1] + wide(from_core[1])), e3), to_x, "in_x")
    input_grad = (
        resid_grad
        + kept[0]
        + wide(from_core[0])
        + wide(in_x)
    )

    time_grad = sums[6] + sums_qkv[0]
    rows_of = [sums[0], sums[1]]
    vec_grad = jnp.concatenate(
        [
            jnp.where(here, sums_qkv[1:3, :256][None], 0.0),
            sums[0:2].reshape(2, 4, 256).transpose(1, 0, 2),
            sums_up.reshape(4, 4, 256),
            sums[2:6].reshape(4, 4, 256).transpose(1, 0, 2),
            (time_frac * time_grad).reshape(4, 1, 256),
            time_grad.reshape(4, 1, 256),
            jnp.zeros((4, 2, 256), jnp.float32),
            head_grad,
        ],
        axis=1,
    )
    vec_grad = vec_grad.reshape(2, 2, 32, 256)
    core_bit, x_bit = j % 2, j // 2
    kept_c = jnp.where(core_bit == 1, vec_grad[:, 1], vec_grad[:, 0])
    sent_c = jnp.where(core_bit == 1, vec_grad[:, 0], vec_grad[:, 1])
    by_x = kept_c + send(sent_c, to_core, "vec_c")
    kept_x = jnp.where(x_bit == 1, by_x[1], by_x[0])
    mine = kept_x + send(jnp.where(x_bit == 1, by_x[0], by_x[1]), to_x, "vec_x")

    grad_flat, square = unpack(after(place, input_grad), inner_part, inner_last, outer_part, outer_last)
    mine = jnp.concatenate([mine, square.reshape(4, 256), jnp.zeros((4, 256), jnp.float32)])
    for route in (to_y, to_near, to_far):
        mine = mine + send(mine, route, "norm")
    vec_sum, head_sum = mine[:14].reshape(-1), mine[16:20].reshape(-1)[:896]
    vector_grad = vec_sum
    square_sum = (jnp.sum(mine[32:36]) + jnp.sum(vec_sum * vec_sum) + jnp.sum(head_sum * head_sum))
    square_sum = jnp.broadcast_to(square_sum, (8, 128))
    for route in (to_x, to_core):
        square_sum = square_sum + send(square_sum, route, "norm")
    grad_norm = jnp.sqrt(square_sum[0, 0])
    grad_flat = grad_flat.reshape(-1)
    edge = grad_flat[SHARD - 3584 : SHARD]
    edge = jnp.where(
        shard == 7,
        vec_sum,
        jnp.where(shard == 1, jnp.concatenate([edge[: 3584 - 896], head_sum]), edge),
    )
    grad_shard = lax.dynamic_update_slice(grad_flat, edge, (SHARD - 3584,))[:SHARD]
    clip_limit = 4.0 * math.sqrt(PARAMS)
    clipped = grad_shard * (clip_limit / jnp.maximum(grad_norm, clip_limit))
    new_first = 0.9 * first_moment + 0.1 * clipped
    new_second = 0.98 * second_moment + 0.02 * clipped * clipped
    first_hat = new_first / (1.0 - 0.9**STEP)
    second_hat = new_second / (1.0 - 0.98**STEP)
    new_master = master - 0.02 * (first_hat / (jnp.sqrt(second_hat) + 1e-06) + 0.01 * master)
    new_average = 0.99 * average + 0.01 * new_master
    return (
        block_out,
        input_grad,
        grad_norm,
        vector_grad,
        new_first,
        new_second,
        new_master,
        new_average,
    )


def solution(mesh):
    return jax.shard_map(
        block_body if mesh.shape["dp"] == 8 and mesh.shape["fsdp"] == 4 else body,
        mesh=mesh,
        in_specs=(
            P(("dp", "fsdp"), None),
            P(("dp", "fsdp"), None),
            P(("dp", "fsdp")),
            P(("dp", "fsdp")),
            P(("dp", "fsdp")),
            P(("dp", "fsdp")),
            P("dp"),
            P("dp"),
            P("dp"),
        ),
        out_specs=(
            P(("dp", "fsdp"), None),
            P(("dp", "fsdp"), None),
            P(),
            P("fsdp"),
            P(("dp", "fsdp")),
            P(("dp", "fsdp")),
            P(("dp", "fsdp")),
            P(("dp", "fsdp")),
        ),
        check_vma=False,
    )
```

```python
from functools import partial
import math

import jax
import jax.numpy as jnp
from jax import lax
from jax.experimental import pallas as pl
from jax.experimental.pallas import tpu as pltpu
from jax.sharding import PartitionSpec as P

D = 1024
H = 16
DH = 64
FF = 4096
STEP = 10
PARAMS = 12597248
NORM_EPS = 1e-05

SHARD = PARAMS // 32
PIECE = 1600
LANE_ROWS = 3080
PAD = 128
TAIL = 1536
REGIONS = (
    ("q", 0, 1024, 256),
    ("k", 262144, 1024, 256),
    ("v", 524288, 1024, 256),
    ("o", 786432, 1024, 256),
    ("up", 1048576, 1024, 1024),
    ("down", 2097152, 4096, 256),
    ("vec", 3145728, 16, 256),
)


def segments(shard):
    low, high = shard * SHARD, (shard + 1) * SHARD
    found, offset = [], 0
    for name, start, rows, width in REGIONS:
        size = 3584 if name == "vec" else rows * width
        first, last = max(low, start), min(high, start + size)
        if first >= last:
            continue
        row_a = (first - start) // width // 16 * 16
        row_b = min(rows, -(-(-(-(last - start) // width)) // 16) * 16)
        found.append((name, row_a, row_b, offset, width // 128, start // 128))
        offset += (row_b - row_a) * (width // 256)
    return found


def lane_start(shard):
    return shard * SHARD // 128


SEGMENTS = [segments(shard) for shard in range(8)]
SLOT = ((0, 1, 3, 2), (2, 0, 3, 1), (1, 3, 0, 2), (2, 3, 1, 0))


def buffers(z):
    x_a, y_b = 9, 11
    over_x = [7, 8, x_a, 13]
    both = [y_b if z == 2 else x_a, y_b, 12, 14]
    return [0, 1, 2, 3, 4, 5, 6, 10, *over_x, *both]


BUFFER = [buffers(z) for z in range(4)]


def dot(left, right):
    return jnp.dot(left, right, preferred_element_type=jnp.float32)


def dot_last(left, right):
    return lax.dot_general(
        left, right, (((1,), (1,)), ((), ())), preferred_element_type=jnp.float32
    )


def dot_first(left, right):
    return lax.dot_general(
        left, right, (((0,), (0,)), ((), ())), preferred_element_type=jnp.float32
    )


def low(values):
    return values.astype(jnp.bfloat16)


def wide(values):
    return values.astype(jnp.float32)


VMEM = pl.BlockSpec(memory_space=pltpu.VMEM)
SMEM = pl.BlockSpec(memory_space=pltpu.SMEM)
ANY = pl.BlockSpec(memory_space=pl.ANY)


def struct(shape, kind=jnp.bfloat16):
    return jax.ShapeDtypeStruct(shape, kind)


def chunks(rows, most=128):
    return [(a, min(most, rows - a)) for a in range(0, rows, most)]


def pack_kernel(place, flat, tails, piece, rolled, rows):
    shard = place[0]
    rows[0:PAD, :] = jnp.zeros((PAD, 128), jnp.float32)
    rows[PAD + LANE_ROWS : PAD + LANE_ROWS + PAD, :] = jnp.zeros((PAD, 128), jnp.float32)
    rolled[0:8, :] = jnp.zeros((8, 128), jnp.float32)

    @pl.when(shard % 2 == 0)
    def _():
        for a, n in chunks(LANE_ROWS):
            rows[PAD + a : PAD + a + n, :] = flat[a : a + n, :]

    @pl.when(shard % 2 == 1)
    def _():
        for a, n in chunks(LANE_ROWS):
            rolled[8 + a : 8 + a + n, :] = pltpu.roll(flat[a : a + n, :], 64, 1)
        for a, n in chunks(LANE_ROWS):
            lane = lax.broadcasted_iota(jnp.int32, (n, 128), 1)
            rows[PAD + a : PAD + a + n, :] = jnp.where(
                lane < 64, rolled[7 + a : 7 + a + n, :], rolled[8 + a : 8 + a + n, :]
            )

    for case in range(8):

        @pl.when(shard == case)
        def _(case=case):
            for _, row_a, row_b, offset, step, first in SEGMENTS[case]:
                if offset == TAIL:
                    piece[TAIL:PIECE, :] = tails[...]
                    continue
                count = row_b - row_a
                base = PAD + first + step * row_a - lane_start(case)
                for t in range(step):
                    out = offset + t // 2 * count
                    lanes = slice(t % 2 * 128, t % 2 * 128 + 128)
                    for a, n in chunks(count):
                        piece[out + a : out + a + n, lanes] = low(
                            rows[pl.ds(base + t + step * a, n, stride=step), :]
                        )


def pack(place, flat, tails):
    return pl.pallas_call(
        pack_kernel,
        out_shape=struct((PIECE, 256)),
        in_specs=[SMEM, VMEM, VMEM],
        out_specs=VMEM,
        scratch_shapes=[
            pltpu.VMEM((8 + LANE_ROWS, 128), jnp.float32),
            pltpu.VMEM((PAD + LANE_ROWS + PAD, 128), jnp.float32),
        ],
        compiler_params=pltpu.CompilerParams(vmem_limit_bytes=24 << 20),
        name="pack",
    )(place, flat, tails)


def unpack_kernel(place, inner, inner_last, outer, outer_last, flat, square, rows, left, right, sem):
    shard = place[0]
    is_inner = (place[1] == 1) | (place[1] == 2)

    def fetch(first, second):
        copies = [
            pltpu.make_async_copy(first, left, sem.at[0]),
            pltpu.make_async_copy(second, right, sem.at[1]),
        ]
        for copy in copies:
            copy.start()
        for copy in copies:
            copy.wait()

    @pl.when(is_inner)
    def _():
        fetch(inner, inner_last)

    @pl.when(jnp.logical_not(is_inner))
    def _():
        fetch(outer, outer_last)

    for case in range(8):

        @pl.when(shard == case)
        def _(case=case):
            for _, row_a, row_b, offset, step, first in SEGMENTS[case]:
                count = row_b - row_a
                base = PAD + first + step * row_a - lane_start(case)
                for t in range(step):
                    source = offset + t // 2 * count
                    lanes = slice(t % 2 * 128, t % 2 * 128 + 128)
                    for a, n in chunks(count):
                        spot = slice(source + a, source + a + n)
                        value = wide(left[spot, lanes]) + wide(right[spot, lanes])
                        if offset == TAIL:
                            value = jnp.zeros((n, 128), jnp.float32)
                        rows[pl.ds(base + t + step * a, n, stride=step), :] = value

    square[...] = jnp.zeros_like(square)
    for odd in range(2):

        @pl.when(shard % 2 == odd)
        def _(odd=odd):
            total = jnp.zeros((8, 128), jnp.float32)
            for a, n in chunks(LANE_ROWS):
                value = rows[PAD + a : PAD + a + n, :]
                lane = lax.broadcasted_iota(jnp.int32, (n, 128), 1)
                if odd:
                    after = rows[PAD + a + 1 : PAD + a + 1 + n, :]
                    value = jnp.where(
                        lane < 64, pltpu.roll(value, 64, 1), pltpu.roll(after, 64, 1)
                    )
                if (a + n) * 128 > SHARD:
                    row = lax.broadcasted_iota(jnp.int32, (n, 128), 0) + a
                    value = jnp.where(row * 128 + lane < SHARD, value, 0.0)
                flat[a : a + n, :] = value
                total += jnp.sum((value * value).reshape(n // 8, 8, 128), axis=0)
            square[...] = total


def unpack(place, *pieces):
    return pl.pallas_call(
        unpack_kernel,
        out_shape=(struct((LANE_ROWS, 128), jnp.float32), struct((8, 128), jnp.float32)),
        in_specs=[SMEM] + [ANY] * 4,
        out_specs=(VMEM, VMEM),
        scratch_shapes=[
            pltpu.VMEM((PAD + LANE_ROWS + PAD, 128), jnp.float32),
            pltpu.VMEM((PIECE, 256), jnp.bfloat16),
            pltpu.VMEM((PIECE, 256), jnp.bfloat16),
            pltpu.SemaphoreType.DMA((2,)),
        ],
        compiler_params=pltpu.CompilerParams(vmem_limit_bytes=60 << 20),
        name="unpack",
    )(place, *pieces)


def combine_kernel(split, place, *refs):
    kept, sent = refs[-2:]
    first = sum(wide(ref[...]) for ref in refs[:split])
    second = sum(wide(ref[...]) for ref in refs[split:-2])
    even = place[1] % 2 == 0
    kept[...] = low(jnp.where(even, first, second))
    sent[...] = low(jnp.where(even, second, first))


def combine(place, first, second):
    blocks = 2
    size = PIECE // blocks

    def spec(piece):
        if piece.ndim == 4:
            return pl.BlockSpec((None, None, size, 256), lambda n: (0, 0, n, 0))
        return pl.BlockSpec((size, 256), lambda n: (n, 0))

    pieces = [*first, *second]
    return pl.pallas_call(
        partial(combine_kernel, len(first)),
        grid=(blocks,),
        out_shape=(struct((PIECE, 256)), struct((PIECE, 256))),
        in_specs=[SMEM] + [spec(piece) for piece in pieces],
        out_specs=(pl.BlockSpec((size, 256), lambda n: (n, 0)),) * 2,
        compiler_params=pltpu.CompilerParams(vmem_limit_bytes=60 << 20),
        name="combine",
    )(place, *pieces)


def column_sum(values):
    return jnp.sum(values, axis=0, keepdims=True)


def inside_column(place, relative):
    rows = lax.broadcasted_iota(jnp.int32, (256, 1), 0)
    position = rows + (place[3] ^ relative) * 256
    return ((position >= place[4]) & (position < place[4] + place[5])).astype(jnp.float32)


def attend_kernel(
    place, embed, bias, t0, t1, t2, t3, p0, p1, p2, p3, p4, p5, p6, p7, p8,
    stream_out, weight_out, q_out, k_out, v_out, h0, h1, h2, h3, lse_out, stack,
    tokens, staged, q_heads, k_t, v_heads, o_heads, edge, sem, sem_tokens, sem_in, sem_out,
):
    fetches = [
        pltpu.make_async_copy(ref, tokens.at[r], sem_tokens.at[r])
        for r, ref in enumerate((t0, t1, t2, t3))
    ]
    for copy in fetches:
        copy.start()

    def copies(first, second):
        return [
            pltpu.make_async_copy(first.at[0:1024, :], weight_out.at[0], sem.at[0]),
            pltpu.make_async_copy(first.at[1024:1552, :], weight_out.at[1, 0:528, :], sem.at[1]),
            pltpu.make_async_copy(second.at[16:512, :], weight_out.at[1, 528:1024, :], sem.at[2]),
            pltpu.make_async_copy(second.at[0:16, :], edge, sem.at[3]),
            pltpu.make_async_copy(second.at[512:1536, :], weight_out.at[2], sem.at[4]),
        ]

    held = ((p0, p1), (p2, p3), (p4, p5))
    for z in range(4):
        for y in range(2):
            own, other = held[SLOT[z][0]]
            pair = (other, own) if y else (own, other)

            @pl.when((place[1] == z) & (place[2] == y))
            def _(pair=pair):
                for copy in copies(*pair):
                    copy.start()

    held_in = [
        pltpu.make_async_copy(ref, staged.at[n], sem_in.at[n])
        for n, ref in enumerate((p0, p2, p4, p6, p1, p3, p5, p7, p8))
    ]
    held_out = [pltpu.make_async_copy(staged.at[n], stack.at[n], sem_out.at[n]) for n in range(9)]
    for copy in held_in:
        copy.start()
    for r, copy in enumerate(fetches):
        copy.wait()
        stream_out[r] = low(wide(tokens[r]) + inside_column(place, r) * embed[...])
    lanes = lax.broadcasted_iota(jnp.int32, (1024, 128), 1)
    v_heads[...] = jnp.broadcast_to((lanes >= 64).astype(jnp.bfloat16), (4, 1024, 128))
    for copy in copies(p0, p1):
        copy.wait()
    weight_out[1, 512:528, :] = weight_out[1, 512:528, :] + edge[...]
    for r in range(4):
        rows = slice(r * 256, r * 256 + 256)
        stream = stream_out[r]
        query = low(dot(stream, weight_out[0]) + bias[0:1, :])
        key = low(dot(stream, weight_out[1]))
        value = low(dot(stream, weight_out[2]) + bias[1:2, :])
        q_out[rows, :] = query
        k_out[rows, :] = key
        v_out[rows, :] = value
        for h in range(4):
            cols = slice(h * 64, h * 64 + 64)
            q_heads[h, rows, :] = query[:, cols] * 0.125
            v_heads[h, rows, 0:64] = value[:, cols]
        k_t[:, rows] = key.T
    lse_out[...] = jnp.zeros_like(lse_out)
    for before, copy in zip(held_in, held_out):
        before.wait()
        copy.start()

    def head_step(h, _):
        key_t = k_t[pl.ds(pl.multiple_of(h * 64, 64), 64), :]
        for r in range(4):
            rows = slice(r * 256, r * 256 + 256)
            scores = dot(q_heads[h, rows, :], key_t)
            highest = jnp.max(scores, axis=1, keepdims=True)
            weights = low(jnp.exp(scores - highest))
            result = dot(weights, v_heads[h])
            total = result[:, 64:65]
            o_heads[h, rows, :] = low(result[:, 0:64] / total)
            lane = lax.broadcasted_iota(jnp.int32, (256, 128), 1)
            lse_out[rows, :] = jnp.where(lane == h, highest + jnp.log(total), lse_out[rows, :])
        return 0

    lax.fori_loop(0, 4, head_step, 0, unroll=4)
    for r, out in enumerate((h0, h1, h2, h3)):
        for h in range(4):
            out[:, h * 64 : h * 64 + 64] = o_heads[h, r * 256 : r * 256 + 256, :]
    for copy in held_out:
        copy.wait()


def attend(place, tokens, embed, bias, pieces):
    square = struct((1024, 256))
    block = struct((256, 256))
    return pl.pallas_call(
        attend_kernel,
        out_shape=(
            struct((4, 256, 1024)), struct((3, 1024, 256)), square, square, square,
            block, block, block, block, struct((1024, 128), jnp.float32), struct((9, PIECE, 256)),
        ),
        in_specs=[SMEM] + [VMEM] * 2 + [ANY] * 13,
        out_specs=(VMEM,) * 10 + (ANY,),
        scratch_shapes=[
            pltpu.VMEM((4, 256, 1024), jnp.bfloat16),
            pltpu.VMEM((9, PIECE, 256), jnp.bfloat16),
            pltpu.VMEM((4, 1024, 64), jnp.bfloat16),
            pltpu.VMEM((256, 1024), jnp.bfloat16),
            pltpu.VMEM((4, 1024, 128), jnp.bfloat16),
            pltpu.VMEM((4, 1024, 64), jnp.bfloat16),
            pltpu.VMEM((16, 256), jnp.bfloat16),
            pltpu.SemaphoreType.DMA((5,)),
            pltpu.SemaphoreType.DMA((4,)),
            pltpu.SemaphoreType.DMA((9,)),
            pltpu.SemaphoreType.DMA((9,)),
        ],
        compiler_params=pltpu.CompilerParams(vmem_limit_bytes=48 << 20),
        cost_estimate=pl.CostEstimate(
            flops=16_000_000_000, bytes_accessed=24_000_000, transcendentals=4_194_304
        ),
        name="attend",
    )(place, embed, bias, *tokens, *pieces)


def attend_back_kernel(
    place, q_in, k_in, v_in, lse, weight, g0, g1, g2, g3,
    q_grad, k_grad, v_grad, kept, sent, sums,
    q_heads, k_heads, g_heads, q_t, k_t, v_t, g_t, dq_heads, dk_t, dv_t,
):
    for r, grad in enumerate((g0, g1, g2, g3)):
        rows = slice(r * 256, r * 256 + 256)
        g_t[:, rows] = grad[...].T
        for h in range(4):
            cols = slice(h * 64, h * 64 + 64)
            q_heads[h, rows, :] = q_in[rows, cols] * 0.125
            k_heads[h, rows, :] = k_in[rows, cols]
            g_heads[h, rows, :] = grad[:, cols]
    q_t[...] = (q_in[...] * 0.125).T
    k_t[...] = k_in[...].T
    v_t[...] = v_in[...].T

    def head_step(h, _):
        mine = pl.ds(pl.multiple_of(h * 64, 64), 64)
        key_t, value_t, key = k_t[mine, :], v_t[mine, :], k_heads[h]
        key_sum = jnp.zeros((64, 1024), jnp.float32)
        value_sum = jnp.zeros((64, 1024), jnp.float32)
        for r in range(4):
            rows = slice(r * 256, r * 256 + 256)
            scores = dot(q_heads[h, rows, :], key_t)
            lane = lax.broadcasted_iota(jnp.int32, (256, 128), 1)
            logsum = jnp.sum(jnp.where(lane == h, lse[rows, :], 0.0), axis=1, keepdims=True)
            probs = jnp.exp(scores - logsum)
            weighted = probs * dot(g_heads[h, rows, :], value_t)
            inner = jnp.sum(weighted, axis=1, keepdims=True)
            score_grad = low(weighted - probs * inner)
            dq_heads[h, rows, :] = low(dot(score_grad, key) * 0.125)
            key_sum += dot(q_t[mine, rows], score_grad)
            value_sum += dot(g_t[mine, rows], low(probs))
        dk_t[mine, :] = low(key_sum)
        dv_t[mine, :] = low(value_sum)
        return 0

    lax.fori_loop(0, 4, head_step, 0, unroll=4)
    for h in range(4):
        q_grad[:, h * 64 : h * 64 + 64] = dq_heads[h]
    k_grad[...] = dk_t[...].T
    v_grad[...] = dv_t[...].T
    sums[...] = jnp.zeros_like(sums)
    sums[1:2, 0:256] = column_sum(wide(q_grad[...]))
    sums[2:3, 0:256] = column_sum(wide(v_grad[...]))
    for r in range(4):
        rows = slice(r * 256, r * 256 + 256)
        part = (
            dot_last(q_grad[rows, :], weight[0])
            + dot_last(k_grad[rows, :], weight[1])
            + dot_last(v_grad[rows, :], weight[2])
        )
        sums[0:1, :] += column_sum(inside_column(place, r) * part)
        if r % 2:
            sent[r // 2] = low(part)
        else:
            kept[r // 2] = part


def attend_back(place, query, key, value, lse, weight, grads):
    square = struct((1024, 256))
    return pl.pallas_call(
        attend_back_kernel,
        out_shape=(
            square, square, square, struct((2, 256, D), jnp.float32), struct((2, 256, D)),
            struct((8, D), jnp.float32),
        ),
        in_specs=[SMEM] + [VMEM] * 9,
        out_specs=(VMEM,) * 6,
        scratch_shapes=[pltpu.VMEM((4, 1024, 64), jnp.bfloat16)] * 3
        + [pltpu.VMEM((256, 1024), jnp.bfloat16)] * 4
        + [pltpu.VMEM((4, 1024, 64), jnp.bfloat16)]
        + [pltpu.VMEM((256, 1024), jnp.bfloat16)] * 2,
        compiler_params=pltpu.CompilerParams(vmem_limit_bytes=40 << 20),
        cost_estimate=pl.CostEstimate(
            flops=20_000_000_000, bytes_accessed=12_000_000, transcendentals=4_194_304
        ),
        name="attend_back",
    )(place, query, key, value, lse, weight, *grads)


def row_mean(values):
    return jnp.sum(values, axis=1, keepdims=True) * (1.0 / D)


def normalise(resid):
    centred = resid - row_mean(resid)
    scale = lax.rsqrt(row_mean(centred * centred) + NORM_EPS)
    return centred * scale, scale


def normalise_back(grad, gain, xhat, scale):
    scaled = grad * gain
    return (scaled - row_mean(scaled) - xhat * row_mean(scaled * xhat)) * scale


def target_piece(targets, k, ry, rx):
    return targets[k - 1].at[ry, rx] if k == 1 else targets[k - 1].at[rx, ry]


def layer_kernel(
    place, h0, h1, h2, h3, tokens, cotangent, embed, vectors, bias_up, out_head, *refs
):
    stack = refs[15]
    pieces = (refs[:15], [stack.at[n] for n in range(9)] + list(refs[16:22]))
    refs = refs[22:]
    (block_out, resid_grad, g0, g1, g2, g3, sums, sums_up, head_grad) = refs[:9]
    grads_own, grads_other = refs[9:12], refs[12:15]
    (w_out, w_up, w_down, edge_up, edge_down, hidden, slope, grad_up, grad_down,
     grad_out, acc, acc_t, grad_t, sem, sem_out) = refs[15:]

    def fetch(z, y):
        made = {"out": [], "up": [], "down": []}
        for k in range(1, 4):
            for ry in range(2):
                case = 2 * k + (y ^ ry)
                for r in range(4):
                    rx, rc = r // 2, r % 2
                    source = pieces[rc][BUFFER[z][rx * 8 + ry * 4 + SLOT[z][k]]]
                    column = place[3] ^ r
                    for name, row_a, row_b, offset, step, _ in SEGMENTS[case]:
                        count = row_b - row_a
                        if name == "o":
                            made["out"].append(
                                (source.at[offset : offset + count, :], w_out.at[:, pl.ds(column * 256, 256)])
                            )
                        elif name == "up":
                            block = source.at[offset : offset + 4 * count, :].reshape(4, count, 256)
                            target = w_up.at[pl.ds(column * 4, 4)]
                            skip = 0
                            if row_a:
                                skip = 16
                                made["up"].append(
                                    (block.at[:, 0:16, :], edge_up.at[case - 3, pl.ds(column * 4, 4)])
                                )
                            made["up"].append(
                                (block.at[:, skip:count, :], target.at[:, row_a + skip : row_b, :])
                            )
                        elif name == "down":
                            skip = 0
                            if row_a:
                                skip = 16
                                made["down"].append(
                                    (source.at[offset : offset + 16, :], edge_down.at[case - 6, :, pl.ds(column * 256, 256)])
                                )
                            made["down"].append(
                                (source.at[offset + skip : offset + count, :],
                                 w_down.at[row_a + skip : row_b, pl.ds(column * 256, 256)])
                            )
        return made

    order = ("out", "up", "down")
    for z in range(4):
        for y in range(2):

            @pl.when((place[1] == z) & (place[2] == y))
            def _(z=z, y=y):
                made = fetch(z, y)
                for n, name in enumerate(order):
                    for source, target in made[name]:
                        pltpu.make_async_copy(source, target, sem.at[n]).start()

    def arrived(refs, n):
        for ref in refs:
            pltpu.make_async_copy(ref, ref, sem.at[n]).wait()

    here = inside_column(place, 0)
    stream = wide(tokens[...]) + here * embed[...]
    arrived([w_out], 0)
    for n in range(4):
        cols = slice(n * 256, n * 256 + 256)
        w_out[0:16, cols] = w_out[0:16, cols] + out_head[n]
    heads = (h0, h1, h2, h3)

    def head_rows(r):
        return pl.ds(pl.multiple_of((place[3] ^ r) * 256, 256), 256)

    acc[...] = sum(dot(heads[r][...], w_out[head_rows(r), :]) for r in range(4))
    bias_out, bias_down, gain_a, shift_a, gain_f, shift_f = (vectors[n : n + 1, :] for n in range(6))
    xhat_a, scale_a = normalise(stream + acc[...] + bias_out)
    normed = xhat_a * gain_a + shift_a
    normed_low = low(normed)

    arrived([w_up] + [edge_up], 1)
    for n, row in enumerate((128, 512, 896)):
        w_up[:, row : row + 16, :] = w_up[:, row : row + 16, :] + edge_up[n]

    def up(g, _):
        pre = dot(normed_low, w_up[g]) + bias_up[pl.ds(g, 1), :]
        inner = 0.5 * (1.0 + lax.erf(pre * (1.0 / math.sqrt(2.0))))
        hidden[:, pl.ds(pl.multiple_of(g * 256, 256), 256)] = low(pre * inner)
        bend = inner + pre * (jnp.exp(-0.5 * pre * pre) * (1.0 / math.sqrt(2.0 * math.pi)))
        slope[pl.ds(pl.multiple_of(g * 256, 256), 256), :] = bend.T
        return 0

    lax.fori_loop(0, 16, up, 0, unroll=8)
    arrived([w_down] + [edge_down], 2)
    for n, row in enumerate((1024, 2560)):
        w_down[row : row + 16, :] = w_down[row : row + 16, :] + edge_down[n]
    acc[...] = normed + bias_down + dot(hidden[...], w_down[...])
    xhat_f, scale_f = normalise(acc[...])
    block_out[...] = low(xhat_f * gain_f + shift_f)

    out_grad = wide(cotangent[...])
    sums[4:5, :] = column_sum(out_grad * xhat_f)
    sums[5:6, :] = column_sum(out_grad)
    acc[...] = normalise_back(out_grad, gain_f, xhat_f, scale_f)
    ffn_grad = low(acc[...])
    sums[1:2, :] = column_sum(wide(ffn_grad))
    grad_t[...] = ffn_grad.T
    normed_t = normed_low.T

    def routes(case, name):
        return [
            (row_a, row_b, offset, row_b - row_a)
            for seg, row_a, row_b, offset, _, _ in SEGMENTS[case]
            if seg == name
        ]

    def outputs_up(case, column, targets, rx):
        piece = target_piece(targets, case // 2, place[2] ^ (case % 2), rx)
        return [
            pltpu.make_async_copy(
                grad_up.at[column * 4 : column * 4 + 4, row_a:row_b, :],
                piece.at[offset : offset + 4 * count, :].reshape(4, count, 256),
                sem_out.at[0],
            )
            for row_a, row_b, offset, count in routes(case, "up")
        ]

    def outputs(case):
        made = []
        for r in range(4):
            rx, rc = r // 2, r % 2
            column = place[3] ^ r
            targets = grads_other if rc else grads_own
            piece = target_piece(targets, case // 2, place[2] ^ (case % 2), rx)
            for row_a, row_b, offset, count in routes(case, "down"):
                source = grad_down.at[row_a:row_b, pl.ds(column * 256, 256)]
                target = piece.at[offset : offset + count, :]
                made.append(pltpu.make_async_copy(source, target, sem_out.at[0]))
        return made

    acc_t[...] = jnp.zeros_like(acc_t)

    for chunk in range(4):
        rows = slice(chunk * 1024, chunk * 1024 + 1024)
        pre_grad_t = low(dot(w_down[rows, :], grad_t[...]) * slope[rows, :])
        pre_grad = pre_grad_t.T
        sums_up[chunk : chunk + 1, :] = column_sum(wide(pre_grad))
        for n in range(4):
            g = chunk * 4 + n
            acc_t[...] += dot(w_up[g], pre_grad_t[n * 256 : n * 256 + 256, :])
            grad_up[g] = low(dot(normed_t, pre_grad[:, n * 256 : n * 256 + 256]))
        grad_down[rows, :] = low(dot_first(hidden[:, rows], ffn_grad))
        relative = place[3] ^ chunk
        for side, targets in enumerate((grads_own, grads_other)):

            @pl.when(relative % 2 == side)
            def _(chunk=chunk, targets=targets, relative=relative):
                for case in range(2, 6):
                    for copy in outputs_up(case, chunk, targets, relative // 2):
                        copy.start()

        for case in {1: (5,), 2: (6,)}.get(chunk, ()):
            for copy in outputs(case):
                copy.start()
    for copy in outputs(7):
        copy.start()
    acc[...] += acc_t[...].T

    normed_grad = acc[...]
    sums[2:3, :] = column_sum(normed_grad * xhat_a)
    sums[3:4, :] = column_sum(normed_grad)
    attn_wide = normalise_back(normed_grad, gain_a, xhat_a, scale_a)
    resid_grad[...] = attn_wide
    sums[6:7, :] = column_sum(here * attn_wide)
    attn_grad = low(attn_wide)
    grad_t[...] = attn_grad.T
    sums[0:1, :] = column_sum(wide(attn_grad))
    sums[7:8, :] = jnp.zeros((1, D), jnp.float32)
    for r, out in enumerate((g0, g1, g2, g3)):
        out[...] = low(dot(w_out[head_rows(r), :], grad_t[...]).T)
        grad_out[head_rows(r), :] = low(dot_first(heads[r][...], attn_grad))
    for n in range(4):
        head_grad[n] = wide(grad_out[0:16, n * 256 : n * 256 + 256])
    last = []
    for r in range(4):
        rx, rc = r // 2, r % 2
        column = place[3] ^ r
        targets = grads_other if rc else grads_own
        piece = target_piece(targets, 1, place[2], rx)
        last.append((grad_out.at[:, pl.ds(column * 256, 256)], piece.at[0:1024, :]))
    for source, target in last:
        pltpu.make_async_copy(source, target, sem_out.at[1]).start()
    for case in range(5, 8):
        for copy in outputs(case):
            copy.wait()
    for column in range(4):
        for case in range(2, 6):
            for copy in outputs_up(case, column, grads_own, 0):
                copy.wait()
    for source, target in last:
        pltpu.make_async_copy(source, target, sem_out.at[1]).wait()


def layer(place, heads, tokens, cotangent, embed, vectors, bias_up, out_head, pieces):
    grads = struct((2, 2, PIECE, 256))
    block = struct((256, 256))
    return pl.pallas_call(
        layer_kernel,
        out_shape=(
            struct((256, D)), struct((256, D), jnp.float32), block, block, block, block,
            struct((8, D), jnp.float32), struct((4, 1024), jnp.float32),
            struct((4, 16, 256), jnp.float32),
        ) + (grads,) * 6,
        in_specs=[SMEM] + [VMEM] * 10 + [ANY] * 22,
        out_specs=(VMEM,) * 9 + (ANY,) * 6,
        scratch_shapes=[
            pltpu.VMEM((D, D), jnp.bfloat16),
            pltpu.VMEM((16, 1024, 256), jnp.bfloat16),
            pltpu.VMEM((FF, D), jnp.bfloat16),
            pltpu.VMEM((3, 16, 16, 256), jnp.bfloat16),
            pltpu.VMEM((2, 16, D), jnp.bfloat16),
            pltpu.VMEM((256, FF), jnp.bfloat16),
            pltpu.VMEM((FF, 256), jnp.float32),
            pltpu.VMEM((16, 1024, 256), jnp.bfloat16),
            pltpu.VMEM((FF, D), jnp.bfloat16),
            pltpu.VMEM((D, D), jnp.bfloat16),
            pltpu.VMEM((256, D), jnp.float32),
            pltpu.VMEM((D, 256), jnp.float32),
            pltpu.VMEM((D, 256), jnp.bfloat16),
            pltpu.SemaphoreType.DMA((3,)),
            pltpu.SemaphoreType.DMA((2,)),
        ],
        compiler_params=pltpu.CompilerParams(vmem_limit_bytes=60 << 20),
        cost_estimate=pl.CostEstimate(
            flops=15_000_000_000, bytes_accessed=40_000_000, transcendentals=2_097_152
        ),
        name="layer",
    )(place, *heads, tokens, cotangent, embed, vectors, bias_up, out_head, *pieces)


def product(left, right):
    return jnp.dot(left, right, preferred_element_type=jnp.float32)


def product_inner(left, right):
    return lax.dot_general(
        left, right, (((0,), (0,)), ((), ())), preferred_element_type=jnp.float32
    )


def layer_norm(resid, gain, shift):
    average = jnp.mean(resid, axis=-1, keepdims=True)
    centred = resid - average
    variance = jnp.mean(centred * centred, axis=-1, keepdims=True)
    return centred * lax.rsqrt(variance + NORM_EPS) * gain + shift


def unpack_all(flat_params, dp_count, fsdp_count):
    shapes = [(D, D)] * 4 + [(D, FF), (FF, D)] + [(1, D)] * 4 + [(1, FF)] + [(1, D)] * 6
    blocks = (
        flat_params.reshape(dp_count, fsdp_count, -1).transpose(1, 0, 2).reshape(fsdp_count, -1)
    )
    pieces = []
    offset = 0
    for rows, cols in shapes:
        width = rows * (cols // fsdp_count)
        part = blocks[:, offset : offset + width].reshape(fsdp_count, rows, cols // fsdp_count)
        whole = part.transpose(1, 0, 2).reshape(rows, cols)
        pieces.append(whole.reshape(-1) if rows == 1 else whole)
        offset += width
    return pieces


def split_heads(values):
    return values.reshape(values.shape[0], H, DH).transpose(1, 0, 2)


def merge_heads(values):
    return values.transpose(1, 0, 2).reshape(values.shape[1], H * DH)


def head_forward(head_item):
    query_h, key_h, value_h = head_item
    scores = product(query_h, key_h.T) * DH ** (-0.5)
    highest = jnp.max(scores, axis=1, keepdims=True)
    weights = jnp.exp(scores - highest)
    totals = jnp.sum(weights, axis=1, keepdims=True)
    probabilities = weights / totals
    result = product(probabilities.astype(jnp.bfloat16), value_h)
    return (result, (highest + jnp.log(totals))[:, 0])


def head_query_back(head_item):
    query_h, key_h, value_h, grad_h, logsum = head_item
    score_scale = DH ** (-0.5)
    scores = product(query_h, key_h.T) * score_scale
    probabilities = jnp.exp(scores - logsum[:, None])
    prob_grad = product(grad_h, value_h.T)
    inner_sum = jnp.sum(probabilities * prob_grad, axis=1)
    score_grad = (probabilities * (prob_grad - inner_sum[:, None])).astype(jnp.bfloat16)
    query_grad = product(score_grad, key_h) * score_scale
    return (query_grad, inner_sum)


def head_key_back(head_item):
    key_h, value_h, query_all, grad_all, logsum_all, inner_all = head_item
    score_scale = DH ** (-0.5)
    scores_t = product(key_h, query_all.T) * score_scale
    probs_t = jnp.exp(scores_t - logsum_all[None, :])
    prob_grad_t = product(value_h, grad_all.T)
    score_grad_t = (probs_t * (prob_grad_t - inner_all[None, :])).astype(jnp.bfloat16)
    key_grad = product(score_grad_t, query_all) * score_scale
    value_grad = product(probs_t.astype(jnp.bfloat16), grad_all)
    return (key_grad, value_grad)


def body(
    tokens,
    cotangent,
    master,
    first_moment,
    second_moment,
    average,
    timestep,
    block_length,
    block_start,
):
    dp_count = lax.axis_size("dp")
    fsdp_count = lax.axis_size("fsdp")
    master_low = master.astype(jnp.bfloat16)
    flat_params = lax.all_gather(master_low, ("dp", "fsdp"), axis=0, tiled=True)
    (
        w_query,
        w_key,
        w_value,
        w_out,
        w_up,
        w_down,
        b_query,
        b_value,
        b_out,
        b_down,
        b_up,
        gain_attn,
        shift_attn,
        gain_ffn,
        shift_ffn,
        w_time,
        b_time,
    ) = unpack_all(flat_params, dp_count, fsdp_count)
    gain_a = gain_attn.astype(jnp.float32)
    shift_a = shift_attn.astype(jnp.float32)
    gain_f = gain_ffn.astype(jnp.float32)
    shift_f = shift_ffn.astype(jnp.float32)
    row_count = tokens.shape[0]
    position = lax.axis_index("fsdp") * row_count + jnp.arange(row_count, dtype=jnp.int32)
    block_first = block_start[0]
    inside = ((position >= block_first) & (position < block_first + block_length[0])).astype(
        jnp.float32
    )[:, None]
    time_frac = timestep[0].astype(jnp.float32) / 5000.0
    time_embed = time_frac * w_time.astype(jnp.float32) + b_time.astype(jnp.float32)
    stream = tokens.astype(jnp.float32) + inside * time_embed
    stream_low = stream.astype(jnp.bfloat16)
    queries = (product(stream_low, w_query) + b_query.astype(jnp.float32)).astype(jnp.bfloat16)
    keys_local = product(stream_low, w_key).astype(jnp.bfloat16)
    values_local = (product(stream_low, w_value) + b_value.astype(jnp.float32)).astype(jnp.bfloat16)
    keys_all, values_all = (
        lax.all_gather(keys_local, "fsdp", axis=0, tiled=True),
        lax.all_gather(values_local, "fsdp", axis=0, tiled=True),
    )
    query_heads = split_heads(queries)
    key_heads = split_heads(keys_all)
    value_heads = split_heads(values_all)
    head_out, logsum = lax.map(head_forward, (query_heads, key_heads, value_heads))
    heads_low = merge_heads(head_out).astype(jnp.bfloat16)
    resid_attn = stream + product(heads_low, w_out) + b_out.astype(jnp.float32)
    normed = layer_norm(resid_attn, gain_a, shift_a)
    normed_low = normed.astype(jnp.bfloat16)
    pre_act = product(normed_low, w_up) + b_up.astype(jnp.float32)
    hidden = jax.nn.gelu(pre_act, approximate=False).astype(jnp.bfloat16)
    resid_ffn = normed + product(hidden, w_down) + b_down.astype(jnp.float32)
    block_out = layer_norm(resid_ffn, gain_f, shift_f).astype(jnp.bfloat16)
    stream_all, heads_all, normed_all, hidden_all = (
        lax.all_gather(stream_low, "fsdp", axis=0, tiled=True),
        lax.all_gather(heads_low, "fsdp", axis=0, tiled=True),
        lax.all_gather(normed_low, "fsdp", axis=0, tiled=True),
        lax.all_gather(hidden, "fsdp", axis=0, tiled=True),
    )
    back_params = lax.all_gather(master_low, ("dp", "fsdp"), axis=0, tiled=True)
    back_pieces = unpack_all(back_params, dp_count, fsdp_count)
    w_query_back, w_key_back, w_value_back, w_out_back, w_up_back, w_down_back = back_pieces[:6]
    out_grad = cotangent.astype(jnp.float32)
    _, pull_ffn = jax.vjp(layer_norm, resid_ffn, gain_f, shift_f)
    resid_ffn_grad, grad_gain_ffn, grad_shift_ffn = pull_ffn(out_grad)
    ffn_grad = resid_ffn_grad.astype(jnp.bfloat16)
    hidden_grad = product(ffn_grad, w_down_back.T)
    _, pull_gelu = jax.vjp(partial(jax.nn.gelu, approximate=False), pre_act)
    pre_grad = pull_gelu(hidden_grad)[0].astype(jnp.bfloat16)
    normed_grad = resid_ffn_grad + product(pre_grad, w_up_back.T)
    _, pull_attn = jax.vjp(layer_norm, resid_attn, gain_a, shift_a)
    resid_attn_grad, grad_gain_attn, grad_shift_attn = pull_attn(normed_grad)
    attn_grad = resid_attn_grad.astype(jnp.bfloat16)
    heads_grad = product(attn_grad, w_out_back.T).astype(jnp.bfloat16)
    query_parts, inner_sum = lax.map(
        head_query_back, (query_heads, key_heads, value_heads, split_heads(heads_grad), logsum)
    )
    query_grad = merge_heads(query_parts).astype(jnp.bfloat16)
    queries_all, heads_grad_all = (
        lax.all_gather(queries, "fsdp", axis=0, tiled=True),
        lax.all_gather(heads_grad, "fsdp", axis=0, tiled=True),
    )
    logsum_all, inner_all = (
        lax.all_gather(logsum, "fsdp", axis=1, tiled=True),
        lax.all_gather(inner_sum, "fsdp", axis=1, tiled=True),
    )
    key_parts, value_parts = lax.map(
        head_key_back,
        (
            split_heads(keys_local),
            split_heads(values_local),
            split_heads(queries_all),
            split_heads(heads_grad_all),
            logsum_all,
            inner_all,
        ),
    )
    key_grad = merge_heads(key_parts).astype(jnp.bfloat16)
    value_grad = merge_heads(value_parts).astype(jnp.bfloat16)
    stream_grad = (
        resid_attn_grad
        + product(query_grad, w_query_back.T)
        + product(key_grad, w_key_back.T)
        + product(value_grad, w_value_back.T)
    )
    grad_b_time = jnp.sum(inside * stream_grad, axis=0)
    grad_w_time = time_frac * grad_b_time
    query_cols, key_cols, value_cols, attn_cols, ffn_cols, pre_cols = (
        lax.all_to_all(query_grad, "fsdp", split_axis=1, concat_axis=0, tiled=True),
        lax.all_to_all(key_grad, "fsdp", split_axis=1, concat_axis=0, tiled=True),
        lax.all_to_all(value_grad, "fsdp", split_axis=1, concat_axis=0, tiled=True),
        lax.all_to_all(attn_grad, "fsdp", split_axis=1, concat_axis=0, tiled=True),
        lax.all_to_all(ffn_grad, "fsdp", split_axis=1, concat_axis=0, tiled=True),
        lax.all_to_all(pre_grad, "fsdp", split_axis=1, concat_axis=0, tiled=True),
    )
    grad_w_query = product_inner(stream_all, query_cols)
    grad_w_key = product_inner(stream_all, key_cols)
    grad_w_value = product_inner(stream_all, value_cols)
    grad_w_out = product_inner(heads_all, attn_cols)
    grad_w_up = product_inner(normed_all, pre_cols)
    grad_w_down = product_inner(hidden_all, ffn_cols)
    grad_b_query = jnp.sum(query_cols.astype(jnp.float32), axis=0)
    grad_b_value = jnp.sum(value_cols.astype(jnp.float32), axis=0)
    grad_b_out = jnp.sum(attn_cols.astype(jnp.float32), axis=0)
    grad_b_down = jnp.sum(ffn_cols.astype(jnp.float32), axis=0)
    grad_b_up = jnp.sum(pre_cols.astype(jnp.float32), axis=0)
    vector_terms = jnp.stack(
        [grad_gain_attn, grad_shift_attn, grad_gain_ffn, grad_shift_ffn, grad_w_time, grad_b_time]
    )
    vector_part = lax.psum_scatter(vector_terms, "fsdp", scatter_dimension=1, tiled=True)
    vector_block = jnp.concatenate(
        [grad_b_query, grad_b_value, grad_b_out, grad_b_down, grad_b_up, vector_part.reshape(-1)]
    )
    grad_block = jnp.concatenate(
        [
            piece.reshape(-1)
            for piece in (
                grad_w_query,
                grad_w_key,
                grad_w_value,
                grad_w_out,
                grad_w_up,
                grad_w_down,
            )
        ]
        + [vector_block]
    )
    grad_shard = lax.psum_scatter(grad_block, "dp", scatter_dimension=0, tiled=True)
    vector_grad = lax.psum(vector_block, "dp")
    square_sum = lax.psum(jnp.sum(grad_shard * grad_shard), ("dp", "fsdp"))
    grad_norm = jnp.sqrt(square_sum)
    clip_limit = 4.0 * math.sqrt(PARAMS)
    clipped = grad_shard * (clip_limit / jnp.maximum(grad_norm, clip_limit))
    new_first = 0.9 * first_moment + 0.1 * clipped
    new_second = 0.98 * second_moment + 0.02 * clipped * clipped
    first_hat = new_first / (1.0 - 0.9**STEP)
    second_hat = new_second / (1.0 - 0.98**STEP)
    new_master = master - 0.02 * (first_hat / (jnp.sqrt(second_hat) + 1e-06) + 0.01 * master)
    new_average = 0.99 * average + 0.01 * new_master
    return (
        block_out,
        stream_grad,
        grad_norm,
        vector_grad,
        new_first,
        new_second,
        new_master,
        new_average,
    )


AXES = ("dp", "fsdp")


def send(values, route, name="move"):
    pairs = []
    for n in range(32):
        there = route(n // 8, n // 4 % 2, n // 2 % 2, n % 2)
        if there is not None:
            z, y, x, c = there
            pairs.append((n, z * 8 + y * 4 + x * 2 + c))
    with jax.named_scope(name):
        return lax.ppermute(values, AXES, pairs)


def to_core(z, y, x, c):
    return z, y, x, 1 - c


def to_x(z, y, x, c):
    return z, y, 1 - x, c


def to_y(z, y, x, c):
    return z, 1 - y, x, c


def to_near(z, y, x, c):
    return z ^ 1, y, x, c


def to_far(z, y, x, c):
    return z ^ 2, y, x, c


def only(route, planes):
    return lambda z, y, x, c: route(z, y, x, c) if z in planes else None


EVERY = (to_core, to_x, to_y, to_near, to_far)


def total(values, name):
    for route in EVERY:
        values = values + send(values, route, name)
    return values


def to_relative(r):
    return lambda z, y, x, c: (z, y, x ^ (r // 2), c ^ (r % 2))


def exchange(blocks, name):
    return [blocks[0]] + [send(blocks[r], to_relative(r), name) for r in range(1, 4)]


def after(values, *earlier):
    return lax.optimization_barrier((values, *earlier))[0]


PLANES = ((1, 2, 3), (0, 1, 3), (0, 2), (0, 1, 2, 3))


def gather_pieces(own, z, y, tokens, run_attend):
    def across(name, values, n):
        return send(values, only(to_x, PLANES[n]), name)

    outer = (z == 0) | (z == 3)
    first = send(own, lambda z, y, x, c: ((2, 0, 3, 1)[z], y, x, c), "first")
    y0 = send(own, to_y, "y0")
    tokens_x = send(tokens, to_x, "tok_x")
    x0 = across("x0", own, 0)
    tokens_c = send(tokens, to_core, "tok_c")
    second = send(after(jnp.where(outer, own, first), tokens_x), to_near, "second")
    crossed = send(
        after(own, first), lambda z, y, x, c: (3 - z, y, x, c) if z in (1, 2) else None, "crossed"
    )
    y1 = send(after(first, y0), to_y, "y1")
    x1 = across("x1", after(first, x0), 1)
    third = send(after(crossed, second), only(to_near, (1, 2)), "third")
    y2 = send(after(second, y1), to_y, "y2")
    x_a = send(jnp.where(z % 2 == 0, second, y0), to_x, "xa")
    last = jnp.where(outer, third, crossed)
    tokens_xc = send(after(tokens_x, third), to_core, "tok_xc")
    y3 = send(after(last, y2), to_y, "y3")
    y_b = send(after(jnp.where(z == 2, x0, x1), y2), to_y, "yb")
    yx2 = across("yx2", after(y2, last), 2)
    x3 = across("x3", after(last, y2), 3)
    tail_0, tail_1, tail_2 = (
        jnp.where(y == 1, mine[TAIL:], other[TAIL:])
        for mine, other in ((own, y0), (first, y1), (second, y2))
    )
    attended = run_attend(
        after(last, y2), (own, y0, first, y1, second, y2, last, x0, x1),
        (tokens, tokens_c, tokens_x, tokens_xc),
        jnp.where(z == 3, tail_0, jnp.where(z == 1, tail_1, tail_2)),
        jnp.where(z == 0, tail_0, jnp.where(z == 2, tail_1, tail_2)),
    )
    attended = lax.optimization_barrier((*attended, x_a, y3, yx2, x3, y_b))[: len(attended)]
    stack = send(attended[-1], to_core, "stack")
    heads = exchange(attended[5:9], "heads")
    yx3 = across("yx3", after(y3, x3, attended[-1]), 3)
    later = [
        send(after(piece, attended[-1]), only(to_core, planes), name)
        for piece, planes, name in (
            (x_a, (0, 1, 2, 3), "cxa"), (y3, (0, 1, 2, 3), "cy3"), (y_b, (0, 1, 2, 3), "cyb"),
            (yx2, PLANES[2], "cyx2"), (x3, (0, 1, 2, 3), "cx3"), (yx3, (0, 1, 2, 3), "cyx3"),
        )
    ]
    mine = [own, first, second, last, y0, y1, y2, x0, x1, x_a, y3, y_b, yx2, x3, yx3]
    return attended[:5], heads, attended[9], [*mine, stack, *later]


def add(left, right):
    return wide(left) + wide(right)


def block_body(
    tokens,
    cotangent,
    master,
    first_moment,
    second_moment,
    average,
    timestep,
    block_length,
    block_start,
):
    shard = lax.axis_index("dp")
    j = lax.axis_index("fsdp")
    z, y = shard // 2, shard % 2
    place = jnp.stack([shard, z, y, j, block_start[0], block_length[0]]).astype(jnp.int32)
    flat = jnp.pad(master, (0, LANE_ROWS * 128 - SHARD)).reshape(LANE_ROWS, 128)
    vec_rows = jnp.pad(master[SHARD - 3584 :].reshape(14, 256), ((0, 2), (0, 0)))
    head_rows = jnp.pad(master[SHARD - 896 :], (0, 3200)).reshape(16, 256)
    tail = low(jnp.where(shard == 7, vec_rows, head_rows))
    tail_x = send(tail, to_x, "tail_x")
    tail_c = send(jnp.concatenate([tail, tail_x]), to_core, "tail_c")
    own = pack(place, flat, jnp.concatenate([tail, tail_c[:16], tail_x, tail_c[16:]]))
    here = (jnp.arange(4) == j)[:, None, None]
    time_frac = timestep[0].astype(jnp.float32) / 5000.0
    vectors = {}

    def absolute(relative):
        blocks = relative.reshape(4, 16, 256)
        blocks = jnp.where(j % 2 == 1, jnp.concatenate([blocks[1:2], blocks[0:1], blocks[3:4], blocks[2:3]]), blocks)
        return jnp.where(j // 2 == 1, jnp.concatenate([blocks[2:4], blocks[0:2]]), blocks)

    def run_attend(ready, held, all_tokens, vec_tail, head_tail):
        vec = wide(absolute(vec_tail))
        full = vec.transpose(1, 0, 2).reshape(16, D)
        vec_own = wide(vec_tail[:16])
        vectors["embed"] = time_frac * full[12:13] + full[13:14]
        vectors["rows"] = jnp.concatenate([full[2:4], full[8:12], jnp.zeros((2, D), jnp.float32)])
        vectors["up"] = vec[:, 4:8].reshape(16, 256)
        vectors["head"] = absolute(head_tail)
        return attend(after(place, ready), all_tokens, vectors["embed"], vec_own[0:8], held)

    attended, heads, lse, pieces = gather_pieces(own, z, y, tokens, run_attend)
    stream, weight, query, key, value = attended

    (block_out, resid_grad, g0, g1, g2, g3, sums, sums_up, head_grad, *grads) = layer(
        place, heads, tokens, cotangent, vectors["embed"],
        vectors["rows"], vectors["up"], vectors["head"], pieces,
    )
    grads_own, grads_other = grads[:3], grads[3:]

    moved = {k: send(grads_other[k - 1], to_core, f"rc{k}") for k in (2, 1)}
    moved[3] = send(after(grads_other[2], moved[2], moved[1]), to_core, "rc3")

    def over_cores(k, a, b):
        return add(grads_own[k - 1][a, b], moved[k][a, b])

    grad_heads = exchange((g0, g1, g2, g3), "heads_grad")
    starts = {
        name: after(low(over_cores(k, 1, b)), *grad_heads)
        for name, k, b in (("d1", 1, 1), ("d2", 2, 1), ("e1", 1, 0), ("e2", 2, 0))
    }
    d1 = send(starts["d1"], to_y, "d1")
    d2 = send(starts["d2"], to_x, "d2")
    e1 = send(starts["e1"], to_y, "e1")
    e2 = send(starts["e2"], to_x, "e2")

    (q_grad, k_grad, v_grad, kept, sent, sums_qkv) = attend_back(
        after(place, *starts.values()),
        query, key, value, lse, weight, grad_heads,
    )

    q_grad, k_grad, v_grad, kept, sent, sums_qkv, d1, d2 = lax.optimization_barrier(
        (q_grad, k_grad, v_grad, kept, sent, sums_qkv, d1, d2)
    )
    sum_1 = low(over_cores(1, 0, 1) + wide(d1))
    sum_2 = low(over_cores(2, 0, 1) + wide(d2))
    sum_3 = low(over_cores(3, 1, 1))
    sum_1, sum_2, sum_3, e1, e2, sent = lax.optimization_barrier(
        (sum_1, sum_2, sum_3, e1, e2, sent)
    )
    from_core = send(sent, to_core, "in_c")
    f1 = send(sum_1, to_x, "f1")
    f2 = send(sum_2, to_y, "f2")
    q_grad, k_grad, v_grad, sum_3, from_core = lax.optimization_barrier(
        (q_grad, k_grad, v_grad, sum_3, from_core)
    )
    d3 = send(sum_3, to_x, "d3")
    e3 = send(after(low(over_cores(3, 1, 0)), f1), to_x, "e3")

    rows = stream.reshape(1024, D)
    w_grads = [low(product_inner(rows, grad)) for grad in (q_grad, k_grad, v_grad)]
    rest = jnp.zeros((PIECE - 1552, 256), jnp.bfloat16)
    piece_0 = jnp.concatenate([w_grads[0], w_grads[1][:528], rest])
    piece_1 = jnp.concatenate([w_grads[1][512:], w_grads[2], rest, rest[:16]])
    low_row = y == 0
    other_row = jnp.where(low_row, piece_1, piece_0)
    ry0 = send(other_row, to_y, "ry0")
    kept_1, sent_1 = combine(
        after(place, other_row, sum_3), (grads_own[1], moved[2], e2, f2), (grads_own[0], moved[1], e1, f1)
    )
    got_inner = send(sent_1, to_near, "rz_inner1")
    inner_part = low(add(kept_1, got_inner))
    inner_last = send(inner_part, only(to_far, (0, 3)), "rz_inner2")
    f3 = send(low(over_cores(3, 0, 1) + wide(after(d3, ry0, got_inner))), to_y, "f3")
    kept_0, sent_0 = combine(
        place, (jnp.where(low_row, piece_0, piece_1), ry0), (grads_own[2], moved[3], e3, f3)
    )
    outer_part = low(add(kept_0, send(after(sent_0, inner_last), to_near, "rz_outer1")))
    outer_last = send(outer_part, only(to_far, (1, 2)), "rz_outer2")

    in_x = send(after(low(kept[1] + wide(from_core[1])), e3), to_x, "in_x")
    input_grad = (
        resid_grad
        + kept[0]
        + wide(from_core[0])
        + wide(in_x)
    )

    time_grad = sums[6] + sums_qkv[0]
    rows_of = [sums[0], sums[1]]
    vec_grad = jnp.concatenate(
        [
            jnp.where(here, sums_qkv[1:3, :256][None], 0.0),
            sums[0:2].reshape(2, 4, 256).transpose(1, 0, 2),
            sums_up.reshape(4, 4, 256),
            sums[2:6].reshape(4, 4, 256).transpose(1, 0, 2),
            (time_frac * time_grad).reshape(4, 1, 256),
            time_grad.reshape(4, 1, 256),
            jnp.zeros((4, 2, 256), jnp.float32),
            head_grad,
        ],
        axis=1,
    )
    vec_grad = vec_grad.reshape(2, 2, 32, 256)
    core_bit, x_bit = j % 2, j // 2
    kept_c = jnp.where(core_bit == 1, vec_grad[:, 1], vec_grad[:, 0])
    sent_c = jnp.where(core_bit == 1, vec_grad[:, 0], vec_grad[:, 1])
    by_x = kept_c + send(sent_c, to_core, "vec_c")
    kept_x = jnp.where(x_bit == 1, by_x[1], by_x[0])
    mine = kept_x + send(jnp.where(x_bit == 1, by_x[0], by_x[1]), to_x, "vec_x")

    grad_flat, square = unpack(after(place, input_grad), inner_part, inner_last, outer_part, outer_last)
    mine = jnp.concatenate([mine, square.reshape(4, 256), jnp.zeros((4, 256), jnp.float32)])
    for route in (to_y, to_near, to_far):
        mine = mine + send(mine, route, "norm")
    vec_sum, head_sum = mine[:14].reshape(-1), mine[16:20].reshape(-1)[:896]
    vector_grad = vec_sum
    square_sum = (jnp.sum(mine[32:36]) + jnp.sum(vec_sum * vec_sum) + jnp.sum(head_sum * head_sum))
    square_sum = jnp.broadcast_to(square_sum, (8, 128))
    for route in (to_x, to_core):
        square_sum = square_sum + send(square_sum, route, "norm")
    grad_norm = jnp.sqrt(square_sum[0, 0])
    grad_flat = grad_flat.reshape(-1)
    edge = grad_flat[SHARD - 3584 : SHARD]
    edge = jnp.where(
        shard == 7,
        vec_sum,
        jnp.where(shard == 1, jnp.concatenate([edge[: 3584 - 896], head_sum]), edge),
    )
    grad_shard = lax.dynamic_update_slice(grad_flat, edge, (SHARD - 3584,))[:SHARD]
    clip_limit = 4.0 * math.sqrt(PARAMS)
    clipped = grad_shard * (clip_limit / jnp.maximum(grad_norm, clip_limit))
    new_first = 0.9 * first_moment + 0.1 * clipped
    new_second = 0.98 * second_moment + 0.02 * clipped * clipped
    first_hat = new_first / (1.0 - 0.9**STEP)
    second_hat = new_second / (1.0 - 0.98**STEP)
    new_master = master - 0.02 * (first_hat / (jnp.sqrt(second_hat) + 1e-06) + 0.01 * master)
    new_average = 0.99 * average + 0.01 * new_master
    return (
        block_out,
        input_grad,
        grad_norm,
        vector_grad,
        new_first,
        new_second,
        new_master,
        new_average,
    )


def solution(mesh):
    return jax.shard_map(
        block_body if mesh.shape["dp"] == 8 and mesh.shape["fsdp"] == 4 else body,
        mesh=mesh,
        in_specs=(
            P(("dp", "fsdp"), None),
            P(("dp", "fsdp"), None),
            P(("dp", "fsdp")),
            P(("dp", "fsdp")),
            P(("dp", "fsdp")),
            P(("dp", "fsdp")),
            P("dp"),
            P("dp"),
            P("dp"),
        ),
        out_specs=(
            P(("dp", "fsdp"), None),
            P(("dp", "fsdp"), None),
            P(),
            P("fsdp"),
            P(("dp", "fsdp")),
            P(("dp", "fsdp")),
            P(("dp", "fsdp")),
            P(("dp", "fsdp")),
        ),
        check_vma=False,
    )
```

```python
from functools import partial
import math

import jax
import jax.numpy as jnp
from jax import lax
from jax.experimental import pallas as pl
from jax.experimental.pallas import tpu as pltpu
from jax.sharding import PartitionSpec as P

D = 1024
H = 16
DH = 64
FF = 4096
STEP = 10
PARAMS = 12597248
NORM_EPS = 1e-05

SHARD = PARAMS // 32
PIECE = 1600
LANE_ROWS = 3080
PAD = 128
TAIL = 1536
REGIONS = (
    ("q", 0, 1024, 256),
    ("k", 262144, 1024, 256),
    ("v", 524288, 1024, 256),
    ("o", 786432, 1024, 256),
    ("up", 1048576, 1024, 1024),
    ("down", 2097152, 4096, 256),
    ("vec", 3145728, 16, 256),
)


def segments(shard):
    low, high = shard * SHARD, (shard + 1) * SHARD
    found, offset = [], 0
    for name, start, rows, width in REGIONS:
        size = 3584 if name == "vec" else rows * width
        first, last = max(low, start), min(high, start + size)
        if first >= last:
            continue
        row_a = (first - start) // width // 16 * 16
        row_b = min(rows, -(-(-(-(last - start) // width)) // 16) * 16)
        found.append((name, row_a, row_b, offset, width // 128, start // 128))
        offset += (row_b - row_a) * (width // 256)
    return found


def lane_start(shard):
    return shard * SHARD // 128


SEGMENTS = [segments(shard) for shard in range(8)]
SLOT = ((0, 1, 3, 2), (2, 0, 3, 1), (1, 3, 0, 2), (2, 3, 1, 0))


def buffers(z):
    x_a, y_b = 9, 11
    over_x = [7, 8, x_a, 13]
    both = [y_b if z == 2 else x_a, y_b, 12, 14]
    return [0, 1, 2, 3, 4, 5, 6, 10, *over_x, *both]


BUFFER = [buffers(z) for z in range(4)]


def dot(left, right):
    return jnp.dot(left, right, preferred_element_type=jnp.float32)


def dot_last(left, right):
    return lax.dot_general(
        left, right, (((1,), (1,)), ((), ())), preferred_element_type=jnp.float32
    )


def dot_first(left, right):
    return lax.dot_general(
        left, right, (((0,), (0,)), ((), ())), preferred_element_type=jnp.float32
    )


def low(values):
    return values.astype(jnp.bfloat16)


def wide(values):
    return values.astype(jnp.float32)


VMEM = pl.BlockSpec(memory_space=pltpu.VMEM)
SMEM = pl.BlockSpec(memory_space=pltpu.SMEM)
ANY = pl.BlockSpec(memory_space=pl.ANY)


def struct(shape, kind=jnp.bfloat16):
    return jax.ShapeDtypeStruct(shape, kind)


def chunks(rows, most=128):
    return [(a, min(most, rows - a)) for a in range(0, rows, most)]


def pack_kernel(place, flat, tails, piece, rolled, rows):
    shard = place[0]
    rows[0:PAD, :] = jnp.zeros((PAD, 128), jnp.float32)
    rows[PAD + LANE_ROWS : PAD + LANE_ROWS + PAD, :] = jnp.zeros((PAD, 128), jnp.float32)
    rolled[0:8, :] = jnp.zeros((8, 128), jnp.float32)

    @pl.when(shard % 2 == 0)
    def _():
        for a, n in chunks(LANE_ROWS):
            rows[PAD + a : PAD + a + n, :] = flat[a : a + n, :]

    @pl.when(shard % 2 == 1)
    def _():
        for a, n in chunks(LANE_ROWS):
            rolled[8 + a : 8 + a + n, :] = pltpu.roll(flat[a : a + n, :], 64, 1)
        for a, n in chunks(LANE_ROWS):
            lane = lax.broadcasted_iota(jnp.int32, (n, 128), 1)
            rows[PAD + a : PAD + a + n, :] = jnp.where(
                lane < 64, rolled[7 + a : 7 + a + n, :], rolled[8 + a : 8 + a + n, :]
            )

    for case in range(8):

        @pl.when(shard == case)
        def _(case=case):
            for _, row_a, row_b, offset, step, first in SEGMENTS[case]:
                if offset == TAIL:
                    piece[TAIL:PIECE, :] = tails[...]
                    continue
                count = row_b - row_a
                base = PAD + first + step * row_a - lane_start(case)
                for t in range(step):
                    out = offset + t // 2 * count
                    lanes = slice(t % 2 * 128, t % 2 * 128 + 128)
                    for a, n in chunks(count):
                        piece[out + a : out + a + n, lanes] = low(
                            rows[pl.ds(base + t + step * a, n, stride=step), :]
                        )


def pack(place, flat, tails):
    return pl.pallas_call(
        pack_kernel,
        out_shape=struct((PIECE, 256)),
        in_specs=[SMEM, VMEM, VMEM],
        out_specs=VMEM,
        scratch_shapes=[
            pltpu.VMEM((8 + LANE_ROWS, 128), jnp.float32),
            pltpu.VMEM((PAD + LANE_ROWS + PAD, 128), jnp.float32),
        ],
        compiler_params=pltpu.CompilerParams(vmem_limit_bytes=24 << 20),
        name="pack",
    )(place, flat, tails)


def unpack_kernel(place, inner, inner_last, outer, outer_last, flat, square, rows, left, right, sem):
    shard = place[0]
    is_inner = (place[1] == 1) | (place[1] == 2)

    def fetch(first, second):
        copies = [
            pltpu.make_async_copy(first, left, sem.at[0]),
            pltpu.make_async_copy(second, right, sem.at[1]),
        ]
        for copy in copies:
            copy.start()
        for copy in copies:
            copy.wait()

    @pl.when(is_inner)
    def _():
        fetch(inner, inner_last)

    @pl.when(jnp.logical_not(is_inner))
    def _():
        fetch(outer, outer_last)

    for case in range(8):

        @pl.when(shard == case)
        def _(case=case):
            for _, row_a, row_b, offset, step, first in SEGMENTS[case]:
                count = row_b - row_a
                base = PAD + first + step * row_a - lane_start(case)
                for t in range(step):
                    source = offset + t // 2 * count
                    lanes = slice(t % 2 * 128, t % 2 * 128 + 128)
                    for a, n in chunks(count):
                        spot = slice(source + a, source + a + n)
                        value = wide(left[spot, lanes]) + wide(right[spot, lanes])
                        if offset == TAIL:
                            value = jnp.zeros((n, 128), jnp.float32)
                        rows[pl.ds(base + t + step * a, n, stride=step), :] = value

    square[...] = jnp.zeros_like(square)
    for odd in range(2):

        @pl.when(shard % 2 == odd)
        def _(odd=odd):
            total = jnp.zeros((8, 128), jnp.float32)
            for a, n in chunks(LANE_ROWS):
                value = rows[PAD + a : PAD + a + n, :]
                lane = lax.broadcasted_iota(jnp.int32, (n, 128), 1)
                if odd:
                    after = rows[PAD + a + 1 : PAD + a + 1 + n, :]
                    value = jnp.where(
                        lane < 64, pltpu.roll(value, 64, 1), pltpu.roll(after, 64, 1)
                    )
                if (a + n) * 128 > SHARD:
                    row = lax.broadcasted_iota(jnp.int32, (n, 128), 0) + a
                    value = jnp.where(row * 128 + lane < SHARD, value, 0.0)
                flat[a : a + n, :] = value
                total += jnp.sum((value * value).reshape(n // 8, 8, 128), axis=0)
            square[:, 0:128] = total


def unpack(place, *pieces):
    return pl.pallas_call(
        unpack_kernel,
        out_shape=(struct((LANE_ROWS, 128), jnp.float32), struct((8, 256), jnp.float32)),
        in_specs=[SMEM] + [ANY] * 4,
        out_specs=(VMEM, VMEM),
        scratch_shapes=[
            pltpu.VMEM((PAD + LANE_ROWS + PAD, 128), jnp.float32),
            pltpu.VMEM((PIECE, 256), jnp.bfloat16),
            pltpu.VMEM((PIECE, 256), jnp.bfloat16),
            pltpu.SemaphoreType.DMA((2,)),
        ],
        compiler_params=pltpu.CompilerParams(vmem_limit_bytes=60 << 20),
        name="unpack",
    )(place, *pieces)


def combine_kernel(split, place, *refs):
    kept, sent = refs[-2:]
    first = sum(wide(ref[...]) for ref in refs[:split])
    second = sum(wide(ref[...]) for ref in refs[split:-2])
    even = place[1] % 2 == 0
    kept[...] = low(jnp.where(even, first, second))
    sent[...] = low(jnp.where(even, second, first))


def combine(place, first, second):
    blocks = 2
    size = PIECE // blocks

    def spec(piece):
        if piece.ndim == 4:
            return pl.BlockSpec((None, None, size, 256), lambda n: (0, 0, n, 0))
        return pl.BlockSpec((size, 256), lambda n: (n, 0))

    pieces = [*first, *second]
    return pl.pallas_call(
        partial(combine_kernel, len(first)),
        grid=(blocks,),
        out_shape=(struct((PIECE, 256)), struct((PIECE, 256))),
        in_specs=[SMEM] + [spec(piece) for piece in pieces],
        out_specs=(pl.BlockSpec((size, 256), lambda n: (n, 0)),) * 2,
        compiler_params=pltpu.CompilerParams(vmem_limit_bytes=60 << 20),
        name="combine",
    )(place, *pieces)


def column_sum(values):
    return jnp.sum(values, axis=0, keepdims=True)


def inside_column(place, relative):
    rows = lax.broadcasted_iota(jnp.int32, (256, 1), 0)
    position = rows + (place[3] ^ relative) * 256
    return ((position >= place[4]) & (position < place[4] + place[5])).astype(jnp.float32)


def attend_kernel(
    place, embed, bias, t0, t1, t2, t3, p0, p1, p2, p3, p4, p5, p6, p7, p8,
    stream_out, weight_out, q_out, k_out, v_out, h0, h1, h2, h3, lse_out, stack,
    tokens, staged, q_heads, k_t, v_heads, o_heads, edge, sem, sem_tokens, sem_in, sem_out,
):
    fetches = [
        pltpu.make_async_copy(ref, tokens.at[r], sem_tokens.at[r])
        for r, ref in enumerate((t0, t1, t2, t3))
    ]
    for copy in fetches:
        copy.start()

    def copies(first, second):
        return [
            pltpu.make_async_copy(first.at[0:1024, :], weight_out.at[0], sem.at[0]),
            pltpu.make_async_copy(first.at[1024:1552, :], weight_out.at[1, 0:528, :], sem.at[1]),
            pltpu.make_async_copy(second.at[16:512, :], weight_out.at[1, 528:1024, :], sem.at[2]),
            pltpu.make_async_copy(second.at[0:16, :], edge, sem.at[3]),
            pltpu.make_async_copy(second.at[512:1536, :], weight_out.at[2], sem.at[4]),
        ]

    held = ((p0, p1), (p2, p3), (p4, p5))
    for z in range(4):
        for y in range(2):
            own, other = held[SLOT[z][0]]
            pair = (other, own) if y else (own, other)

            @pl.when((place[1] == z) & (place[2] == y))
            def _(pair=pair):
                for copy in copies(*pair):
                    copy.start()

    held_in = [
        pltpu.make_async_copy(ref, staged.at[n], sem_in.at[n])
        for n, ref in enumerate((p0, p2, p4, p6, p1, p3, p5, p7, p8))
    ]
    held_out = [pltpu.make_async_copy(staged.at[n], stack.at[n], sem_out.at[n]) for n in range(9)]
    for copy in held_in:
        copy.start()
    for r, copy in enumerate(fetches):
        copy.wait()
        stream_out[r] = low(wide(tokens[r]) + inside_column(place, r) * embed[...])
    lanes = lax.broadcasted_iota(jnp.int32, (1024, 128), 1)
    v_heads[...] = jnp.broadcast_to((lanes >= 64).astype(jnp.bfloat16), (4, 1024, 128))
    for copy in copies(p0, p1):
        copy.wait()
    weight_out[1, 512:528, :] = weight_out[1, 512:528, :] + edge[...]
    for r in range(4):
        rows = slice(r * 256, r * 256 + 256)
        stream = stream_out[r]
        query = low(dot(stream, weight_out[0]) + bias[0:1, :])
        key = low(dot(stream, weight_out[1]))
        value = low(dot(stream, weight_out[2]) + bias[1:2, :])
        q_out[rows, :] = query
        k_out[rows, :] = key
        v_out[rows, :] = value
        for h in range(4):
            cols = slice(h * 64, h * 64 + 64)
            q_heads[h, rows, :] = query[:, cols] * 0.125
            v_heads[h, rows, 0:64] = value[:, cols]
        k_t[:, rows] = key.T
    lse_out[...] = jnp.zeros_like(lse_out)
    for before, copy in zip(held_in, held_out):
        before.wait()
        copy.start()

    def head_step(h, _):
        key_t = k_t[pl.ds(pl.multiple_of(h * 64, 64), 64), :]
        for r in range(4):
            rows = slice(r * 256, r * 256 + 256)
            scores = dot(q_heads[h, rows, :], key_t)
            highest = jnp.max(scores, axis=1, keepdims=True)
            weights = low(jnp.exp(scores - highest))
            result = dot(weights, v_heads[h])
            total = result[:, 64:65]
            o_heads[h, rows, :] = low(result[:, 0:64] / total)
            lane = lax.broadcasted_iota(jnp.int32, (256, 128), 1)
            lse_out[rows, :] = jnp.where(lane == h, highest + jnp.log(total), lse_out[rows, :])
        return 0

    lax.fori_loop(0, 4, head_step, 0, unroll=4)
    for r, out in enumerate((h0, h1, h2, h3)):
        for h in range(4):
            out[:, h * 64 : h * 64 + 64] = o_heads[h, r * 256 : r * 256 + 256, :]
    for copy in held_out:
        copy.wait()


def attend(place, tokens, embed, bias, pieces):
    square = struct((1024, 256))
    block = struct((256, 256))
    return pl.pallas_call(
        attend_kernel,
        out_shape=(
            struct((4, 256, 1024)), struct((3, 1024, 256)), square, square, square,
            block, block, block, block, struct((1024, 128), jnp.float32), struct((9, PIECE, 256)),
        ),
        in_specs=[SMEM] + [VMEM] * 2 + [ANY] * 13,
        out_specs=(VMEM,) * 10 + (ANY,),
        scratch_shapes=[
            pltpu.VMEM((4, 256, 1024), jnp.bfloat16),
            pltpu.VMEM((9, PIECE, 256), jnp.bfloat16),
            pltpu.VMEM((4, 1024, 64), jnp.bfloat16),
            pltpu.VMEM((256, 1024), jnp.bfloat16),
            pltpu.VMEM((4, 1024, 128), jnp.bfloat16),
            pltpu.VMEM((4, 1024, 64), jnp.bfloat16),
            pltpu.VMEM((16, 256), jnp.bfloat16),
            pltpu.SemaphoreType.DMA((5,)),
            pltpu.SemaphoreType.DMA((4,)),
            pltpu.SemaphoreType.DMA((9,)),
            pltpu.SemaphoreType.DMA((9,)),
        ],
        compiler_params=pltpu.CompilerParams(vmem_limit_bytes=48 << 20),
        cost_estimate=pl.CostEstimate(
            flops=16_000_000_000, bytes_accessed=24_000_000, transcendentals=4_194_304
        ),
        name="attend",
    )(place, embed, bias, *tokens, *pieces)


def attend_back_kernel(
    place, q_in, k_in, v_in, lse, weight, g0, g1, g2, g3,
    q_grad, k_grad, v_grad, kept, sent, sums,
    q_heads, k_heads, g_heads, q_t, k_t, v_t, g_t, dq_heads, dk_t, dv_t,
):
    for r, grad in enumerate((g0, g1, g2, g3)):
        rows = slice(r * 256, r * 256 + 256)
        g_t[:, rows] = grad[...].T
        for h in range(4):
            cols = slice(h * 64, h * 64 + 64)
            q_heads[h, rows, :] = q_in[rows, cols] * 0.125
            k_heads[h, rows, :] = k_in[rows, cols]
            g_heads[h, rows, :] = grad[:, cols]
    q_t[...] = (q_in[...] * 0.125).T
    k_t[...] = k_in[...].T
    v_t[...] = v_in[...].T

    def head_step(h, _):
        mine = pl.ds(pl.multiple_of(h * 64, 64), 64)
        key_t, value_t, key = k_t[mine, :], v_t[mine, :], k_heads[h]
        key_sum = jnp.zeros((64, 1024), jnp.float32)
        value_sum = jnp.zeros((64, 1024), jnp.float32)
        for r in range(4):
            rows = slice(r * 256, r * 256 + 256)
            scores = dot(q_heads[h, rows, :], key_t)
            lane = lax.broadcasted_iota(jnp.int32, (256, 128), 1)
            logsum = jnp.sum(jnp.where(lane == h, lse[rows, :], 0.0), axis=1, keepdims=True)
            probs = jnp.exp(scores - logsum)
            weighted = probs * dot(g_heads[h, rows, :], value_t)
            inner = jnp.sum(weighted, axis=1, keepdims=True)
            score_grad = low(weighted - probs * inner)
            dq_heads[h, rows, :] = low(dot(score_grad, key) * 0.125)
            key_sum += dot(q_t[mine, rows], score_grad)
            value_sum += dot(g_t[mine, rows], low(probs))
        dk_t[mine, :] = low(key_sum)
        dv_t[mine, :] = low(value_sum)
        return 0

    lax.fori_loop(0, 4, head_step, 0, unroll=4)
    for h in range(4):
        q_grad[:, h * 64 : h * 64 + 64] = dq_heads[h]
    k_grad[...] = dk_t[...].T
    v_grad[...] = dv_t[...].T
    sums[...] = jnp.zeros_like(sums)
    sums[1:2, 0:256] = column_sum(wide(q_grad[...]))
    sums[2:3, 0:256] = column_sum(wide(v_grad[...]))
    for r in range(4):
        rows = slice(r * 256, r * 256 + 256)
        part = (
            dot_last(q_grad[rows, :], weight[0])
            + dot_last(k_grad[rows, :], weight[1])
            + dot_last(v_grad[rows, :], weight[2])
        )
        sums[0:1, :] += column_sum(inside_column(place, r) * part)
        if r % 2:
            sent[r // 2] = low(part)
        else:
            kept[r // 2] = part


def attend_back(place, query, key, value, lse, weight, grads):
    square = struct((1024, 256))
    return pl.pallas_call(
        attend_back_kernel,
        out_shape=(
            square, square, square, struct((2, 256, D), jnp.float32), struct((2, 256, D)),
            struct((8, D), jnp.float32),
        ),
        in_specs=[SMEM] + [VMEM] * 9,
        out_specs=(VMEM,) * 6,
        scratch_shapes=[pltpu.VMEM((4, 1024, 64), jnp.bfloat16)] * 3
        + [pltpu.VMEM((256, 1024), jnp.bfloat16)] * 4
        + [pltpu.VMEM((4, 1024, 64), jnp.bfloat16)]
        + [pltpu.VMEM((256, 1024), jnp.bfloat16)] * 2,
        compiler_params=pltpu.CompilerParams(vmem_limit_bytes=40 << 20),
        cost_estimate=pl.CostEstimate(
            flops=20_000_000_000, bytes_accessed=12_000_000, transcendentals=4_194_304
        ),
        name="attend_back",
    )(place, query, key, value, lse, weight, *grads)


def row_mean(values):
    return jnp.sum(values, axis=1, keepdims=True) * (1.0 / D)


def normalise(resid):
    centred = resid - row_mean(resid)
    scale = lax.rsqrt(row_mean(centred * centred) + NORM_EPS)
    return centred * scale, scale


def normalise_back(grad, gain, xhat, scale):
    scaled = grad * gain
    return (scaled - row_mean(scaled) - xhat * row_mean(scaled * xhat)) * scale


def target_piece(targets, k, ry, rx):
    return targets[k - 1].at[ry, rx] if k == 1 else targets[k - 1].at[rx, ry]


def layer_kernel(
    place, h0, h1, h2, h3, tokens, cotangent, embed, vectors, bias_up, out_head, *refs
):
    stack = refs[15]
    pieces = (refs[:15], [stack.at[n] for n in range(9)] + list(refs[16:22]))
    refs = refs[22:]
    (block_out, resid_grad, g0, g1, g2, g3, sums, sums_up, head_grad) = refs[:9]
    grads_own, grads_other = refs[9:12], refs[12:15]
    (w_out, w_up, w_down, edge_up, edge_down, hidden, slope, grad_up, grad_down,
     grad_out, acc, acc_t, grad_t, sem, sem_out) = refs[15:]

    def fetch(z, y):
        made = {"out": [], "up": [], "down": []}
        for k in range(1, 4):
            for ry in range(2):
                case = 2 * k + (y ^ ry)
                for r in range(4):
                    rx, rc = r // 2, r % 2
                    source = pieces[rc][BUFFER[z][rx * 8 + ry * 4 + SLOT[z][k]]]
                    column = place[3] ^ r
                    for name, row_a, row_b, offset, step, _ in SEGMENTS[case]:
                        count = row_b - row_a
                        if name == "o":
                            made["out"].append(
                                (source.at[offset : offset + count, :], w_out.at[:, pl.ds(column * 256, 256)])
                            )
                        elif name == "up":
                            block = source.at[offset : offset + 4 * count, :].reshape(4, count, 256)
                            target = w_up.at[pl.ds(column * 4, 4)]
                            skip = 0
                            if row_a:
                                skip = 16
                                made["up"].append(
                                    (block.at[:, 0:16, :], edge_up.at[case - 3, pl.ds(column * 4, 4)])
                                )
                            made["up"].append(
                                (block.at[:, skip:count, :], target.at[:, row_a + skip : row_b, :])
                            )
                        elif name == "down":
                            skip = 0
                            if row_a:
                                skip = 16
                                made["down"].append(
                                    (source.at[offset : offset + 16, :], edge_down.at[case - 6, :, pl.ds(column * 256, 256)])
                                )
                            made["down"].append(
                                (source.at[offset + skip : offset + count, :],
                                 w_down.at[row_a + skip : row_b, pl.ds(column * 256, 256)])
                            )
        return made

    order = ("out", "up", "down")
    for z in range(4):
        for y in range(2):

            @pl.when((place[1] == z) & (place[2] == y))
            def _(z=z, y=y):
                made = fetch(z, y)
                for n, name in enumerate(order):
                    for source, target in made[name]:
                        pltpu.make_async_copy(source, target, sem.at[n]).start()

    def arrived(refs, n):
        for ref in refs:
            pltpu.make_async_copy(ref, ref, sem.at[n]).wait()

    here = inside_column(place, 0)
    stream = wide(tokens[...]) + here * embed[...]
    arrived([w_out], 0)
    for n in range(4):
        cols = slice(n * 256, n * 256 + 256)
        w_out[0:16, cols] = w_out[0:16, cols] + out_head[n]
    heads = (h0, h1, h2, h3)

    def head_rows(r):
        return pl.ds(pl.multiple_of((place[3] ^ r) * 256, 256), 256)

    acc[...] = sum(dot(heads[r][...], w_out[head_rows(r), :]) for r in range(4))
    bias_out, bias_down, gain_a, shift_a, gain_f, shift_f = (vectors[n : n + 1, :] for n in range(6))
    xhat_a, scale_a = normalise(stream + acc[...] + bias_out)
    normed = xhat_a * gain_a + shift_a
    normed_low = low(normed)

    arrived([w_up] + [edge_up], 1)
    for n, row in enumerate((128, 512, 896)):
        w_up[:, row : row + 16, :] = w_up[:, row : row + 16, :] + edge_up[n]

    def up(g, _):
        pre = dot(normed_low, w_up[g]) + bias_up[pl.ds(g, 1), :]
        inner = 0.5 * (1.0 + lax.erf(pre * (1.0 / math.sqrt(2.0))))
        hidden[:, pl.ds(pl.multiple_of(g * 256, 256), 256)] = low(pre * inner)
        bend = inner + pre * (jnp.exp(-0.5 * pre * pre) * (1.0 / math.sqrt(2.0 * math.pi)))
        slope[pl.ds(pl.multiple_of(g * 256, 256), 256), :] = bend.T
        return 0

    lax.fori_loop(0, 16, up, 0, unroll=8)
    arrived([w_down] + [edge_down], 2)
    for n, row in enumerate((1024, 2560)):
        w_down[row : row + 16, :] = w_down[row : row + 16, :] + edge_down[n]
    acc[...] = normed + bias_down + dot(hidden[...], w_down[...])
    xhat_f, scale_f = normalise(acc[...])
    block_out[...] = low(xhat_f * gain_f + shift_f)

    out_grad = wide(cotangent[...])
    sums[4:5, :] = column_sum(out_grad * xhat_f)
    sums[5:6, :] = column_sum(out_grad)
    acc[...] = normalise_back(out_grad, gain_f, xhat_f, scale_f)
    ffn_grad = low(acc[...])
    sums[1:2, :] = column_sum(wide(ffn_grad))
    grad_t[...] = ffn_grad.T
    normed_t = normed_low.T

    def routes(case, name):
        return [
            (row_a, row_b, offset, row_b - row_a)
            for seg, row_a, row_b, offset, _, _ in SEGMENTS[case]
            if seg == name
        ]

    def outputs_up(case, column, targets, rx):
        piece = target_piece(targets, case // 2, place[2] ^ (case % 2), rx)
        return [
            pltpu.make_async_copy(
                grad_up.at[column * 4 : column * 4 + 4, row_a:row_b, :],
                piece.at[offset : offset + 4 * count, :].reshape(4, count, 256),
                sem_out.at[0],
            )
            for row_a, row_b, offset, count in routes(case, "up")
        ]

    def outputs(case):
        made = []
        for r in range(4):
            rx, rc = r // 2, r % 2
            column = place[3] ^ r
            targets = grads_other if rc else grads_own
            piece = target_piece(targets, case // 2, place[2] ^ (case % 2), rx)
            for row_a, row_b, offset, count in routes(case, "down"):
                source = grad_down.at[row_a:row_b, pl.ds(column * 256, 256)]
                target = piece.at[offset : offset + count, :]
                made.append(pltpu.make_async_copy(source, target, sem_out.at[0]))
        return made

    acc_t[...] = jnp.zeros_like(acc_t)

    for chunk in range(4):
        rows = slice(chunk * 1024, chunk * 1024 + 1024)
        pre_grad_t = low(dot(w_down[rows, :], grad_t[...]) * slope[rows, :])
        pre_grad = pre_grad_t.T
        sums_up[chunk : chunk + 1, :] = column_sum(wide(pre_grad))
        for n in range(4):
            g = chunk * 4 + n
            acc_t[...] += dot(w_up[g], pre_grad_t[n * 256 : n * 256 + 256, :])
            grad_up[g] = low(dot(normed_t, pre_grad[:, n * 256 : n * 256 + 256]))
        grad_down[rows, :] = low(dot_first(hidden[:, rows], ffn_grad))
        relative = place[3] ^ chunk
        for side, targets in enumerate((grads_own, grads_other)):

            @pl.when(relative % 2 == side)
            def _(chunk=chunk, targets=targets, relative=relative):
                for case in range(2, 6):
                    for copy in outputs_up(case, chunk, targets, relative // 2):
                        copy.start()

        for case in {1: (5,), 2: (6,)}.get(chunk, ()):
            for copy in outputs(case):
                copy.start()
    for copy in outputs(7):
        copy.start()
    acc[...] += acc_t[...].T

    normed_grad = acc[...]
    sums[2:3, :] = column_sum(normed_grad * xhat_a)
    sums[3:4, :] = column_sum(normed_grad)
    attn_wide = normalise_back(normed_grad, gain_a, xhat_a, scale_a)
    resid_grad[...] = attn_wide
    sums[6:7, :] = column_sum(here * attn_wide)
    attn_grad = low(attn_wide)
    grad_t[...] = attn_grad.T
    sums[0:1, :] = column_sum(wide(attn_grad))
    sums[7:8, :] = jnp.zeros((1, D), jnp.float32)
    for r, out in enumerate((g0, g1, g2, g3)):
        out[...] = low(dot(w_out[head_rows(r), :], grad_t[...]).T)
        grad_out[head_rows(r), :] = low(dot_first(heads[r][...], attn_grad))
    for n in range(4):
        head_grad[n] = wide(grad_out[0:16, n * 256 : n * 256 + 256])
    last = []
    for r in range(4):
        rx, rc = r // 2, r % 2
        column = place[3] ^ r
        targets = grads_other if rc else grads_own
        piece = target_piece(targets, 1, place[2], rx)
        last.append((grad_out.at[:, pl.ds(column * 256, 256)], piece.at[0:1024, :]))
    for source, target in last:
        pltpu.make_async_copy(source, target, sem_out.at[1]).start()
    for case in range(5, 8):
        for copy in outputs(case):
            copy.wait()
    for column in range(4):
        for case in range(2, 6):
            for copy in outputs_up(case, column, grads_own, 0):
                copy.wait()
    for source, target in last:
        pltpu.make_async_copy(source, target, sem_out.at[1]).wait()


def layer(place, heads, tokens, cotangent, embed, vectors, bias_up, out_head, pieces):
    grads = struct((2, 2, PIECE, 256))
    block = struct((256, 256))
    return pl.pallas_call(
        layer_kernel,
        out_shape=(
            struct((256, D)), struct((256, D), jnp.float32), block, block, block, block,
            struct((8, D), jnp.float32), struct((4, 1024), jnp.float32),
            struct((4, 16, 256), jnp.float32),
        ) + (grads,) * 6,
        in_specs=[SMEM] + [VMEM] * 10 + [ANY] * 22,
        out_specs=(VMEM,) * 9 + (ANY,) * 6,
        scratch_shapes=[
            pltpu.VMEM((D, D), jnp.bfloat16),
            pltpu.VMEM((16, 1024, 256), jnp.bfloat16),
            pltpu.VMEM((FF, D), jnp.bfloat16),
            pltpu.VMEM((3, 16, 16, 256), jnp.bfloat16),
            pltpu.VMEM((2, 16, D), jnp.bfloat16),
            pltpu.VMEM((256, FF), jnp.bfloat16),
            pltpu.VMEM((FF, 256), jnp.float32),
            pltpu.VMEM((16, 1024, 256), jnp.bfloat16),
            pltpu.VMEM((FF, D), jnp.bfloat16),
            pltpu.VMEM((D, D), jnp.bfloat16),
            pltpu.VMEM((256, D), jnp.float32),
            pltpu.VMEM((D, 256), jnp.float32),
            pltpu.VMEM((D, 256), jnp.bfloat16),
            pltpu.SemaphoreType.DMA((3,)),
            pltpu.SemaphoreType.DMA((2,)),
        ],
        compiler_params=pltpu.CompilerParams(vmem_limit_bytes=60 << 20),
        cost_estimate=pl.CostEstimate(
            flops=15_000_000_000, bytes_accessed=40_000_000, transcendentals=2_097_152
        ),
        name="layer",
    )(place, *heads, tokens, cotangent, embed, vectors, bias_up, out_head, *pieces)


def product(left, right):
    return jnp.dot(left, right, preferred_element_type=jnp.float32)


def product_inner(left, right):
    return lax.dot_general(
        left, right, (((0,), (0,)), ((), ())), preferred_element_type=jnp.float32
    )


def layer_norm(resid, gain, shift):
    average = jnp.mean(resid, axis=-1, keepdims=True)
    centred = resid - average
    variance = jnp.mean(centred * centred, axis=-1, keepdims=True)
    return centred * lax.rsqrt(variance + NORM_EPS) * gain + shift


def unpack_all(flat_params, dp_count, fsdp_count):
    shapes = [(D, D)] * 4 + [(D, FF), (FF, D)] + [(1, D)] * 4 + [(1, FF)] + [(1, D)] * 6
    blocks = (
        flat_params.reshape(dp_count, fsdp_count, -1).transpose(1, 0, 2).reshape(fsdp_count, -1)
    )
    pieces = []
    offset = 0
    for rows, cols in shapes:
        width = rows * (cols // fsdp_count)
        part = blocks[:, offset : offset + width].reshape(fsdp_count, rows, cols // fsdp_count)
        whole = part.transpose(1, 0, 2).reshape(rows, cols)
        pieces.append(whole.reshape(-1) if rows == 1 else whole)
        offset += width
    return pieces


def split_heads(values):
    return values.reshape(values.shape[0], H, DH).transpose(1, 0, 2)


def merge_heads(values):
    return values.transpose(1, 0, 2).reshape(values.shape[1], H * DH)


def head_forward(head_item):
    query_h, key_h, value_h = head_item
    scores = product(query_h, key_h.T) * DH ** (-0.5)
    highest = jnp.max(scores, axis=1, keepdims=True)
    weights = jnp.exp(scores - highest)
    totals = jnp.sum(weights, axis=1, keepdims=True)
    probabilities = weights / totals
    result = product(probabilities.astype(jnp.bfloat16), value_h)
    return (result, (highest + jnp.log(totals))[:, 0])


def head_query_back(head_item):
    query_h, key_h, value_h, grad_h, logsum = head_item
    score_scale = DH ** (-0.5)
    scores = product(query_h, key_h.T) * score_scale
    probabilities = jnp.exp(scores - logsum[:, None])
    prob_grad = product(grad_h, value_h.T)
    inner_sum = jnp.sum(probabilities * prob_grad, axis=1)
    score_grad = (probabilities * (prob_grad - inner_sum[:, None])).astype(jnp.bfloat16)
    query_grad = product(score_grad, key_h) * score_scale
    return (query_grad, inner_sum)


def head_key_back(head_item):
    key_h, value_h, query_all, grad_all, logsum_all, inner_all = head_item
    score_scale = DH ** (-0.5)
    scores_t = product(key_h, query_all.T) * score_scale
    probs_t = jnp.exp(scores_t - logsum_all[None, :])
    prob_grad_t = product(value_h, grad_all.T)
    score_grad_t = (probs_t * (prob_grad_t - inner_all[None, :])).astype(jnp.bfloat16)
    key_grad = product(score_grad_t, query_all) * score_scale
    value_grad = product(probs_t.astype(jnp.bfloat16), grad_all)
    return (key_grad, value_grad)


def body(
    tokens,
    cotangent,
    master,
    first_moment,
    second_moment,
    average,
    timestep,
    block_length,
    block_start,
):
    dp_count = lax.axis_size("dp")
    fsdp_count = lax.axis_size("fsdp")
    master_low = master.astype(jnp.bfloat16)
    flat_params = lax.all_gather(master_low, ("dp", "fsdp"), axis=0, tiled=True)
    (
        w_query,
        w_key,
        w_value,
        w_out,
        w_up,
        w_down,
        b_query,
        b_value,
        b_out,
        b_down,
        b_up,
        gain_attn,
        shift_attn,
        gain_ffn,
        shift_ffn,
        w_time,
        b_time,
    ) = unpack_all(flat_params, dp_count, fsdp_count)
    gain_a = gain_attn.astype(jnp.float32)
    shift_a = shift_attn.astype(jnp.float32)
    gain_f = gain_ffn.astype(jnp.float32)
    shift_f = shift_ffn.astype(jnp.float32)
    row_count = tokens.shape[0]
    position = lax.axis_index("fsdp") * row_count + jnp.arange(row_count, dtype=jnp.int32)
    block_first = block_start[0]
    inside = ((position >= block_first) & (position < block_first + block_length[0])).astype(
        jnp.float32
    )[:, None]
    time_frac = timestep[0].astype(jnp.float32) / 5000.0
    time_embed = time_frac * w_time.astype(jnp.float32) + b_time.astype(jnp.float32)
    stream = tokens.astype(jnp.float32) + inside * time_embed
    stream_low = stream.astype(jnp.bfloat16)
    queries = (product(stream_low, w_query) + b_query.astype(jnp.float32)).astype(jnp.bfloat16)
    keys_local = product(stream_low, w_key).astype(jnp.bfloat16)
    values_local = (product(stream_low, w_value) + b_value.astype(jnp.float32)).astype(jnp.bfloat16)
    keys_all, values_all = (
        lax.all_gather(keys_local, "fsdp", axis=0, tiled=True),
        lax.all_gather(values_local, "fsdp", axis=0, tiled=True),
    )
    query_heads = split_heads(queries)
    key_heads = split_heads(keys_all)
    value_heads = split_heads(values_all)
    head_out, logsum = lax.map(head_forward, (query_heads, key_heads, value_heads))
    heads_low = merge_heads(head_out).astype(jnp.bfloat16)
    resid_attn = stream + product(heads_low, w_out) + b_out.astype(jnp.float32)
    normed = layer_norm(resid_attn, gain_a, shift_a)
    normed_low = normed.astype(jnp.bfloat16)
    pre_act = product(normed_low, w_up) + b_up.astype(jnp.float32)
    hidden = jax.nn.gelu(pre_act, approximate=False).astype(jnp.bfloat16)
    resid_ffn = normed + product(hidden, w_down) + b_down.astype(jnp.float32)
    block_out = layer_norm(resid_ffn, gain_f, shift_f).astype(jnp.bfloat16)
    stream_all, heads_all, normed_all, hidden_all = (
        lax.all_gather(stream_low, "fsdp", axis=0, tiled=True),
        lax.all_gather(heads_low, "fsdp", axis=0, tiled=True),
        lax.all_gather(normed_low, "fsdp", axis=0, tiled=True),
        lax.all_gather(hidden, "fsdp", axis=0, tiled=True),
    )
    back_params = lax.all_gather(master_low, ("dp", "fsdp"), axis=0, tiled=True)
    back_pieces = unpack_all(back_params, dp_count, fsdp_count)
    w_query_back, w_key_back, w_value_back, w_out_back, w_up_back, w_down_back = back_pieces[:6]
    out_grad = cotangent.astype(jnp.float32)
    _, pull_ffn = jax.vjp(layer_norm, resid_ffn, gain_f, shift_f)
    resid_ffn_grad, grad_gain_ffn, grad_shift_ffn = pull_ffn(out_grad)
    ffn_grad = resid_ffn_grad.astype(jnp.bfloat16)
    hidden_grad = product(ffn_grad, w_down_back.T)
    _, pull_gelu = jax.vjp(partial(jax.nn.gelu, approximate=False), pre_act)
    pre_grad = pull_gelu(hidden_grad)[0].astype(jnp.bfloat16)
    normed_grad = resid_ffn_grad + product(pre_grad, w_up_back.T)
    _, pull_attn = jax.vjp(layer_norm, resid_attn, gain_a, shift_a)
    resid_attn_grad, grad_gain_attn, grad_shift_attn = pull_attn(normed_grad)
    attn_grad = resid_attn_grad.astype(jnp.bfloat16)
    heads_grad = product(attn_grad, w_out_back.T).astype(jnp.bfloat16)
    query_parts, inner_sum = lax.map(
        head_query_back, (query_heads, key_heads, value_heads, split_heads(heads_grad), logsum)
    )
    query_grad = merge_heads(query_parts).astype(jnp.bfloat16)
    queries_all, heads_grad_all = (
        lax.all_gather(queries, "fsdp", axis=0, tiled=True),
        lax.all_gather(heads_grad, "fsdp", axis=0, tiled=True),
    )
    logsum_all, inner_all = (
        lax.all_gather(logsum, "fsdp", axis=1, tiled=True),
        lax.all_gather(inner_sum, "fsdp", axis=1, tiled=True),
    )
    key_parts, value_parts = lax.map(
        head_key_back,
        (
            split_heads(keys_local),
            split_heads(values_local),
            split_heads(queries_all),
            split_heads(heads_grad_all),
            logsum_all,
            inner_all,
        ),
    )
    key_grad = merge_heads(key_parts).astype(jnp.bfloat16)
    value_grad = merge_heads(value_parts).astype(jnp.bfloat16)
    stream_grad = (
        resid_attn_grad
        + product(query_grad, w_query_back.T)
        + product(key_grad, w_key_back.T)
        + product(value_grad, w_value_back.T)
    )
    grad_b_time = jnp.sum(inside * stream_grad, axis=0)
    grad_w_time = time_frac * grad_b_time
    query_cols, key_cols, value_cols, attn_cols, ffn_cols, pre_cols = (
        lax.all_to_all(query_grad, "fsdp", split_axis=1, concat_axis=0, tiled=True),
        lax.all_to_all(key_grad, "fsdp", split_axis=1, concat_axis=0, tiled=True),
        lax.all_to_all(value_grad, "fsdp", split_axis=1, concat_axis=0, tiled=True),
        lax.all_to_all(attn_grad, "fsdp", split_axis=1, concat_axis=0, tiled=True),
        lax.all_to_all(ffn_grad, "fsdp", split_axis=1, concat_axis=0, tiled=True),
        lax.all_to_all(pre_grad, "fsdp", split_axis=1, concat_axis=0, tiled=True),
    )
    grad_w_query = product_inner(stream_all, query_cols)
    grad_w_key = product_inner(stream_all, key_cols)
    grad_w_value = product_inner(stream_all, value_cols)
    grad_w_out = product_inner(heads_all, attn_cols)
    grad_w_up = product_inner(normed_all, pre_cols)
    grad_w_down = product_inner(hidden_all, ffn_cols)
    grad_b_query = jnp.sum(query_cols.astype(jnp.float32), axis=0)
    grad_b_value = jnp.sum(value_cols.astype(jnp.float32), axis=0)
    grad_b_out = jnp.sum(attn_cols.astype(jnp.float32), axis=0)
    grad_b_down = jnp.sum(ffn_cols.astype(jnp.float32), axis=0)
    grad_b_up = jnp.sum(pre_cols.astype(jnp.float32), axis=0)
    vector_terms = jnp.stack(
        [grad_gain_attn, grad_shift_attn, grad_gain_ffn, grad_shift_ffn, grad_w_time, grad_b_time]
    )
    vector_part = lax.psum_scatter(vector_terms, "fsdp", scatter_dimension=1, tiled=True)
    vector_block = jnp.concatenate(
        [grad_b_query, grad_b_value, grad_b_out, grad_b_down, grad_b_up, vector_part.reshape(-1)]
    )
    grad_block = jnp.concatenate(
        [
            piece.reshape(-1)
            for piece in (
                grad_w_query,
                grad_w_key,
                grad_w_value,
                grad_w_out,
                grad_w_up,
                grad_w_down,
            )
        ]
        + [vector_block]
    )
    grad_shard = lax.psum_scatter(grad_block, "dp", scatter_dimension=0, tiled=True)
    vector_grad = lax.psum(vector_block, "dp")
    square_sum = lax.psum(jnp.sum(grad_shard * grad_shard), ("dp", "fsdp"))
    grad_norm = jnp.sqrt(square_sum)
    clip_limit = 4.0 * math.sqrt(PARAMS)
    clipped = grad_shard * (clip_limit / jnp.maximum(grad_norm, clip_limit))
    new_first = 0.9 * first_moment + 0.1 * clipped
    new_second = 0.98 * second_moment + 0.02 * clipped * clipped
    first_hat = new_first / (1.0 - 0.9**STEP)
    second_hat = new_second / (1.0 - 0.98**STEP)
    new_master = master - 0.02 * (first_hat / (jnp.sqrt(second_hat) + 1e-06) + 0.01 * master)
    new_average = 0.99 * average + 0.01 * new_master
    return (
        block_out,
        stream_grad,
        grad_norm,
        vector_grad,
        new_first,
        new_second,
        new_master,
        new_average,
    )


AXES = ("dp", "fsdp")


def send(values, route, name="move"):
    pairs = []
    for n in range(32):
        there = route(n // 8, n // 4 % 2, n // 2 % 2, n % 2)
        if there is not None:
            z, y, x, c = there
            pairs.append((n, z * 8 + y * 4 + x * 2 + c))
    with jax.named_scope(name):
        return lax.ppermute(values, AXES, pairs)


def to_core(z, y, x, c):
    return z, y, x, 1 - c


def to_x(z, y, x, c):
    return z, y, 1 - x, c


def to_y(z, y, x, c):
    return z, 1 - y, x, c


def to_near(z, y, x, c):
    return z ^ 1, y, x, c


def to_far(z, y, x, c):
    return z ^ 2, y, x, c


def only(route, planes):
    return lambda z, y, x, c: route(z, y, x, c) if z in planes else None


EVERY = (to_core, to_x, to_y, to_near, to_far)


def total(values, name):
    for route in EVERY:
        values = values + send(values, route, name)
    return values


def to_relative(r):
    return lambda z, y, x, c: (z, y, x ^ (r // 2), c ^ (r % 2))


def exchange(blocks, name):
    return [blocks[0]] + [send(blocks[r], to_relative(r), name) for r in range(1, 4)]


def after(values, *earlier):
    return lax.optimization_barrier((values, *earlier))[0]


PLANES = ((1, 2, 3), (0, 1, 3), (0, 2), (0, 1, 2, 3))


def gather_pieces(own, z, y, tokens, run_attend):
    def across(name, values, n):
        return send(values, only(to_x, PLANES[n]), name)

    outer = (z == 0) | (z == 3)
    first = send(own, lambda z, y, x, c: ((2, 0, 3, 1)[z], y, x, c), "first")
    y0 = send(own, to_y, "y0")
    tokens_x = send(tokens, to_x, "tok_x")
    x0 = across("x0", own, 0)
    tokens_c = send(tokens, to_core, "tok_c")
    second = send(after(jnp.where(outer, own, first), tokens_x), to_near, "second")
    crossed = send(
        after(own, first), lambda z, y, x, c: (3 - z, y, x, c) if z in (1, 2) else None, "crossed"
    )
    y1 = send(after(first, y0), to_y, "y1")
    x1 = across("x1", after(first, x0), 1)
    third = send(after(crossed, second), only(to_near, (1, 2)), "third")
    y2 = send(after(second, y1), to_y, "y2")
    x_a = send(jnp.where(z % 2 == 0, second, y0), to_x, "xa")
    last = jnp.where(outer, third, crossed)
    tokens_xc = send(after(tokens_x, third), to_core, "tok_xc")
    y3 = send(after(last, y2), to_y, "y3")
    y_b = send(after(jnp.where(z == 2, x0, x1), y2), to_y, "yb")
    yx2 = across("yx2", after(y2, last), 2)
    x3 = across("x3", after(last, y2), 3)
    tail_0, tail_1, tail_2 = (
        jnp.where(y == 1, mine[TAIL:], other[TAIL:])
        for mine, other in ((own, y0), (first, y1), (second, y2))
    )
    attended = run_attend(
        after(last, y2), (own, y0, first, y1, second, y2, last, x0, x1),
        (tokens, tokens_c, tokens_x, tokens_xc),
        jnp.where(z == 3, tail_0, jnp.where(z == 1, tail_1, tail_2)),
        jnp.where(z == 0, tail_0, jnp.where(z == 2, tail_1, tail_2)),
    )
    attended = lax.optimization_barrier((*attended, x_a, y3, yx2, x3, y_b))[: len(attended)]
    stack = send(attended[-1], to_core, "stack")
    heads = exchange(attended[5:9], "heads")
    yx3 = across("yx3", after(y3, x3, attended[-1]), 3)
    later = [
        send(after(piece, attended[-1]), only(to_core, planes), name)
        for piece, planes, name in (
            (x_a, (0, 1, 2, 3), "cxa"), (y3, (0, 1, 2, 3), "cy3"), (y_b, (0, 1, 2, 3), "cyb"),
            (yx2, PLANES[2], "cyx2"), (x3, (0, 1, 2, 3), "cx3"), (yx3, (0, 1, 2, 3), "cyx3"),
        )
    ]
    mine = [own, first, second, last, y0, y1, y2, x0, x1, x_a, y3, y_b, yx2, x3, yx3]
    return attended[:5], heads, attended[9], [*mine, stack, *later]


def add(left, right):
    return wide(left) + wide(right)


def block_body(
    tokens,
    cotangent,
    master,
    first_moment,
    second_moment,
    average,
    timestep,
    block_length,
    block_start,
):
    shard = lax.axis_index("dp")
    j = lax.axis_index("fsdp")
    z, y = shard // 2, shard % 2
    place = jnp.stack([shard, z, y, j, block_start[0], block_length[0]]).astype(jnp.int32)
    flat = jnp.pad(master, (0, LANE_ROWS * 128 - SHARD)).reshape(LANE_ROWS, 128)
    vec_rows = jnp.pad(master[SHARD - 3584 :].reshape(14, 256), ((0, 2), (0, 0)))
    head_rows = jnp.pad(master[SHARD - 896 :], (0, 3200)).reshape(16, 256)
    tail = low(jnp.where(shard == 7, vec_rows, head_rows))
    tail_x = after(send(tail, to_x, "tail_x"), flat)
    tail_c = send(jnp.concatenate([tail, tail_x]), to_core, "tail_c")
    own = pack(place, flat, jnp.concatenate([tail, tail_c[:16], tail_x, tail_c[16:]]))
    here = (jnp.arange(4) == j)[:, None, None]
    time_frac = timestep[0].astype(jnp.float32) / 5000.0
    vectors = {}

    def absolute(relative):
        blocks = relative.reshape(4, 16, 256)
        blocks = jnp.where(j % 2 == 1, jnp.concatenate([blocks[1:2], blocks[0:1], blocks[3:4], blocks[2:3]]), blocks)
        return jnp.where(j // 2 == 1, jnp.concatenate([blocks[2:4], blocks[0:2]]), blocks)

    def run_attend(ready, held, all_tokens, vec_tail, head_tail):
        vec = wide(absolute(vec_tail))
        full = vec.transpose(1, 0, 2).reshape(16, D)
        vec_own = wide(vec_tail[:16])
        vectors["embed"] = time_frac * full[12:13] + full[13:14]
        vectors["rows"] = jnp.concatenate([full[2:4], full[8:12], jnp.zeros((2, D), jnp.float32)])
        vectors["up"] = vec[:, 4:8].reshape(16, 256)
        vectors["head"] = absolute(head_tail)
        return attend(after(place, ready), all_tokens, vectors["embed"], vec_own[0:8], held)

    attended, heads, lse, pieces = gather_pieces(own, z, y, tokens, run_attend)
    stream, weight, query, key, value = attended

    (block_out, resid_grad, g0, g1, g2, g3, sums, sums_up, head_grad, *grads) = layer(
        place, heads, tokens, cotangent, vectors["embed"],
        vectors["rows"], vectors["up"], vectors["head"], pieces,
    )
    grads_own, grads_other = grads[:3], grads[3:]

    moved = {k: send(grads_other[k - 1], to_core, f"rc{k}") for k in (2, 1)}
    moved[3] = send(after(grads_other[2], moved[2], moved[1]), to_core, "rc3")

    def over_cores(k, a, b):
        return add(grads_own[k - 1][a, b], moved[k][a, b])

    grad_heads = exchange((g0, g1, g2, g3), "heads_grad")
    starts = {
        name: after(low(over_cores(k, 1, b)), *grad_heads)
        for name, k, b in (("d1", 1, 1), ("d2", 2, 1), ("e1", 1, 0), ("e2", 2, 0))
    }
    d1 = send(starts["d1"], to_y, "d1")
    d2 = send(starts["d2"], to_x, "d2")
    e1 = send(starts["e1"], to_y, "e1")
    e2 = send(starts["e2"], to_x, "e2")

    (q_grad, k_grad, v_grad, kept, sent, sums_qkv) = attend_back(
        after(place, *starts.values()),
        query, key, value, lse, weight, grad_heads,
    )

    q_grad, k_grad, v_grad, kept, sent, sums_qkv, d1, d2 = lax.optimization_barrier(
        (q_grad, k_grad, v_grad, kept, sent, sums_qkv, d1, d2)
    )
    sum_1 = low(over_cores(1, 0, 1) + wide(d1))
    sum_2 = low(over_cores(2, 0, 1) + wide(d2))
    sum_3 = low(over_cores(3, 1, 1))
    sum_1, sum_2, sum_3, e1, e2, sent = lax.optimization_barrier(
        (sum_1, sum_2, sum_3, e1, e2, sent)
    )
    from_core = send(sent, to_core, "in_c")
    f1 = send(sum_1, to_x, "f1")
    f2 = send(sum_2, to_y, "f2")
    q_grad, k_grad, v_grad, sum_3, from_core = lax.optimization_barrier(
        (q_grad, k_grad, v_grad, sum_3, from_core)
    )
    d3 = send(sum_3, to_x, "d3")
    e3 = send(after(low(over_cores(3, 1, 0)), f1), to_x, "e3")

    rows = stream.reshape(1024, D)
    w_grads = [low(product_inner(rows, grad)) for grad in (q_grad, k_grad, v_grad)]
    rest = jnp.zeros((PIECE - 1552, 256), jnp.bfloat16)
    piece_0 = jnp.concatenate([w_grads[0], w_grads[1][:528], rest])
    piece_1 = jnp.concatenate([w_grads[1][512:], w_grads[2], rest, rest[:16]])
    low_row = y == 0
    other_row = jnp.where(low_row, piece_1, piece_0)
    ry0 = send(other_row, to_y, "ry0")
    kept_1, sent_1 = combine(
        after(place, other_row, sum_3), (grads_own[1], moved[2], e2, f2), (grads_own[0], moved[1], e1, f1)
    )
    got_inner = send(sent_1, to_near, "rz_inner1")
    inner_part = low(add(kept_1, got_inner))
    inner_last = send(inner_part, only(to_far, (0, 3)), "rz_inner2")
    f3 = send(low(over_cores(3, 0, 1) + wide(after(d3, ry0))), to_y, "f3")
    kept_0, sent_0 = combine(
        after(place, inner_part), (jnp.where(low_row, piece_0, piece_1), ry0), (grads_own[2], moved[3], e3, f3)
    )
    outer_part = low(add(kept_0, send(after(sent_0, inner_last), to_near, "rz_outer1")))
    outer_last = send(outer_part, only(to_far, (1, 2)), "rz_outer2")

    in_x = send(after(low(kept[1] + wide(from_core[1])), e3), to_x, "in_x")
    input_grad = (
        resid_grad
        + kept[0]
        + wide(from_core[0])
        + wide(in_x)
    )

    time_grad = sums[6] + sums_qkv[0]
    rows_of = [sums[0], sums[1]]
    vec_grad = jnp.concatenate(
        [
            jnp.where(here, sums_qkv[1:3, :256][None], 0.0),
            sums[0:2].reshape(2, 4, 256).transpose(1, 0, 2),
            sums_up.reshape(4, 4, 256),
            sums[2:6].reshape(4, 4, 256).transpose(1, 0, 2),
            (time_frac * time_grad).reshape(4, 1, 256),
            time_grad.reshape(4, 1, 256),
            jnp.zeros((4, 2, 256), jnp.float32),
            jnp.where(jnp.arange(4096).reshape(1, 16, 256) < 896, head_grad, 0.0),
        ],
        axis=1,
    )
    vec_grad = vec_grad.reshape(2, 2, 32, 256)
    core_bit, x_bit = j % 2, j // 2
    kept_c = jnp.where(core_bit == 1, vec_grad[:, 1], vec_grad[:, 0])
    sent_c = jnp.where(core_bit == 1, vec_grad[:, 0], vec_grad[:, 1])
    by_x = kept_c + send(sent_c, to_core, "vec_c")
    kept_x = jnp.where(x_bit == 1, by_x[1], by_x[0])
    mine = kept_x + send(jnp.where(x_bit == 1, by_x[0], by_x[1]), to_x, "vec_x")

    grad_flat, square = unpack(after(place, input_grad), inner_part, inner_last, outer_part, outer_last)
    mine = jnp.concatenate([mine, square])
    for route in (to_y, to_near, to_far):
        mine = mine + send(mine, route, "norm")
    vec_sum, head_sum = mine[:14].reshape(-1), mine[16:20].reshape(-1)[:896]
    vector_grad = vec_sum
    is_sum = jnp.arange(40)[:, None] >= 32
    square_sum = jnp.sum(jnp.where(is_sum, mine, mine * mine))
    square_sum = jnp.broadcast_to(square_sum, (8, 128))
    for route in (to_x, to_core):
        square_sum = square_sum + send(square_sum, route, "norm")
    grad_norm = jnp.sqrt(square_sum[0, 0])
    grad_flat = grad_flat.reshape(-1)
    edge = grad_flat[SHARD - 3584 : SHARD]
    edge = jnp.where(
        shard == 7,
        vec_sum,
        jnp.where(shard == 1, jnp.concatenate([edge[: 3584 - 896], head_sum]), edge),
    )
    grad_shard = lax.dynamic_update_slice(grad_flat, edge, (SHARD - 3584,))[:SHARD]
    clip_limit = 4.0 * math.sqrt(PARAMS)
    clipped = grad_shard * (clip_limit / jnp.maximum(grad_norm, clip_limit))
    new_first = 0.9 * first_moment + 0.1 * clipped
    new_second = 0.98 * second_moment + 0.02 * clipped * clipped
    first_hat = new_first / (1.0 - 0.9**STEP)
    second_hat = new_second / (1.0 - 0.98**STEP)
    new_master = master - 0.02 * (first_hat / (jnp.sqrt(second_hat) + 1e-06) + 0.01 * master)
    new_average = 0.99 * average + 0.01 * new_master
    return (
        block_out,
        input_grad,
        grad_norm,
        vector_grad,
        new_first,
        new_second,
        new_master,
        new_average,
    )


def solution(mesh):
    return jax.shard_map(
        block_body if mesh.shape["dp"] == 8 and mesh.shape["fsdp"] == 4 else body,
        mesh=mesh,
        in_specs=(
            P(("dp", "fsdp"), None),
            P(("dp", "fsdp"), None),
            P(("dp", "fsdp")),
            P(("dp", "fsdp")),
            P(("dp", "fsdp")),
            P(("dp", "fsdp")),
            P("dp"),
            P("dp"),
            P("dp"),
        ),
        out_specs=(
            P(("dp", "fsdp"), None),
            P(("dp", "fsdp"), None),
            P(),
            P("fsdp"),
            P(("dp", "fsdp")),
            P(("dp", "fsdp")),
            P(("dp", "fsdp")),
            P(("dp", "fsdp")),
        ),
        check_vma=False,
    )
```

```python
from functools import partial
import math

import jax
import jax.numpy as jnp
from jax import lax
from jax.experimental import pallas as pl
from jax.experimental.pallas import tpu as pltpu
from jax.sharding import PartitionSpec as P

D = 1024
H = 16
DH = 64
FF = 4096
STEP = 10
PARAMS = 12597248
NORM_EPS = 1e-05

SHARD = PARAMS // 32
PIECE = 1600
LANE_ROWS = 3080
PAD = 128
TAIL = 1536
REGIONS = (
    ("q", 0, 1024, 256),
    ("k", 262144, 1024, 256),
    ("v", 524288, 1024, 256),
    ("o", 786432, 1024, 256),
    ("up", 1048576, 1024, 1024),
    ("down", 2097152, 4096, 256),
    ("vec", 3145728, 16, 256),
)


def segments(shard):
    low, high = shard * SHARD, (shard + 1) * SHARD
    found, offset = [], 0
    for name, start, rows, width in REGIONS:
        size = 3584 if name == "vec" else rows * width
        first, last = max(low, start), min(high, start + size)
        if first >= last:
            continue
        row_a = (first - start) // width // 16 * 16
        row_b = min(rows, -(-(-(-(last - start) // width)) // 16) * 16)
        found.append((name, row_a, row_b, offset, width // 128, start // 128))
        offset += (row_b - row_a) * (width // 256)
    return found


def lane_start(shard):
    return shard * SHARD // 128


SEGMENTS = [segments(shard) for shard in range(8)]
SLOT = ((0, 1, 3, 2), (2, 0, 3, 1), (1, 3, 0, 2), (2, 3, 1, 0))


def buffers(z):
    x_a, y_b = 9, 11
    over_x = [7, 8, x_a, 13]
    both = [y_b if z == 2 else x_a, y_b, 12, 14]
    return [0, 1, 2, 3, 4, 5, 6, 10, *over_x, *both]


BUFFER = [buffers(z) for z in range(4)]


def dot(left, right):
    return jnp.dot(left, right, preferred_element_type=jnp.float32)


def dot_last(left, right):
    return lax.dot_general(
        left, right, (((1,), (1,)), ((), ())), preferred_element_type=jnp.float32
    )


def dot_first(left, right):
    return lax.dot_general(
        left, right, (((0,), (0,)), ((), ())), preferred_element_type=jnp.float32
    )


def low(values):
    return values.astype(jnp.bfloat16)


def wide(values):
    return values.astype(jnp.float32)


VMEM = pl.BlockSpec(memory_space=pltpu.VMEM)
SMEM = pl.BlockSpec(memory_space=pltpu.SMEM)
ANY = pl.BlockSpec(memory_space=pl.ANY)


def struct(shape, kind=jnp.bfloat16):
    return jax.ShapeDtypeStruct(shape, kind)


def chunks(rows, most=128):
    return [(a, min(most, rows - a)) for a in range(0, rows, most)]


def pack_kernel(place, flat, tails, piece, rolled, rows):
    shard = place[0]
    rows[0:PAD, :] = jnp.zeros((PAD, 128), jnp.float32)
    rows[PAD + LANE_ROWS : PAD + LANE_ROWS + PAD, :] = jnp.zeros((PAD, 128), jnp.float32)
    rolled[0:8, :] = jnp.zeros((8, 128), jnp.float32)

    @pl.when(shard % 2 == 0)
    def _():
        for a, n in chunks(LANE_ROWS):
            rows[PAD + a : PAD + a + n, :] = flat[a : a + n, :]

    @pl.when(shard % 2 == 1)
    def _():
        for a, n in chunks(LANE_ROWS):
            rolled[8 + a : 8 + a + n, :] = pltpu.roll(flat[a : a + n, :], 64, 1)
        for a, n in chunks(LANE_ROWS):
            lane = lax.broadcasted_iota(jnp.int32, (n, 128), 1)
            rows[PAD + a : PAD + a + n, :] = jnp.where(
                lane < 64, rolled[7 + a : 7 + a + n, :], rolled[8 + a : 8 + a + n, :]
            )

    for case in range(8):

        @pl.when(shard == case)
        def _(case=case):
            for _, row_a, row_b, offset, step, first in SEGMENTS[case]:
                if offset == TAIL:
                    piece[TAIL:PIECE, :] = tails[...]
                    continue
                count = row_b - row_a
                base = PAD + first + step * row_a - lane_start(case)
                for t in range(step):
                    out = offset + t // 2 * count
                    lanes = slice(t % 2 * 128, t % 2 * 128 + 128)
                    for a, n in chunks(count):
                        piece[out + a : out + a + n, lanes] = low(
                            rows[pl.ds(base + t + step * a, n, stride=step), :]
                        )


def pack(place, flat, tails):
    return pl.pallas_call(
        pack_kernel,
        out_shape=struct((PIECE, 256)),
        in_specs=[SMEM, VMEM, VMEM],
        out_specs=VMEM,
        scratch_shapes=[
            pltpu.VMEM((8 + LANE_ROWS, 128), jnp.float32),
            pltpu.VMEM((PAD + LANE_ROWS + PAD, 128), jnp.float32),
        ],
        compiler_params=pltpu.CompilerParams(vmem_limit_bytes=24 << 20),
        name="pack",
    )(place, flat, tails)


def unpack_kernel(place, inner, inner_last, outer, outer_last, flat, square, rows, left, right, sem):
    shard = place[0]
    is_inner = (place[1] == 1) | (place[1] == 2)

    def fetch(first, second):
        copies = [
            pltpu.make_async_copy(first, left, sem.at[0]),
            pltpu.make_async_copy(second, right, sem.at[1]),
        ]
        for copy in copies:
            copy.start()
        for copy in copies:
            copy.wait()

    @pl.when(is_inner)
    def _():
        fetch(inner, inner_last)

    @pl.when(jnp.logical_not(is_inner))
    def _():
        fetch(outer, outer_last)

    for case in range(8):

        @pl.when(shard == case)
        def _(case=case):
            for _, row_a, row_b, offset, step, first in SEGMENTS[case]:
                count = row_b - row_a
                base = PAD + first + step * row_a - lane_start(case)
                for t in range(step):
                    source = offset + t // 2 * count
                    lanes = slice(t % 2 * 128, t % 2 * 128 + 128)
                    for a, n in chunks(count):
                        spot = slice(source + a, source + a + n)
                        value = wide(left[spot, lanes]) + wide(right[spot, lanes])
                        if offset == TAIL:
                            value = jnp.zeros((n, 128), jnp.float32)
                        rows[pl.ds(base + t + step * a, n, stride=step), :] = value

    square[...] = jnp.zeros_like(square)
    for odd in range(2):

        @pl.when(shard % 2 == odd)
        def _(odd=odd):
            total = jnp.zeros((8, 128), jnp.float32)
            for a, n in chunks(LANE_ROWS):
                value = rows[PAD + a : PAD + a + n, :]
                lane = lax.broadcasted_iota(jnp.int32, (n, 128), 1)
                if odd:
                    after = rows[PAD + a + 1 : PAD + a + 1 + n, :]
                    value = jnp.where(
                        lane < 64, pltpu.roll(value, 64, 1), pltpu.roll(after, 64, 1)
                    )
                if (a + n) * 128 > SHARD:
                    row = lax.broadcasted_iota(jnp.int32, (n, 128), 0) + a
                    value = jnp.where(row * 128 + lane < SHARD, value, 0.0)
                flat[a : a + n, :] = value
                total += jnp.sum((value * value).reshape(n // 8, 8, 128), axis=0)
            square[:, 0:128] = total


def unpack(place, *pieces):
    return pl.pallas_call(
        unpack_kernel,
        out_shape=(struct((LANE_ROWS, 128), jnp.float32), struct((8, 256), jnp.float32)),
        in_specs=[SMEM] + [ANY] * 4,
        out_specs=(VMEM, VMEM),
        scratch_shapes=[
            pltpu.VMEM((PAD + LANE_ROWS + PAD, 128), jnp.float32),
            pltpu.VMEM((PIECE, 256), jnp.bfloat16),
            pltpu.VMEM((PIECE, 256), jnp.bfloat16),
            pltpu.SemaphoreType.DMA((2,)),
        ],
        compiler_params=pltpu.CompilerParams(vmem_limit_bytes=60 << 20),
        name="unpack",
    )(place, *pieces)


def combine_kernel(split, place, *refs):
    kept, sent = refs[-2:]
    first = sum(wide(ref[...]) for ref in refs[:split])
    second = sum(wide(ref[...]) for ref in refs[split:-2])
    even = place[1] % 2 == 0
    kept[...] = low(jnp.where(even, first, second))
    sent[...] = low(jnp.where(even, second, first))


def combine(place, first, second):
    blocks = 2
    size = PIECE // blocks

    def spec(piece):
        if piece.ndim == 4:
            return pl.BlockSpec((None, None, size, 256), lambda n: (0, 0, n, 0))
        return pl.BlockSpec((size, 256), lambda n: (n, 0))

    pieces = [*first, *second]
    return pl.pallas_call(
        partial(combine_kernel, len(first)),
        grid=(blocks,),
        out_shape=(struct((PIECE, 256)), struct((PIECE, 256))),
        in_specs=[SMEM] + [spec(piece) for piece in pieces],
        out_specs=(pl.BlockSpec((size, 256), lambda n: (n, 0)),) * 2,
        compiler_params=pltpu.CompilerParams(vmem_limit_bytes=60 << 20),
        name="combine",
    )(place, *pieces)


def column_sum(values):
    return jnp.sum(values, axis=0, keepdims=True)


def inside_column(place, relative):
    rows = lax.broadcasted_iota(jnp.int32, (256, 1), 0)
    position = rows + (place[3] ^ relative) * 256
    return ((position >= place[4]) & (position < place[4] + place[5])).astype(jnp.float32)


def attend_kernel(
    place, embed, bias, t0, t1, t2, t3, p0, p1, p2, p3, p4, p5, p6, p7, p8,
    stream_out, weight_out, q_out, k_out, v_out, h0, h1, h2, h3, lse_out, stack,
    tokens, staged, q_heads, k_t, v_heads, o_heads, edge, sem, sem_tokens, sem_in, sem_out,
):
    fetches = [
        pltpu.make_async_copy(ref, tokens.at[r], sem_tokens.at[r])
        for r, ref in enumerate((t0, t1, t2, t3))
    ]
    for copy in fetches:
        copy.start()

    def copies(first, second):
        return [
            pltpu.make_async_copy(first.at[0:1024, :], weight_out.at[0], sem.at[0]),
            pltpu.make_async_copy(first.at[1024:1552, :], weight_out.at[1, 0:528, :], sem.at[1]),
            pltpu.make_async_copy(second.at[16:512, :], weight_out.at[1, 528:1024, :], sem.at[2]),
            pltpu.make_async_copy(second.at[0:16, :], edge, sem.at[3]),
            pltpu.make_async_copy(second.at[512:1536, :], weight_out.at[2], sem.at[4]),
        ]

    held = ((p0, p1), (p2, p3), (p4, p5))
    for z in range(4):
        for y in range(2):
            own, other = held[SLOT[z][0]]
            pair = (other, own) if y else (own, other)

            @pl.when((place[1] == z) & (place[2] == y))
            def _(pair=pair):
                for copy in copies(*pair):
                    copy.start()

    held_in = [
        pltpu.make_async_copy(ref, staged.at[n], sem_in.at[n])
        for n, ref in enumerate((p0, p2, p4, p6, p1, p3, p5, p7, p8))
    ]
    held_out = [pltpu.make_async_copy(staged.at[n], stack.at[n], sem_out.at[n]) for n in range(9)]
    for copy in held_in:
        copy.start()
    for r, copy in enumerate(fetches):
        copy.wait()
        stream_out[r] = low(wide(tokens[r]) + inside_column(place, r) * embed[...])
    lanes = lax.broadcasted_iota(jnp.int32, (1024, 128), 1)
    v_heads[...] = jnp.broadcast_to((lanes >= 64).astype(jnp.bfloat16), (4, 1024, 128))
    for copy in copies(p0, p1):
        copy.wait()
    weight_out[1, 512:528, :] = weight_out[1, 512:528, :] + edge[...]
    for r in range(4):
        rows = slice(r * 256, r * 256 + 256)
        stream = stream_out[r]
        query = low(dot(stream, weight_out[0]) + bias[0:1, :])
        key = low(dot(stream, weight_out[1]))
        value = low(dot(stream, weight_out[2]) + bias[1:2, :])
        q_out[rows, :] = query
        k_out[rows, :] = key
        v_out[rows, :] = value
        for h in range(4):
            cols = slice(h * 64, h * 64 + 64)
            q_heads[h, rows, :] = query[:, cols] * 0.125
            v_heads[h, rows, 0:64] = value[:, cols]
        k_t[:, rows] = key.T
    lse_out[...] = jnp.zeros_like(lse_out)
    for before, copy in zip(held_in, held_out):
        before.wait()
        copy.start()

    def head_step(h, _):
        key_t = k_t[pl.ds(pl.multiple_of(h * 64, 64), 64), :]
        for r in range(4):
            rows = slice(r * 256, r * 256 + 256)
            scores = dot(q_heads[h, rows, :], key_t)
            highest = jnp.max(scores, axis=1, keepdims=True)
            weights = low(jnp.exp(scores - highest))
            result = dot(weights, v_heads[h])
            total = result[:, 64:65]
            o_heads[h, rows, :] = low(result[:, 0:64] / total)
            lane = lax.broadcasted_iota(jnp.int32, (256, 128), 1)
            lse_out[rows, :] = jnp.where(lane == h, highest + jnp.log(total), lse_out[rows, :])
        return 0

    lax.fori_loop(0, 4, head_step, 0, unroll=4)
    for r, out in enumerate((h0, h1, h2, h3)):
        for h in range(4):
            out[:, h * 64 : h * 64 + 64] = o_heads[h, r * 256 : r * 256 + 256, :]
    for copy in held_out:
        copy.wait()


def attend(place, tokens, embed, bias, pieces):
    square = struct((1024, 256))
    block = struct((256, 256))
    return pl.pallas_call(
        attend_kernel,
        out_shape=(
            struct((4, 256, 1024)), struct((3, 1024, 256)), square, square, square,
            block, block, block, block, struct((1024, 128), jnp.float32), struct((9, PIECE, 256)),
        ),
        in_specs=[SMEM] + [VMEM] * 2 + [ANY] * 13,
        out_specs=(VMEM,) * 10 + (ANY,),
        scratch_shapes=[
            pltpu.VMEM((4, 256, 1024), jnp.bfloat16),
            pltpu.VMEM((9, PIECE, 256), jnp.bfloat16),
            pltpu.VMEM((4, 1024, 64), jnp.bfloat16),
            pltpu.VMEM((256, 1024), jnp.bfloat16),
            pltpu.VMEM((4, 1024, 128), jnp.bfloat16),
            pltpu.VMEM((4, 1024, 64), jnp.bfloat16),
            pltpu.VMEM((16, 256), jnp.bfloat16),
            pltpu.SemaphoreType.DMA((5,)),
            pltpu.SemaphoreType.DMA((4,)),
            pltpu.SemaphoreType.DMA((9,)),
            pltpu.SemaphoreType.DMA((9,)),
        ],
        compiler_params=pltpu.CompilerParams(vmem_limit_bytes=48 << 20),
        cost_estimate=pl.CostEstimate(
            flops=16_000_000_000, bytes_accessed=24_000_000, transcendentals=4_194_304
        ),
        name="attend",
    )(place, embed, bias, *tokens, *pieces)


def attend_back_kernel(
    place, q_in, k_in, v_in, lse, weight, g0, g1, g2, g3,
    q_grad, k_grad, v_grad, kept, sent, sums,
    q_heads, k_heads, g_heads, q_t, k_t, v_t, g_t, dq_heads, dk_t, dv_t,
):
    for r, grad in enumerate((g0, g1, g2, g3)):
        rows = slice(r * 256, r * 256 + 256)
        g_t[:, rows] = grad[...].T
        for h in range(4):
            cols = slice(h * 64, h * 64 + 64)
            q_heads[h, rows, :] = q_in[rows, cols] * 0.125
            k_heads[h, rows, :] = k_in[rows, cols]
            g_heads[h, rows, :] = grad[:, cols]
    q_t[...] = (q_in[...] * 0.125).T
    k_t[...] = k_in[...].T
    v_t[...] = v_in[...].T

    def head_step(h, _):
        mine = pl.ds(pl.multiple_of(h * 64, 64), 64)
        key_t, value_t, key = k_t[mine, :], v_t[mine, :], k_heads[h]
        key_sum = jnp.zeros((64, 1024), jnp.float32)
        value_sum = jnp.zeros((64, 1024), jnp.float32)
        for r in range(4):
            rows = slice(r * 256, r * 256 + 256)
            scores = dot(q_heads[h, rows, :], key_t)
            lane = lax.broadcasted_iota(jnp.int32, (256, 128), 1)
            logsum = jnp.sum(jnp.where(lane == h, lse[rows, :], 0.0), axis=1, keepdims=True)
            probs = jnp.exp(scores - logsum)
            weighted = probs * dot(g_heads[h, rows, :], value_t)
            inner = jnp.sum(weighted, axis=1, keepdims=True)
            score_grad = low(weighted - probs * inner)
            dq_heads[h, rows, :] = low(dot(score_grad, key) * 0.125)
            key_sum += dot(q_t[mine, rows], score_grad)
            value_sum += dot(g_t[mine, rows], low(probs))
        dk_t[mine, :] = low(key_sum)
        dv_t[mine, :] = low(value_sum)
        return 0

    lax.fori_loop(0, 4, head_step, 0, unroll=4)
    for h in range(4):
        q_grad[:, h * 64 : h * 64 + 64] = dq_heads[h]
    k_grad[...] = dk_t[...].T
    v_grad[...] = dv_t[...].T
    sums[...] = jnp.zeros_like(sums)
    sums[1:2, 0:256] = column_sum(wide(q_grad[...]))
    sums[2:3, 0:256] = column_sum(wide(v_grad[...]))
    for r in range(4):
        rows = slice(r * 256, r * 256 + 256)
        part = (
            dot_last(q_grad[rows, :], weight[0])
            + dot_last(k_grad[rows, :], weight[1])
            + dot_last(v_grad[rows, :], weight[2])
        )
        sums[0:1, :] += column_sum(inside_column(place, r) * part)
        if r % 2:
            sent[r // 2] = low(part)
        else:
            kept[r // 2] = part


def attend_back(place, query, key, value, lse, weight, grads):
    square = struct((1024, 256))
    return pl.pallas_call(
        attend_back_kernel,
        out_shape=(
            square, square, square, struct((2, 256, D), jnp.float32), struct((2, 256, D)),
            struct((8, D), jnp.float32),
        ),
        in_specs=[SMEM] + [VMEM] * 9,
        out_specs=(VMEM,) * 6,
        scratch_shapes=[pltpu.VMEM((4, 1024, 64), jnp.bfloat16)] * 3
        + [pltpu.VMEM((256, 1024), jnp.bfloat16)] * 4
        + [pltpu.VMEM((4, 1024, 64), jnp.bfloat16)]
        + [pltpu.VMEM((256, 1024), jnp.bfloat16)] * 2,
        compiler_params=pltpu.CompilerParams(vmem_limit_bytes=40 << 20),
        cost_estimate=pl.CostEstimate(
            flops=20_000_000_000, bytes_accessed=12_000_000, transcendentals=4_194_304
        ),
        name="attend_back",
    )(place, query, key, value, lse, weight, *grads)


def row_mean(values):
    return jnp.sum(values, axis=1, keepdims=True) * (1.0 / D)


def normalise(resid):
    centred = resid - row_mean(resid)
    scale = lax.rsqrt(row_mean(centred * centred) + NORM_EPS)
    return centred * scale, scale


def normalise_back(grad, gain, xhat, scale):
    scaled = grad * gain
    return (scaled - row_mean(scaled) - xhat * row_mean(scaled * xhat)) * scale


def target_piece(targets, k, ry, rx):
    return targets[k - 1].at[ry, rx] if k == 1 else targets[k - 1].at[rx, ry]


def layer_kernel(
    place, h0, h1, h2, h3, tokens, cotangent, embed, vectors, bias_up, out_head, *refs
):
    stack = refs[15]
    pieces = (refs[:15], [stack.at[n] for n in range(9)] + list(refs[16:22]))
    refs = refs[22:]
    (block_out, resid_grad, g0, g1, g2, g3, sums, sums_up, head_grad) = refs[:9]
    grads_own, grads_other = refs[9:12], refs[12:15]
    (w_out, w_up, w_down, edge_up, edge_down, hidden, slope, grad_up, grad_down,
     grad_out, acc, acc_t, grad_t, sem, sem_out) = refs[15:]

    def fetch(z, y):
        made = {"out": [], "up": [], "down": []}
        for k in range(1, 4):
            for ry in range(2):
                case = 2 * k + (y ^ ry)
                for r in range(4):
                    rx, rc = r // 2, r % 2
                    source = pieces[rc][BUFFER[z][rx * 8 + ry * 4 + SLOT[z][k]]]
                    column = place[3] ^ r
                    for name, row_a, row_b, offset, step, _ in SEGMENTS[case]:
                        count = row_b - row_a
                        if name == "o":
                            made["out"].append(
                                (source.at[offset : offset + count, :], w_out.at[:, pl.ds(column * 256, 256)])
                            )
                        elif name == "up":
                            block = source.at[offset : offset + 4 * count, :].reshape(4, count, 256)
                            target = w_up.at[pl.ds(column * 4, 4)]
                            skip = 0
                            if row_a:
                                skip = 16
                                made["up"].append(
                                    (block.at[:, 0:16, :], edge_up.at[case - 3, pl.ds(column * 4, 4)])
                                )
                            made["up"].append(
                                (block.at[:, skip:count, :], target.at[:, row_a + skip : row_b, :])
                            )
                        elif name == "down":
                            skip = 0
                            if row_a:
                                skip = 16
                                made["down"].append(
                                    (source.at[offset : offset + 16, :], edge_down.at[case - 6, :, pl.ds(column * 256, 256)])
                                )
                            made["down"].append(
                                (source.at[offset + skip : offset + count, :],
                                 w_down.at[row_a + skip : row_b, pl.ds(column * 256, 256)])
                            )
        return made

    order = ("out", "up", "down")
    for z in range(4):
        for y in range(2):

            @pl.when((place[1] == z) & (place[2] == y))
            def _(z=z, y=y):
                made = fetch(z, y)
                for n, name in enumerate(order):
                    for source, target in made[name]:
                        pltpu.make_async_copy(source, target, sem.at[n]).start()

    def arrived(refs, n):
        for ref in refs:
            pltpu.make_async_copy(ref, ref, sem.at[n]).wait()

    here = inside_column(place, 0)
    stream = wide(tokens[...]) + here * embed[...]
    arrived([w_out], 0)
    for n in range(4):
        cols = slice(n * 256, n * 256 + 256)
        w_out[0:16, cols] = w_out[0:16, cols] + out_head[n]
    heads = (h0, h1, h2, h3)

    def head_rows(r):
        return pl.ds(pl.multiple_of((place[3] ^ r) * 256, 256), 256)

    acc[...] = sum(dot(heads[r][...], w_out[head_rows(r), :]) for r in range(4))
    bias_out, bias_down, gain_a, shift_a, gain_f, shift_f = (vectors[n : n + 1, :] for n in range(6))
    xhat_a, scale_a = normalise(stream + acc[...] + bias_out)
    normed = xhat_a * gain_a + shift_a
    normed_low = low(normed)

    arrived([w_up] + [edge_up], 1)
    for n, row in enumerate((128, 512, 896)):
        w_up[:, row : row + 16, :] = w_up[:, row : row + 16, :] + edge_up[n]

    def up(g, _):
        pre = dot(normed_low, w_up[g]) + bias_up[pl.ds(g, 1), :]
        inner = 0.5 * (1.0 + lax.erf(pre * (1.0 / math.sqrt(2.0))))
        hidden[:, pl.ds(pl.multiple_of(g * 256, 256), 256)] = low(pre * inner)
        bend = inner + pre * (jnp.exp(-0.5 * pre * pre) * (1.0 / math.sqrt(2.0 * math.pi)))
        slope[pl.ds(pl.multiple_of(g * 256, 256), 256), :] = bend.T
        return 0

    lax.fori_loop(0, 16, up, 0, unroll=8)
    arrived([w_down] + [edge_down], 2)
    for n, row in enumerate((1024, 2560)):
        w_down[row : row + 16, :] = w_down[row : row + 16, :] + edge_down[n]
    acc[...] = normed + bias_down + dot(hidden[...], w_down[...])
    xhat_f, scale_f = normalise(acc[...])
    block_out[...] = low(xhat_f * gain_f + shift_f)

    out_grad = wide(cotangent[...])
    sums[4:5, :] = column_sum(out_grad * xhat_f)
    sums[5:6, :] = column_sum(out_grad)
    acc[...] = normalise_back(out_grad, gain_f, xhat_f, scale_f)
    ffn_grad = low(acc[...])
    sums[1:2, :] = column_sum(wide(ffn_grad))
    grad_t[...] = ffn_grad.T
    normed_t = normed_low.T

    def routes(case, name):
        return [
            (row_a, row_b, offset, row_b - row_a)
            for seg, row_a, row_b, offset, _, _ in SEGMENTS[case]
            if seg == name
        ]

    def outputs_up(case, column, targets, rx):
        piece = target_piece(targets, case // 2, place[2] ^ (case % 2), rx)
        return [
            pltpu.make_async_copy(
                grad_up.at[column * 4 : column * 4 + 4, row_a:row_b, :],
                piece.at[offset : offset + 4 * count, :].reshape(4, count, 256),
                sem_out.at[0],
            )
            for row_a, row_b, offset, count in routes(case, "up")
        ]

    def outputs(case):
        made = []
        for r in range(4):
            rx, rc = r // 2, r % 2
            column = place[3] ^ r
            targets = grads_other if rc else grads_own
            piece = target_piece(targets, case // 2, place[2] ^ (case % 2), rx)
            for row_a, row_b, offset, count in routes(case, "down"):
                source = grad_down.at[row_a:row_b, pl.ds(column * 256, 256)]
                target = piece.at[offset : offset + count, :]
                made.append(pltpu.make_async_copy(source, target, sem_out.at[0]))
        return made

    acc_t[...] = jnp.zeros_like(acc_t)

    for chunk in range(4):
        rows = slice(chunk * 1024, chunk * 1024 + 1024)
        pre_grad_t = low(dot(w_down[rows, :], grad_t[...]) * slope[rows, :])
        pre_grad = pre_grad_t.T
        sums_up[chunk : chunk + 1, :] = column_sum(wide(pre_grad))
        for n in range(4):
            g = chunk * 4 + n
            acc_t[...] += dot(w_up[g], pre_grad_t[n * 256 : n * 256 + 256, :])
            grad_up[g] = low(dot(normed_t, pre_grad[:, n * 256 : n * 256 + 256]))
        grad_down[rows, :] = low(dot_first(hidden[:, rows], ffn_grad))
        relative = place[3] ^ chunk
        for side, targets in enumerate((grads_own, grads_other)):

            @pl.when(relative % 2 == side)
            def _(chunk=chunk, targets=targets, relative=relative):
                for case in range(2, 6):
                    for copy in outputs_up(case, chunk, targets, relative // 2):
                        copy.start()

        for case in {1: (5,), 2: (6,)}.get(chunk, ()):
            for copy in outputs(case):
                copy.start()
    for copy in outputs(7):
        copy.start()
    acc[...] += acc_t[...].T

    normed_grad = acc[...]
    sums[2:3, :] = column_sum(normed_grad * xhat_a)
    sums[3:4, :] = column_sum(normed_grad)
    attn_wide = normalise_back(normed_grad, gain_a, xhat_a, scale_a)
    resid_grad[...] = attn_wide
    sums[6:7, :] = column_sum(here * attn_wide)
    attn_grad = low(attn_wide)
    grad_t[...] = attn_grad.T
    sums[0:1, :] = column_sum(wide(attn_grad))
    sums[7:8, :] = jnp.zeros((1, D), jnp.float32)
    for r, out in enumerate((g0, g1, g2, g3)):
        out[...] = low(dot(w_out[head_rows(r), :], grad_t[...]).T)
        grad_out[head_rows(r), :] = low(dot_first(heads[r][...], attn_grad))
    for n in range(4):
        head_grad[n] = wide(grad_out[0:16, n * 256 : n * 256 + 256])
    last = []
    for r in range(4):
        rx, rc = r // 2, r % 2
        column = place[3] ^ r
        targets = grads_other if rc else grads_own
        piece = target_piece(targets, 1, place[2], rx)
        last.append((grad_out.at[:, pl.ds(column * 256, 256)], piece.at[0:1024, :]))
    for source, target in last:
        pltpu.make_async_copy(source, target, sem_out.at[1]).start()
    for case in range(5, 8):
        for copy in outputs(case):
            copy.wait()
    for column in range(4):
        for case in range(2, 6):
            for copy in outputs_up(case, column, grads_own, 0):
                copy.wait()
    for source, target in last:
        pltpu.make_async_copy(source, target, sem_out.at[1]).wait()


def layer(place, heads, tokens, cotangent, embed, vectors, bias_up, out_head, pieces):
    grads = struct((2, 2, PIECE, 256))
    block = struct((256, 256))
    return pl.pallas_call(
        layer_kernel,
        out_shape=(
            struct((256, D)), struct((256, D), jnp.float32), block, block, block, block,
            struct((8, D), jnp.float32), struct((4, 1024), jnp.float32),
            struct((4, 16, 256), jnp.float32),
        ) + (grads,) * 6,
        in_specs=[SMEM] + [VMEM] * 10 + [ANY] * 22,
        out_specs=(VMEM,) * 9 + (ANY,) * 6,
        scratch_shapes=[
            pltpu.VMEM((D, D), jnp.bfloat16),
            pltpu.VMEM((16, 1024, 256), jnp.bfloat16),
            pltpu.VMEM((FF, D), jnp.bfloat16),
            pltpu.VMEM((3, 16, 16, 256), jnp.bfloat16),
            pltpu.VMEM((2, 16, D), jnp.bfloat16),
            pltpu.VMEM((256, FF), jnp.bfloat16),
            pltpu.VMEM((FF, 256), jnp.float32),
            pltpu.VMEM((16, 1024, 256), jnp.bfloat16),
            pltpu.VMEM((FF, D), jnp.bfloat16),
            pltpu.VMEM((D, D), jnp.bfloat16),
            pltpu.VMEM((256, D), jnp.float32),
            pltpu.VMEM((D, 256), jnp.float32),
            pltpu.VMEM((D, 256), jnp.bfloat16),
            pltpu.SemaphoreType.DMA((3,)),
            pltpu.SemaphoreType.DMA((2,)),
        ],
        compiler_params=pltpu.CompilerParams(vmem_limit_bytes=60 << 20),
        cost_estimate=pl.CostEstimate(
            flops=15_000_000_000, bytes_accessed=40_000_000, transcendentals=2_097_152
        ),
        name="layer",
    )(place, *heads, tokens, cotangent, embed, vectors, bias_up, out_head, *pieces)


def product(left, right):
    return jnp.dot(left, right, preferred_element_type=jnp.float32)


def product_inner(left, right):
    return lax.dot_general(
        left, right, (((0,), (0,)), ((), ())), preferred_element_type=jnp.float32
    )


def layer_norm(resid, gain, shift):
    average = jnp.mean(resid, axis=-1, keepdims=True)
    centred = resid - average
    variance = jnp.mean(centred * centred, axis=-1, keepdims=True)
    return centred * lax.rsqrt(variance + NORM_EPS) * gain + shift


def unpack_all(flat_params, dp_count, fsdp_count):
    shapes = [(D, D)] * 4 + [(D, FF), (FF, D)] + [(1, D)] * 4 + [(1, FF)] + [(1, D)] * 6
    blocks = (
        flat_params.reshape(dp_count, fsdp_count, -1).transpose(1, 0, 2).reshape(fsdp_count, -1)
    )
    pieces = []
    offset = 0
    for rows, cols in shapes:
        width = rows * (cols // fsdp_count)
        part = blocks[:, offset : offset + width].reshape(fsdp_count, rows, cols // fsdp_count)
        whole = part.transpose(1, 0, 2).reshape(rows, cols)
        pieces.append(whole.reshape(-1) if rows == 1 else whole)
        offset += width
    return pieces


def split_heads(values):
    return values.reshape(values.shape[0], H, DH).transpose(1, 0, 2)


def merge_heads(values):
    return values.transpose(1, 0, 2).reshape(values.shape[1], H * DH)


def head_forward(head_item):
    query_h, key_h, value_h = head_item
    scores = product(query_h, key_h.T) * DH ** (-0.5)
    highest = jnp.max(scores, axis=1, keepdims=True)
    weights = jnp.exp(scores - highest)
    totals = jnp.sum(weights, axis=1, keepdims=True)
    probabilities = weights / totals
    result = product(probabilities.astype(jnp.bfloat16), value_h)
    return (result, (highest + jnp.log(totals))[:, 0])


def head_query_back(head_item):
    query_h, key_h, value_h, grad_h, logsum = head_item
    score_scale = DH ** (-0.5)
    scores = product(query_h, key_h.T) * score_scale
    probabilities = jnp.exp(scores - logsum[:, None])
    prob_grad = product(grad_h, value_h.T)
    inner_sum = jnp.sum(probabilities * prob_grad, axis=1)
    score_grad = (probabilities * (prob_grad - inner_sum[:, None])).astype(jnp.bfloat16)
    query_grad = product(score_grad, key_h) * score_scale
    return (query_grad, inner_sum)


def head_key_back(head_item):
    key_h, value_h, query_all, grad_all, logsum_all, inner_all = head_item
    score_scale = DH ** (-0.5)
    scores_t = product(key_h, query_all.T) * score_scale
    probs_t = jnp.exp(scores_t - logsum_all[None, :])
    prob_grad_t = product(value_h, grad_all.T)
    score_grad_t = (probs_t * (prob_grad_t - inner_all[None, :])).astype(jnp.bfloat16)
    key_grad = product(score_grad_t, query_all) * score_scale
    value_grad = product(probs_t.astype(jnp.bfloat16), grad_all)
    return (key_grad, value_grad)


def body(
    tokens,
    cotangent,
    master,
    first_moment,
    second_moment,
    average,
    timestep,
    block_length,
    block_start,
):
    dp_count = lax.axis_size("dp")
    fsdp_count = lax.axis_size("fsdp")
    master_low = master.astype(jnp.bfloat16)
    flat_params = lax.all_gather(master_low, ("dp", "fsdp"), axis=0, tiled=True)
    (
        w_query,
        w_key,
        w_value,
        w_out,
        w_up,
        w_down,
        b_query,
        b_value,
        b_out,
        b_down,
        b_up,
        gain_attn,
        shift_attn,
        gain_ffn,
        shift_ffn,
        w_time,
        b_time,
    ) = unpack_all(flat_params, dp_count, fsdp_count)
    gain_a = gain_attn.astype(jnp.float32)
    shift_a = shift_attn.astype(jnp.float32)
    gain_f = gain_ffn.astype(jnp.float32)
    shift_f = shift_ffn.astype(jnp.float32)
    row_count = tokens.shape[0]
    position = lax.axis_index("fsdp") * row_count + jnp.arange(row_count, dtype=jnp.int32)
    block_first = block_start[0]
    inside = ((position >= block_first) & (position < block_first + block_length[0])).astype(
        jnp.float32
    )[:, None]
    time_frac = timestep[0].astype(jnp.float32) / 5000.0
    time_embed = time_frac * w_time.astype(jnp.float32) + b_time.astype(jnp.float32)
    stream = tokens.astype(jnp.float32) + inside * time_embed
    stream_low = stream.astype(jnp.bfloat16)
    queries = (product(stream_low, w_query) + b_query.astype(jnp.float32)).astype(jnp.bfloat16)
    keys_local = product(stream_low, w_key).astype(jnp.bfloat16)
    values_local = (product(stream_low, w_value) + b_value.astype(jnp.float32)).astype(jnp.bfloat16)
    keys_all, values_all = (
        lax.all_gather(keys_local, "fsdp", axis=0, tiled=True),
        lax.all_gather(values_local, "fsdp", axis=0, tiled=True),
    )
    query_heads = split_heads(queries)
    key_heads = split_heads(keys_all)
    value_heads = split_heads(values_all)
    head_out, logsum = lax.map(head_forward, (query_heads, key_heads, value_heads))
    heads_low = merge_heads(head_out).astype(jnp.bfloat16)
    resid_attn = stream + product(heads_low, w_out) + b_out.astype(jnp.float32)
    normed = layer_norm(resid_attn, gain_a, shift_a)
    normed_low = normed.astype(jnp.bfloat16)
    pre_act = product(normed_low, w_up) + b_up.astype(jnp.float32)
    hidden = jax.nn.gelu(pre_act, approximate=False).astype(jnp.bfloat16)
    resid_ffn = normed + product(hidden, w_down) + b_down.astype(jnp.float32)
    block_out = layer_norm(resid_ffn, gain_f, shift_f).astype(jnp.bfloat16)
    stream_all, heads_all, normed_all, hidden_all = (
        lax.all_gather(stream_low, "fsdp", axis=0, tiled=True),
        lax.all_gather(heads_low, "fsdp", axis=0, tiled=True),
        lax.all_gather(normed_low, "fsdp", axis=0, tiled=True),
        lax.all_gather(hidden, "fsdp", axis=0, tiled=True),
    )
    back_params = lax.all_gather(master_low, ("dp", "fsdp"), axis=0, tiled=True)
    back_pieces = unpack_all(back_params, dp_count, fsdp_count)
    w_query_back, w_key_back, w_value_back, w_out_back, w_up_back, w_down_back = back_pieces[:6]
    out_grad = cotangent.astype(jnp.float32)
    _, pull_ffn = jax.vjp(layer_norm, resid_ffn, gain_f, shift_f)
    resid_ffn_grad, grad_gain_ffn, grad_shift_ffn = pull_ffn(out_grad)
    ffn_grad = resid_ffn_grad.astype(jnp.bfloat16)
    hidden_grad = product(ffn_grad, w_down_back.T)
    _, pull_gelu = jax.vjp(partial(jax.nn.gelu, approximate=False), pre_act)
    pre_grad = pull_gelu(hidden_grad)[0].astype(jnp.bfloat16)
    normed_grad = resid_ffn_grad + product(pre_grad, w_up_back.T)
    _, pull_attn = jax.vjp(layer_norm, resid_attn, gain_a, shift_a)
    resid_attn_grad, grad_gain_attn, grad_shift_attn = pull_attn(normed_grad)
    attn_grad = resid_attn_grad.astype(jnp.bfloat16)
    heads_grad = product(attn_grad, w_out_back.T).astype(jnp.bfloat16)
    query_parts, inner_sum = lax.map(
        head_query_back, (query_heads, key_heads, value_heads, split_heads(heads_grad), logsum)
    )
    query_grad = merge_heads(query_parts).astype(jnp.bfloat16)
    queries_all, heads_grad_all = (
        lax.all_gather(queries, "fsdp", axis=0, tiled=True),
        lax.all_gather(heads_grad, "fsdp", axis=0, tiled=True),
    )
    logsum_all, inner_all = (
        lax.all_gather(logsum, "fsdp", axis=1, tiled=True),
        lax.all_gather(inner_sum, "fsdp", axis=1, tiled=True),
    )
    key_parts, value_parts = lax.map(
        head_key_back,
        (
            split_heads(keys_local),
            split_heads(values_local),
            split_heads(queries_all),
            split_heads(heads_grad_all),
            logsum_all,
            inner_all,
        ),
    )
    key_grad = merge_heads(key_parts).astype(jnp.bfloat16)
    value_grad = merge_heads(value_parts).astype(jnp.bfloat16)
    stream_grad = (
        resid_attn_grad
        + product(query_grad, w_query_back.T)
        + product(key_grad, w_key_back.T)
        + product(value_grad, w_value_back.T)
    )
    grad_b_time = jnp.sum(inside * stream_grad, axis=0)
    grad_w_time = time_frac * grad_b_time
    query_cols, key_cols, value_cols, attn_cols, ffn_cols, pre_cols = (
        lax.all_to_all(query_grad, "fsdp", split_axis=1, concat_axis=0, tiled=True),
        lax.all_to_all(key_grad, "fsdp", split_axis=1, concat_axis=0, tiled=True),
        lax.all_to_all(value_grad, "fsdp", split_axis=1, concat_axis=0, tiled=True),
        lax.all_to_all(attn_grad, "fsdp", split_axis=1, concat_axis=0, tiled=True),
        lax.all_to_all(ffn_grad, "fsdp", split_axis=1, concat_axis=0, tiled=True),
        lax.all_to_all(pre_grad, "fsdp", split_axis=1, concat_axis=0, tiled=True),
    )
    grad_w_query = product_inner(stream_all, query_cols)
    grad_w_key = product_inner(stream_all, key_cols)
    grad_w_value = product_inner(stream_all, value_cols)
    grad_w_out = product_inner(heads_all, attn_cols)
    grad_w_up = product_inner(normed_all, pre_cols)
    grad_w_down = product_inner(hidden_all, ffn_cols)
    grad_b_query = jnp.sum(query_cols.astype(jnp.float32), axis=0)
    grad_b_value = jnp.sum(value_cols.astype(jnp.float32), axis=0)
    grad_b_out = jnp.sum(attn_cols.astype(jnp.float32), axis=0)
    grad_b_down = jnp.sum(ffn_cols.astype(jnp.float32), axis=0)
    grad_b_up = jnp.sum(pre_cols.astype(jnp.float32), axis=0)
    vector_terms = jnp.stack(
        [grad_gain_attn, grad_shift_attn, grad_gain_ffn, grad_shift_ffn, grad_w_time, grad_b_time]
    )
    vector_part = lax.psum_scatter(vector_terms, "fsdp", scatter_dimension=1, tiled=True)
    vector_block = jnp.concatenate(
        [grad_b_query, grad_b_value, grad_b_out, grad_b_down, grad_b_up, vector_part.reshape(-1)]
    )
    grad_block = jnp.concatenate(
        [
            piece.reshape(-1)
            for piece in (
                grad_w_query,
                grad_w_key,
                grad_w_value,
                grad_w_out,
                grad_w_up,
                grad_w_down,
            )
        ]
        + [vector_block]
    )
    grad_shard = lax.psum_scatter(grad_block, "dp", scatter_dimension=0, tiled=True)
    vector_grad = lax.psum(vector_block, "dp")
    square_sum = lax.psum(jnp.sum(grad_shard * grad_shard), ("dp", "fsdp"))
    grad_norm = jnp.sqrt(square_sum)
    clip_limit = 4.0 * math.sqrt(PARAMS)
    clipped = grad_shard * (clip_limit / jnp.maximum(grad_norm, clip_limit))
    new_first = 0.9 * first_moment + 0.1 * clipped
    new_second = 0.98 * second_moment + 0.02 * clipped * clipped
    first_hat = new_first / (1.0 - 0.9**STEP)
    second_hat = new_second / (1.0 - 0.98**STEP)
    new_master = master - 0.02 * (first_hat / (jnp.sqrt(second_hat) + 1e-06) + 0.01 * master)
    new_average = 0.99 * average + 0.01 * new_master
    return (
        block_out,
        stream_grad,
        grad_norm,
        vector_grad,
        new_first,
        new_second,
        new_master,
        new_average,
    )


AXES = ("dp", "fsdp")


def send(values, route, name="move"):
    pairs = []
    for n in range(32):
        there = route(n // 8, n // 4 % 2, n // 2 % 2, n % 2)
        if there is not None:
            z, y, x, c = there
            pairs.append((n, z * 8 + y * 4 + x * 2 + c))
    with jax.named_scope(name):
        return lax.ppermute(values, AXES, pairs)


def to_core(z, y, x, c):
    return z, y, x, 1 - c


def to_x(z, y, x, c):
    return z, y, 1 - x, c


def to_y(z, y, x, c):
    return z, 1 - y, x, c


def to_near(z, y, x, c):
    return z ^ 1, y, x, c


def to_far(z, y, x, c):
    return z ^ 2, y, x, c


def only(route, planes):
    return lambda z, y, x, c: route(z, y, x, c) if z in planes else None


def to_opposite(z, y, x, c):
    return 3 - z, y, x, c


def to_relative(r):
    return lambda z, y, x, c: (z, y, x ^ (r // 2), c ^ (r % 2))


def exchange(blocks, name):
    return [blocks[0]] + [send(blocks[r], to_relative(r), name) for r in range(1, 4)]


def after(values, *earlier):
    return lax.optimization_barrier((values, *earlier))[0]


def together(values, routes, *beside):
    near, far, both = (send(values, route, "norm") for route in routes)
    return (values + near) + (far + after(both, *beside))


PLANES = ((1, 2, 3), (0, 1, 3), (0, 2), (0, 1, 2, 3))


def gather_pieces(own, z, y, tokens, run_attend):
    def across(name, values, n):
        return send(values, only(to_x, PLANES[n]), name)

    outer = (z == 0) | (z == 3)
    first = send(own, lambda z, y, x, c: ((2, 0, 3, 1)[z], y, x, c), "first")
    y0 = send(own, to_y, "y0")
    tokens_x = send(tokens, to_x, "tok_x")
    x0 = across("x0", own, 0)
    tokens_c = send(tokens, to_core, "tok_c")
    second = send(after(jnp.where(outer, own, first), tokens_x), to_near, "second")
    crossed = send(
        after(own, first), lambda z, y, x, c: (3 - z, y, x, c) if z in (1, 2) else None, "crossed"
    )
    y1 = send(after(first, y0), to_y, "y1")
    x1 = across("x1", after(first, x0), 1)
    third = send(after(crossed, second), only(to_near, (1, 2)), "third")
    y2 = send(after(second, y1), to_y, "y2")
    x_a = send(jnp.where(z % 2 == 0, second, y0), to_x, "xa")
    last = jnp.where(outer, third, crossed)
    tokens_xc = send(after(tokens_x, third), to_core, "tok_xc")
    y3 = send(after(last, y2), to_y, "y3")
    y_b = send(after(jnp.where(z == 2, x0, x1), y2), to_y, "yb")
    yx2 = across("yx2", after(y2, last), 2)
    x3 = across("x3", after(last, y2), 3)
    tail_0, tail_1, tail_2 = (
        jnp.where(y == 1, mine[TAIL:], other[TAIL:])
        for mine, other in ((own, y0), (first, y1), (second, y2))
    )
    attended = run_attend(
        after(last, y2), (own, y0, first, y1, second, y2, last, x0, x1),
        (tokens, tokens_c, tokens_x, tokens_xc),
        jnp.where(z == 3, tail_0, jnp.where(z == 1, tail_1, tail_2)),
        jnp.where(z == 0, tail_0, jnp.where(z == 2, tail_1, tail_2)),
    )
    attended = lax.optimization_barrier((*attended, x_a, y3, yx2, x3, y_b))[: len(attended)]
    stack = send(attended[-1], to_core, "stack")
    heads = exchange(attended[5:9], "heads")
    yx3 = across("yx3", after(y3, x3, attended[-1]), 3)
    later = [
        send(after(piece, attended[-1]), only(to_core, planes), name)
        for piece, planes, name in (
            (x_a, (0, 1, 2, 3), "cxa"), (y3, (0, 1, 2, 3), "cy3"), (y_b, (0, 1, 2, 3), "cyb"),
            (yx2, PLANES[2], "cyx2"), (x3, (0, 1, 2, 3), "cx3"), (yx3, (0, 1, 2, 3), "cyx3"),
        )
    ]
    mine = [own, first, second, last, y0, y1, y2, x0, x1, x_a, y3, y_b, yx2, x3, yx3]
    return attended[:5], heads, attended[9], [*mine, stack, *later]


def add(left, right):
    return wide(left) + wide(right)


def block_body(
    tokens,
    cotangent,
    master,
    first_moment,
    second_moment,
    average,
    timestep,
    block_length,
    block_start,
):
    shard = lax.axis_index("dp")
    j = lax.axis_index("fsdp")
    z, y = shard // 2, shard % 2
    place = jnp.stack([shard, z, y, j, block_start[0], block_length[0]]).astype(jnp.int32)
    flat = jnp.pad(master, (0, LANE_ROWS * 128 - SHARD)).reshape(LANE_ROWS, 128)
    vec_rows = jnp.pad(master[SHARD - 3584 :].reshape(14, 256), ((0, 2), (0, 0)))
    head_rows = jnp.pad(master[SHARD - 896 :], (0, 3200)).reshape(16, 256)
    tail = low(jnp.where(shard == 7, vec_rows, head_rows))
    tail_x = after(send(tail, to_x, "tail_x"), flat)
    tail_c = send(jnp.concatenate([tail, tail_x]), to_core, "tail_c")
    own = pack(place, flat, jnp.concatenate([tail, tail_c[:16], tail_x, tail_c[16:]]))
    here = (jnp.arange(4) == j)[:, None, None]
    time_frac = timestep[0].astype(jnp.float32) / 5000.0
    vectors = {}

    def absolute(relative):
        blocks = relative.reshape(4, 16, 256)
        blocks = jnp.where(j % 2 == 1, jnp.concatenate([blocks[1:2], blocks[0:1], blocks[3:4], blocks[2:3]]), blocks)
        return jnp.where(j // 2 == 1, jnp.concatenate([blocks[2:4], blocks[0:2]]), blocks)

    def run_attend(ready, held, all_tokens, vec_tail, head_tail):
        vec = wide(absolute(vec_tail))
        full = vec.transpose(1, 0, 2).reshape(16, D)
        vec_own = wide(vec_tail[:16])
        vectors["embed"] = time_frac * full[12:13] + full[13:14]
        vectors["rows"] = jnp.concatenate([full[2:4], full[8:12], jnp.zeros((2, D), jnp.float32)])
        vectors["up"] = vec[:, 4:8].reshape(16, 256)
        vectors["head"] = absolute(head_tail)
        return attend(after(place, ready), all_tokens, vectors["embed"], vec_own[0:8], held)

    attended, heads, lse, pieces = gather_pieces(own, z, y, tokens, run_attend)
    stream, weight, query, key, value = attended

    (block_out, resid_grad, g0, g1, g2, g3, sums, sums_up, head_grad, *grads) = layer(
        place, heads, tokens, cotangent, vectors["embed"],
        vectors["rows"], vectors["up"], vectors["head"], pieces,
    )
    grads_own, grads_other = grads[:3], grads[3:]

    moved = {k: send(grads_other[k - 1], to_core, f"rc{k}") for k in (2, 1)}
    moved[3] = send(after(grads_other[2], moved[2], moved[1]), to_core, "rc3")

    def over_cores(k, a, b):
        return add(grads_own[k - 1][a, b], moved[k][a, b])

    grad_heads = exchange((g0, g1, g2, g3), "heads_grad")
    starts = {
        name: after(low(over_cores(k, 1, b)), *grad_heads)
        for name, k, b in (("d1", 1, 1), ("d2", 2, 1), ("e1", 1, 0), ("e2", 2, 0))
    }
    d1 = send(starts["d1"], to_y, "d1")
    d2 = send(starts["d2"], to_x, "d2")
    e1 = send(starts["e1"], to_y, "e1")
    e2 = send(starts["e2"], to_x, "e2")

    (q_grad, k_grad, v_grad, kept, sent, sums_qkv) = attend_back(
        after(place, *starts.values()),
        query, key, value, lse, weight, grad_heads,
    )

    q_grad, k_grad, v_grad, kept, sent, sums_qkv, d1, d2 = lax.optimization_barrier(
        (q_grad, k_grad, v_grad, kept, sent, sums_qkv, d1, d2)
    )
    sum_1 = low(over_cores(1, 0, 1) + wide(d1))
    sum_2 = low(over_cores(2, 0, 1) + wide(d2))
    sum_3 = low(over_cores(3, 1, 1))
    sum_1, sum_2, sum_3, e1, e2, sent = lax.optimization_barrier(
        (sum_1, sum_2, sum_3, e1, e2, sent)
    )
    from_core = send(sent, to_core, "in_c")
    f1 = send(sum_1, to_x, "f1")
    f2 = send(sum_2, to_y, "f2")
    q_grad, k_grad, v_grad, sum_3, from_core = lax.optimization_barrier(
        (q_grad, k_grad, v_grad, sum_3, from_core)
    )
    d3 = send(sum_3, to_x, "d3")
    e3 = send(after(low(over_cores(3, 1, 0)), f1), to_x, "e3")

    rows = stream.reshape(1024, D)
    w_grads = [low(product_inner(rows, grad)) for grad in (q_grad, k_grad, v_grad)]
    rest = jnp.zeros((PIECE - 1552, 256), jnp.bfloat16)
    piece_0 = jnp.concatenate([w_grads[0], w_grads[1][:528], rest])
    piece_1 = jnp.concatenate([w_grads[1][512:], w_grads[2], rest, rest[:16]])
    low_row = y == 0
    other_row = jnp.where(low_row, piece_1, piece_0)
    ry0 = send(other_row, to_y, "ry0")
    kept_1, sent_1 = combine(
        after(place, other_row, sum_3), (grads_own[1], moved[2], e2, f2), (grads_own[0], moved[1], e1, f1)
    )
    got_inner = send(sent_1, to_near, "rz_inner1")
    inner_part = low(add(kept_1, got_inner))
    inner_last = send(inner_part, only(to_far, (0, 3)), "rz_inner2")
    f3 = send(low(over_cores(3, 0, 1) + wide(after(d3, ry0))), to_y, "f3")
    kept_0, sent_0 = combine(
        after(place, inner_part), (jnp.where(low_row, piece_0, piece_1), ry0), (grads_own[2], moved[3], e3, f3)
    )
    outer_part = low(add(kept_0, send(after(sent_0, inner_last), to_near, "rz_outer1")))
    outer_last = send(outer_part, only(to_far, (1, 2)), "rz_outer2")

    in_x = send(after(low(kept[1] + wide(from_core[1])), e3), to_x, "in_x")
    input_grad = (
        resid_grad
        + kept[0]
        + wide(from_core[0])
        + wide(in_x)
    )

    time_grad = sums[6] + sums_qkv[0]
    rows_of = [sums[0], sums[1]]
    vec_grad = jnp.concatenate(
        [
            jnp.where(here, sums_qkv[1:3, :256][None], 0.0),
            sums[0:2].reshape(2, 4, 256).transpose(1, 0, 2),
            sums_up.reshape(4, 4, 256),
            sums[2:6].reshape(4, 4, 256).transpose(1, 0, 2),
            (time_frac * time_grad).reshape(4, 1, 256),
            time_grad.reshape(4, 1, 256),
            jnp.zeros((4, 2, 256), jnp.float32),
            jnp.where(jnp.arange(4096).reshape(1, 16, 256) < 896, head_grad, 0.0),
        ],
        axis=1,
    )
    vec_grad = vec_grad.reshape(2, 2, 32, 256)
    core_bit, x_bit = j % 2, j // 2
    kept_c = jnp.where(core_bit == 1, vec_grad[:, 1], vec_grad[:, 0])
    sent_c = jnp.where(core_bit == 1, vec_grad[:, 0], vec_grad[:, 1])
    by_x = kept_c + send(sent_c, to_core, "vec_c")
    kept_x = jnp.where(x_bit == 1, by_x[1], by_x[0])
    mine = kept_x + send(jnp.where(x_bit == 1, by_x[0], by_x[1]), to_x, "vec_x")

    grad_flat, square = unpack(after(place, input_grad), inner_part, inner_last, outer_part, outer_last)
    mine = jnp.concatenate([mine, square])
    mine = mine + send(mine, to_y, "norm")
    mine = together(mine, (to_near, to_far, to_opposite))
    vec_sum, head_sum = mine[:14].reshape(-1), mine[16:20].reshape(-1)[:896]
    vector_grad = vec_sum
    is_sum = jnp.arange(40)[:, None] >= 32
    square_sum = jnp.sum(jnp.where(is_sum, mine, mine * mine))
    square_sum = jnp.broadcast_to(square_sum, (8, 128))
    grad_flat = grad_flat.reshape(-1)
    edge = grad_flat[SHARD - 3584 : SHARD]
    edge = jnp.where(
        shard == 7,
        vec_sum,
        jnp.where(shard == 1, jnp.concatenate([edge[: 3584 - 896], head_sum]), edge),
    )
    grad_shard = lax.dynamic_update_slice(grad_flat, edge, (SHARD - 3584,))
    square_sum = together(square_sum, (to_core, to_x, to_relative(3)), grad_shard)
    grad_shard = grad_shard[:SHARD]
    grad_norm = jnp.sqrt(square_sum[0, 0])
    clip_limit = 4.0 * math.sqrt(PARAMS)
    clipped = grad_shard * (clip_limit / jnp.maximum(grad_norm, clip_limit))
    new_first = 0.9 * first_moment + 0.1 * clipped
    new_second = 0.98 * second_moment + 0.02 * clipped * clipped
    first_hat = new_first / (1.0 - 0.9**STEP)
    second_hat = new_second / (1.0 - 0.98**STEP)
    new_master = master - 0.02 * (first_hat / (jnp.sqrt(second_hat) + 1e-06) + 0.01 * master)
    new_average = 0.99 * average + 0.01 * new_master
    return (
        block_out,
        input_grad,
        grad_norm,
        vector_grad,
        new_first,
        new_second,
        new_master,
        new_average,
    )


def solution(mesh):
    return jax.shard_map(
        block_body if mesh.shape["dp"] == 8 and mesh.shape["fsdp"] == 4 else body,
        mesh=mesh,
        in_specs=(
            P(("dp", "fsdp"), None),
            P(("dp", "fsdp"), None),
            P(("dp", "fsdp")),
            P(("dp", "fsdp")),
            P(("dp", "fsdp")),
            P(("dp", "fsdp")),
            P("dp"),
            P("dp"),
            P("dp"),
        ),
        out_specs=(
            P(("dp", "fsdp"), None),
            P(("dp", "fsdp"), None),
            P(),
            P("fsdp"),
            P(("dp", "fsdp")),
            P(("dp", "fsdp")),
            P(("dp", "fsdp")),
            P(("dp", "fsdp")),
        ),
        check_vma=False,
    )
```

```python
from functools import partial
import math

import jax
import jax.numpy as jnp
from jax import lax
from jax.experimental import pallas as pl
from jax.experimental.pallas import tpu as pltpu
from jax.sharding import PartitionSpec as P

D = 1024
H = 16
DH = 64
FF = 4096
STEP = 10
PARAMS = 12597248
NORM_EPS = 1e-05

SHARD = PARAMS // 32
PIECE = 1600
LANE_ROWS = 3080
PAD = 128
TAIL = 1536
REGIONS = (
    ("q", 0, 1024, 256),
    ("k", 262144, 1024, 256),
    ("v", 524288, 1024, 256),
    ("o", 786432, 1024, 256),
    ("up", 1048576, 1024, 1024),
    ("down", 2097152, 4096, 256),
    ("vec", 3145728, 16, 256),
)


def segments(shard):
    low, high = shard * SHARD, (shard + 1) * SHARD
    found, offset = [], 0
    for name, start, rows, width in REGIONS:
        size = 3584 if name == "vec" else rows * width
        first, last = max(low, start), min(high, start + size)
        if first >= last:
            continue
        row_a = (first - start) // width // 16 * 16
        row_b = min(rows, -(-(-(-(last - start) // width)) // 16) * 16)
        found.append((name, row_a, row_b, offset, width // 128, start // 128))
        offset += (row_b - row_a) * (width // 256)
    return found


def lane_start(shard):
    return shard * SHARD // 128


SEGMENTS = [segments(shard) for shard in range(8)]
SLOT = ((0, 1, 3, 2), (2, 0, 3, 1), (1, 3, 0, 2), (2, 3, 1, 0))


def buffers(z):
    x_a, y_b = 9, 11
    over_x = [7, 8, x_a, 13]
    both = [y_b if z == 2 else x_a, y_b, 12, 14]
    return [0, 1, 2, 3, 4, 5, 6, 10, *over_x, *both]


BUFFER = [buffers(z) for z in range(4)]


def dot(left, right):
    return jnp.dot(left, right, preferred_element_type=jnp.float32)


def dot_last(left, right):
    return lax.dot_general(
        left, right, (((1,), (1,)), ((), ())), preferred_element_type=jnp.float32
    )


def dot_first(left, right):
    return lax.dot_general(
        left, right, (((0,), (0,)), ((), ())), preferred_element_type=jnp.float32
    )


def low(values):
    return values.astype(jnp.bfloat16)


def wide(values):
    return values.astype(jnp.float32)


VMEM = pl.BlockSpec(memory_space=pltpu.VMEM)
SMEM = pl.BlockSpec(memory_space=pltpu.SMEM)
ANY = pl.BlockSpec(memory_space=pl.ANY)


def struct(shape, kind=jnp.bfloat16):
    return jax.ShapeDtypeStruct(shape, kind)


def chunks(rows, most=128):
    return [(a, min(most, rows - a)) for a in range(0, rows, most)]


def pack_kernel(place, flat, tails, piece, rolled, rows):
    shard = place[0]
    rows[0:PAD, :] = jnp.zeros((PAD, 128), jnp.float32)
    rows[PAD + LANE_ROWS : PAD + LANE_ROWS + PAD, :] = jnp.zeros((PAD, 128), jnp.float32)
    rolled[0:8, :] = jnp.zeros((8, 128), jnp.float32)

    @pl.when(shard % 2 == 0)
    def _():
        for a, n in chunks(LANE_ROWS):
            rows[PAD + a : PAD + a + n, :] = flat[a : a + n, :]

    @pl.when(shard % 2 == 1)
    def _():
        for a, n in chunks(LANE_ROWS):
            rolled[8 + a : 8 + a + n, :] = pltpu.roll(flat[a : a + n, :], 64, 1)
        for a, n in chunks(LANE_ROWS):
            lane = lax.broadcasted_iota(jnp.int32, (n, 128), 1)
            rows[PAD + a : PAD + a + n, :] = jnp.where(
                lane < 64, rolled[7 + a : 7 + a + n, :], rolled[8 + a : 8 + a + n, :]
            )

    for case in range(8):

        @pl.when(shard == case)
        def _(case=case):
            for _, row_a, row_b, offset, step, first in SEGMENTS[case]:
                if offset == TAIL:
                    piece[TAIL:PIECE, :] = tails[...]
                    continue
                count = row_b - row_a
                base = PAD + first + step * row_a - lane_start(case)
                for t in range(step):
                    out = offset + t // 2 * count
                    lanes = slice(t % 2 * 128, t % 2 * 128 + 128)
                    for a, n in chunks(count):
                        piece[out + a : out + a + n, lanes] = low(
                            rows[pl.ds(base + t + step * a, n, stride=step), :]
                        )


def pack(place, flat, tails):
    return pl.pallas_call(
        pack_kernel,
        out_shape=struct((PIECE, 256)),
        in_specs=[SMEM, VMEM, VMEM],
        out_specs=VMEM,
        scratch_shapes=[
            pltpu.VMEM((8 + LANE_ROWS, 128), jnp.float32),
            pltpu.VMEM((PAD + LANE_ROWS + PAD, 128), jnp.float32),
        ],
        compiler_params=pltpu.CompilerParams(vmem_limit_bytes=24 << 20),
        name="pack",
    )(place, flat, tails)


def unpack_kernel(place, inner, inner_last, outer, outer_last, flat, square, rows, left, right, sem):
    shard = place[0]
    is_inner = (place[1] == 1) | (place[1] == 2)

    def fetch(first, second):
        copies = [
            pltpu.make_async_copy(first, left, sem.at[0]),
            pltpu.make_async_copy(second, right, sem.at[1]),
        ]
        for copy in copies:
            copy.start()
        for copy in copies:
            copy.wait()

    @pl.when(is_inner)
    def _():
        fetch(inner, inner_last)

    @pl.when(jnp.logical_not(is_inner))
    def _():
        fetch(outer, outer_last)

    for case in range(8):

        @pl.when(shard == case)
        def _(case=case):
            for _, row_a, row_b, offset, step, first in SEGMENTS[case]:
                count = row_b - row_a
                base = PAD + first + step * row_a - lane_start(case)
                for t in range(step):
                    source = offset + t // 2 * count
                    lanes = slice(t % 2 * 128, t % 2 * 128 + 128)
                    for a, n in chunks(count):
                        spot = slice(source + a, source + a + n)
                        value = wide(left[spot, lanes]) + wide(right[spot, lanes])
                        if offset == TAIL:
                            value = jnp.zeros((n, 128), jnp.float32)
                        rows[pl.ds(base + t + step * a, n, stride=step), :] = value

    square[...] = jnp.zeros_like(square)
    for odd in range(2):

        @pl.when(shard % 2 == odd)
        def _(odd=odd):
            total = jnp.zeros((8, 128), jnp.float32)
            for a, n in chunks(LANE_ROWS):
                value = rows[PAD + a : PAD + a + n, :]
                lane = lax.broadcasted_iota(jnp.int32, (n, 128), 1)
                if odd:
                    after = rows[PAD + a + 1 : PAD + a + 1 + n, :]
                    value = jnp.where(
                        lane < 64, pltpu.roll(value, 64, 1), pltpu.roll(after, 64, 1)
                    )
                if (a + n) * 128 > SHARD:
                    row = lax.broadcasted_iota(jnp.int32, (n, 128), 0) + a
                    value = jnp.where(row * 128 + lane < SHARD, value, 0.0)
                flat[a : a + n, :] = value
                total += jnp.sum((value * value).reshape(n // 8, 8, 128), axis=0)
            square[:, 0:128] = total


def unpack(place, *pieces):
    return pl.pallas_call(
        unpack_kernel,
        out_shape=(struct((LANE_ROWS, 128), jnp.float32), struct((8, 256), jnp.float32)),
        in_specs=[SMEM] + [ANY] * 4,
        out_specs=(VMEM, VMEM),
        scratch_shapes=[
            pltpu.VMEM((PAD + LANE_ROWS + PAD, 128), jnp.float32),
            pltpu.VMEM((PIECE, 256), jnp.bfloat16),
            pltpu.VMEM((PIECE, 256), jnp.bfloat16),
            pltpu.SemaphoreType.DMA((2,)),
        ],
        compiler_params=pltpu.CompilerParams(vmem_limit_bytes=60 << 20),
        name="unpack",
    )(place, *pieces)


def combine_kernel(split, place, *refs):
    kept, sent = refs[-2:]
    first = sum(wide(ref[...]) for ref in refs[:split])
    second = sum(wide(ref[...]) for ref in refs[split:-2])
    even = place[1] % 2 == 0
    kept[...] = low(jnp.where(even, first, second))
    sent[...] = low(jnp.where(even, second, first))


def combine(place, first, second):
    blocks = 2
    size = PIECE // blocks

    def spec(piece):
        if piece.ndim == 4:
            return pl.BlockSpec((None, None, size, 256), lambda n: (0, 0, n, 0))
        return pl.BlockSpec((size, 256), lambda n: (n, 0))

    pieces = [*first, *second]
    return pl.pallas_call(
        partial(combine_kernel, len(first)),
        grid=(blocks,),
        out_shape=(struct((PIECE, 256)), struct((PIECE, 256))),
        in_specs=[SMEM] + [spec(piece) for piece in pieces],
        out_specs=(pl.BlockSpec((size, 256), lambda n: (n, 0)),) * 2,
        compiler_params=pltpu.CompilerParams(vmem_limit_bytes=60 << 20),
        name="combine",
    )(place, *pieces)


def column_sum(values):
    return jnp.sum(values, axis=0, keepdims=True)


def inside_column(place, relative):
    rows = lax.broadcasted_iota(jnp.int32, (256, 1), 0)
    position = rows + (place[3] ^ relative) * 256
    return ((position >= place[4]) & (position < place[4] + place[5])).astype(jnp.float32)


def attend_kernel(
    place, embed, bias, t0, t1, t2, t3, p0, p1, p2, p3, p4, p5, p6, p7, p8,
    stream_out, weight_out, q_out, k_out, v_out, h0, h1, h2, h3, lse_out, stack,
    tokens, staged, q_heads, k_t, v_heads, o_heads, edge, sem, sem_tokens, sem_in, sem_out,
):
    fetches = [
        pltpu.make_async_copy(ref, tokens.at[r], sem_tokens.at[r])
        for r, ref in enumerate((t0, t1, t2, t3))
    ]
    for copy in fetches:
        copy.start()

    def copies(first, second):
        return [
            pltpu.make_async_copy(first.at[0:1024, :], weight_out.at[0], sem.at[0]),
            pltpu.make_async_copy(first.at[1024:1552, :], weight_out.at[1, 0:528, :], sem.at[1]),
            pltpu.make_async_copy(second.at[16:512, :], weight_out.at[1, 528:1024, :], sem.at[2]),
            pltpu.make_async_copy(second.at[0:16, :], edge, sem.at[3]),
            pltpu.make_async_copy(second.at[512:1536, :], weight_out.at[2], sem.at[4]),
        ]

    held = ((p0, p1), (p2, p3), (p4, p5))
    for z in range(4):
        for y in range(2):
            own, other = held[SLOT[z][0]]
            pair = (other, own) if y else (own, other)

            @pl.when((place[1] == z) & (place[2] == y))
            def _(pair=pair):
                for copy in copies(*pair):
                    copy.start()

    held_in = [
        pltpu.make_async_copy(ref, staged.at[n], sem_in.at[n])
        for n, ref in enumerate((p0, p2, p4, p6, p1, p3, p5, p7, p8))
    ]
    held_out = [pltpu.make_async_copy(staged.at[n], stack.at[n], sem_out.at[n]) for n in range(9)]
    for copy in held_in:
        copy.start()
    for r, copy in enumerate(fetches):
        copy.wait()
        stream_out[r] = low(wide(tokens[r]) + inside_column(place, r) * embed[...])
    lanes = lax.broadcasted_iota(jnp.int32, (1024, 128), 1)
    v_heads[...] = jnp.broadcast_to((lanes >= 64).astype(jnp.bfloat16), (4, 1024, 128))
    for copy in copies(p0, p1):
        copy.wait()
    weight_out[1, 512:528, :] = weight_out[1, 512:528, :] + edge[...]
    for r in range(4):
        rows = slice(r * 256, r * 256 + 256)
        stream = stream_out[r]
        query = low(dot(stream, weight_out[0]) + bias[0:1, :])
        key = low(dot(stream, weight_out[1]))
        value = low(dot(stream, weight_out[2]) + bias[1:2, :])
        q_out[rows, :] = query
        k_out[rows, :] = key
        v_out[rows, :] = value
        for h in range(4):
            cols = slice(h * 64, h * 64 + 64)
            q_heads[h, rows, :] = query[:, cols] * 0.125
            v_heads[h, rows, 0:64] = value[:, cols]
        k_t[:, rows] = key.T
    lse_out[...] = jnp.zeros_like(lse_out)
    for before, copy in zip(held_in, held_out):
        before.wait()
        copy.start()

    def head_step(h, _):
        key_t = k_t[pl.ds(pl.multiple_of(h * 64, 64), 64), :]
        for r in range(4):
            rows = slice(r * 256, r * 256 + 256)
            scores = dot(q_heads[h, rows, :], key_t)
            highest = jnp.max(scores, axis=1, keepdims=True)
            weights = low(jnp.exp(scores - highest))
            result = dot(weights, v_heads[h])
            total = result[:, 64:65]
            o_heads[h, rows, :] = low(result[:, 0:64] / total)
            lane = lax.broadcasted_iota(jnp.int32, (256, 128), 1)
            lse_out[rows, :] = jnp.where(lane == h, highest + jnp.log(total), lse_out[rows, :])
        return 0

    lax.fori_loop(0, 4, head_step, 0, unroll=4)
    for r, out in enumerate((h0, h1, h2, h3)):
        for h in range(4):
            out[:, h * 64 : h * 64 + 64] = o_heads[h, r * 256 : r * 256 + 256, :]
    for copy in held_out:
        copy.wait()


def attend(place, tokens, embed, bias, pieces):
    square = struct((1024, 256))
    block = struct((256, 256))
    return pl.pallas_call(
        attend_kernel,
        out_shape=(
            struct((4, 256, 1024)), struct((3, 1024, 256)), square, square, square,
            block, block, block, block, struct((1024, 128), jnp.float32), struct((9, PIECE, 256)),
        ),
        in_specs=[SMEM] + [VMEM] * 2 + [ANY] * 13,
        out_specs=(VMEM,) * 10 + (ANY,),
        scratch_shapes=[
            pltpu.VMEM((4, 256, 1024), jnp.bfloat16),
            pltpu.VMEM((9, PIECE, 256), jnp.bfloat16),
            pltpu.VMEM((4, 1024, 64), jnp.bfloat16),
            pltpu.VMEM((256, 1024), jnp.bfloat16),
            pltpu.VMEM((4, 1024, 128), jnp.bfloat16),
            pltpu.VMEM((4, 1024, 64), jnp.bfloat16),
            pltpu.VMEM((16, 256), jnp.bfloat16),
            pltpu.SemaphoreType.DMA((5,)),
            pltpu.SemaphoreType.DMA((4,)),
            pltpu.SemaphoreType.DMA((9,)),
            pltpu.SemaphoreType.DMA((9,)),
        ],
        compiler_params=pltpu.CompilerParams(vmem_limit_bytes=48 << 20),
        cost_estimate=pl.CostEstimate(
            flops=16_000_000_000, bytes_accessed=24_000_000, transcendentals=4_194_304
        ),
        name="attend",
    )(place, embed, bias, *tokens, *pieces)


def attend_back_kernel(
    place, q_in, k_in, v_in, lse, weight, g0, g1, g2, g3,
    q_grad, k_grad, v_grad, kept, sent, sums,
    q_heads, k_heads, g_heads, q_t, k_t, v_t, g_t, dq_heads, dk_t, dv_t,
):
    for r, grad in enumerate((g0, g1, g2, g3)):
        rows = slice(r * 256, r * 256 + 256)
        g_t[:, rows] = grad[...].T
        for h in range(4):
            cols = slice(h * 64, h * 64 + 64)
            q_heads[h, rows, :] = q_in[rows, cols] * 0.125
            k_heads[h, rows, :] = k_in[rows, cols]
            g_heads[h, rows, :] = grad[:, cols]
    q_t[...] = (q_in[...] * 0.125).T
    k_t[...] = k_in[...].T
    v_t[...] = v_in[...].T

    def head_step(h, _):
        mine = pl.ds(pl.multiple_of(h * 64, 64), 64)
        key_t, value_t, key = k_t[mine, :], v_t[mine, :], k_heads[h]
        key_sum = jnp.zeros((64, 1024), jnp.float32)
        value_sum = jnp.zeros((64, 1024), jnp.float32)
        for r in range(4):
            rows = slice(r * 256, r * 256 + 256)
            scores = dot(q_heads[h, rows, :], key_t)
            lane = lax.broadcasted_iota(jnp.int32, (256, 128), 1)
            logsum = jnp.sum(jnp.where(lane == h, lse[rows, :], 0.0), axis=1, keepdims=True)
            probs = jnp.exp(scores - logsum)
            weighted = probs * dot(g_heads[h, rows, :], value_t)
            inner = jnp.sum(weighted, axis=1, keepdims=True)
            score_grad = low(weighted - probs * inner)
            dq_heads[h, rows, :] = low(dot(score_grad, key) * 0.125)
            key_sum += dot(q_t[mine, rows], score_grad)
            value_sum += dot(g_t[mine, rows], low(probs))
        dk_t[mine, :] = low(key_sum)
        dv_t[mine, :] = low(value_sum)
        return 0

    lax.fori_loop(0, 4, head_step, 0, unroll=4)
    for h in range(4):
        q_grad[:, h * 64 : h * 64 + 64] = dq_heads[h]
    k_grad[...] = dk_t[...].T
    v_grad[...] = dv_t[...].T
    sums[...] = jnp.zeros_like(sums)
    sums[1:2, 0:256] = column_sum(wide(q_grad[...]))
    sums[2:3, 0:256] = column_sum(wide(v_grad[...]))
    for r in range(4):
        rows = slice(r * 256, r * 256 + 256)
        part = (
            dot_last(q_grad[rows, :], weight[0])
            + dot_last(k_grad[rows, :], weight[1])
            + dot_last(v_grad[rows, :], weight[2])
        )
        sums[0:1, :] += column_sum(inside_column(place, r) * part)
        if r % 2:
            sent[r // 2] = low(part)
        else:
            kept[r // 2] = part


def attend_back(place, query, key, value, lse, weight, grads):
    square = struct((1024, 256))
    return pl.pallas_call(
        attend_back_kernel,
        out_shape=(
            square, square, square, struct((2, 256, D), jnp.float32), struct((2, 256, D)),
            struct((8, D), jnp.float32),
        ),
        in_specs=[SMEM] + [VMEM] * 9,
        out_specs=(VMEM,) * 6,
        scratch_shapes=[pltpu.VMEM((4, 1024, 64), jnp.bfloat16)] * 3
        + [pltpu.VMEM((256, 1024), jnp.bfloat16)] * 4
        + [pltpu.VMEM((4, 1024, 64), jnp.bfloat16)]
        + [pltpu.VMEM((256, 1024), jnp.bfloat16)] * 2,
        compiler_params=pltpu.CompilerParams(vmem_limit_bytes=40 << 20),
        cost_estimate=pl.CostEstimate(
            flops=20_000_000_000, bytes_accessed=12_000_000, transcendentals=4_194_304
        ),
        name="attend_back",
    )(place, query, key, value, lse, weight, *grads)


def row_mean(values):
    return jnp.sum(values, axis=1, keepdims=True) * (1.0 / D)


def normalise(resid):
    centred = resid - row_mean(resid)
    scale = lax.rsqrt(row_mean(centred * centred) + NORM_EPS)
    return centred * scale, scale


def normalise_back(grad, gain, xhat, scale):
    scaled = grad * gain
    return (scaled - row_mean(scaled) - xhat * row_mean(scaled * xhat)) * scale


def target_piece(targets, k, ry, rx):
    return targets[k - 1].at[ry, rx] if k == 1 else targets[k - 1].at[rx, ry]


def layer_kernel(
    place, h0, h1, h2, h3, tokens, cotangent, embed, vectors, bias_up, out_head, *refs
):
    stack = refs[15]
    pieces = (refs[:15], [stack.at[n] for n in range(9)] + list(refs[16:22]))
    refs = refs[22:]
    (block_out, resid_grad, g0, g1, g2, g3, sums, sums_up, head_grad) = refs[:9]
    grads_own, grads_other = refs[9:12], refs[12:15]
    (w_out, w_up, w_down, edge_up, edge_down, hidden, slope, grad_up, grad_down,
     grad_out, acc, acc_t, grad_t, sem, sem_out) = refs[15:]

    def fetch(z, y):
        made = {"out": [], "up": [], "down": []}
        for k in range(1, 4):
            for ry in range(2):
                case = 2 * k + (y ^ ry)
                for r in range(4):
                    rx, rc = r // 2, r % 2
                    source = pieces[rc][BUFFER[z][rx * 8 + ry * 4 + SLOT[z][k]]]
                    column = place[3] ^ r
                    for name, row_a, row_b, offset, step, _ in SEGMENTS[case]:
                        count = row_b - row_a
                        if name == "o":
                            made["out"].append(
                                (source.at[offset : offset + count, :], w_out.at[:, pl.ds(column * 256, 256)])
                            )
                        elif name == "up":
                            block = source.at[offset : offset + 4 * count, :].reshape(4, count, 256)
                            target = w_up.at[pl.ds(column * 4, 4)]
                            skip = 0
                            if row_a:
                                skip = 16
                                made["up"].append(
                                    (block.at[:, 0:16, :], edge_up.at[case - 3, pl.ds(column * 4, 4)])
                                )
                            made["up"].append(
                                (block.at[:, skip:count, :], target.at[:, row_a + skip : row_b, :])
                            )
                        elif name == "down":
                            skip = 0
                            if row_a:
                                skip = 16
                                made["down"].append(
                                    (source.at[offset : offset + 16, :], edge_down.at[case - 6, :, pl.ds(column * 256, 256)])
                                )
                            made["down"].append(
                                (source.at[offset + skip : offset + count, :],
                                 w_down.at[row_a + skip : row_b, pl.ds(column * 256, 256)])
                            )
        return made

    order = ("out", "up", "down")
    for z in range(4):
        for y in range(2):

            @pl.when((place[1] == z) & (place[2] == y))
            def _(z=z, y=y):
                made = fetch(z, y)
                for n, name in enumerate(order):
                    for source, target in made[name]:
                        pltpu.make_async_copy(source, target, sem.at[n]).start()

    def arrived(refs, n):
        for ref in refs:
            pltpu.make_async_copy(ref, ref, sem.at[n]).wait()

    here = inside_column(place, 0)
    stream = wide(tokens[...]) + here * embed[...]
    arrived([w_out], 0)
    for n in range(4):
        cols = slice(n * 256, n * 256 + 256)
        w_out[0:16, cols] = w_out[0:16, cols] + out_head[n]
    heads = (h0, h1, h2, h3)

    def head_rows(r):
        return pl.ds(pl.multiple_of((place[3] ^ r) * 256, 256), 256)

    acc[...] = sum(dot(heads[r][...], w_out[head_rows(r), :]) for r in range(4))
    bias_out, bias_down, gain_a, shift_a, gain_f, shift_f = (vectors[n : n + 1, :] for n in range(6))
    xhat_a, scale_a = normalise(stream + acc[...] + bias_out)
    normed = xhat_a * gain_a + shift_a
    normed_low = low(normed)

    arrived([w_up] + [edge_up], 1)
    for n, row in enumerate((128, 512, 896)):
        w_up[:, row : row + 16, :] = w_up[:, row : row + 16, :] + edge_up[n]

    def up(g, _):
        pre = dot(normed_low, w_up[g]) + bias_up[pl.ds(g, 1), :]
        inner = 0.5 * (1.0 + lax.erf(pre * (1.0 / math.sqrt(2.0))))
        hidden[:, pl.ds(pl.multiple_of(g * 256, 256), 256)] = low(pre * inner)
        bend = inner + pre * (jnp.exp(-0.5 * pre * pre) * (1.0 / math.sqrt(2.0 * math.pi)))
        slope[pl.ds(pl.multiple_of(g * 256, 256), 256), :] = bend.T
        return 0

    lax.fori_loop(0, 16, up, 0, unroll=16)
    arrived([w_down] + [edge_down], 2)
    for n, row in enumerate((1024, 2560)):
        w_down[row : row + 16, :] = w_down[row : row + 16, :] + edge_down[n]
    acc[...] = normed + bias_down + dot(hidden[...], w_down[...])
    xhat_f, scale_f = normalise(acc[...])
    block_out[...] = low(xhat_f * gain_f + shift_f)

    out_grad = wide(cotangent[...])
    sums[4:5, :] = column_sum(out_grad * xhat_f)
    sums[5:6, :] = column_sum(out_grad)
    acc[...] = normalise_back(out_grad, gain_f, xhat_f, scale_f)
    ffn_grad = low(acc[...])
    sums[1:2, :] = column_sum(wide(ffn_grad))
    grad_t[...] = ffn_grad.T
    normed_t = normed_low.T

    def routes(case, name):
        return [
            (row_a, row_b, offset, row_b - row_a)
            for seg, row_a, row_b, offset, _, _ in SEGMENTS[case]
            if seg == name
        ]

    def outputs_up(case, column, targets, rx):
        piece = target_piece(targets, case // 2, place[2] ^ (case % 2), rx)
        return [
            pltpu.make_async_copy(
                grad_up.at[column * 4 : column * 4 + 4, row_a:row_b, :],
                piece.at[offset : offset + 4 * count, :].reshape(4, count, 256),
                sem_out.at[0],
            )
            for row_a, row_b, offset, count in routes(case, "up")
        ]

    def outputs(case):
        made = []
        for r in range(4):
            rx, rc = r // 2, r % 2
            column = place[3] ^ r
            targets = grads_other if rc else grads_own
            piece = target_piece(targets, case // 2, place[2] ^ (case % 2), rx)
            for row_a, row_b, offset, count in routes(case, "down"):
                source = grad_down.at[row_a:row_b, pl.ds(column * 256, 256)]
                target = piece.at[offset : offset + count, :]
                made.append(pltpu.make_async_copy(source, target, sem_out.at[0]))
        return made

    acc_t[...] = jnp.zeros_like(acc_t)

    for chunk in range(4):
        rows = slice(chunk * 1024, chunk * 1024 + 1024)
        pre_grad_t = low(dot(w_down[rows, :], grad_t[...]) * slope[rows, :])
        pre_grad = pre_grad_t.T
        sums_up[chunk : chunk + 1, :] = column_sum(wide(pre_grad))
        for n in range(4):
            g = chunk * 4 + n
            acc_t[...] += dot(w_up[g], pre_grad_t[n * 256 : n * 256 + 256, :])
            grad_up[g] = low(dot(normed_t, pre_grad[:, n * 256 : n * 256 + 256]))
        grad_down[rows, :] = low(dot_first(hidden[:, rows], ffn_grad))
        relative = place[3] ^ chunk
        for side, targets in enumerate((grads_own, grads_other)):

            @pl.when(relative % 2 == side)
            def _(chunk=chunk, targets=targets, relative=relative):
                for case in range(2, 6):
                    for copy in outputs_up(case, chunk, targets, relative // 2):
                        copy.start()

        for case in {1: (5,), 2: (6,)}.get(chunk, ()):
            for copy in outputs(case):
                copy.start()
    for copy in outputs(7):
        copy.start()
    acc[...] += acc_t[...].T

    normed_grad = acc[...]
    sums[2:3, :] = column_sum(normed_grad * xhat_a)
    sums[3:4, :] = column_sum(normed_grad)
    attn_wide = normalise_back(normed_grad, gain_a, xhat_a, scale_a)
    resid_grad[...] = attn_wide
    sums[6:7, :] = column_sum(here * attn_wide)
    attn_grad = low(attn_wide)
    grad_t[...] = attn_grad.T
    sums[0:1, :] = column_sum(wide(attn_grad))
    sums[7:8, :] = jnp.zeros((1, D), jnp.float32)
    for r, out in enumerate((g0, g1, g2, g3)):
        out[...] = low(dot(w_out[head_rows(r), :], grad_t[...]).T)
        grad_out[head_rows(r), :] = low(dot_first(heads[r][...], attn_grad))
    for n in range(4):
        head_grad[n] = wide(grad_out[0:16, n * 256 : n * 256 + 256])
    last = []
    for r in range(4):
        rx, rc = r // 2, r % 2
        column = place[3] ^ r
        targets = grads_other if rc else grads_own
        piece = target_piece(targets, 1, place[2], rx)
        last.append((grad_out.at[:, pl.ds(column * 256, 256)], piece.at[0:1024, :]))
    for source, target in last:
        pltpu.make_async_copy(source, target, sem_out.at[1]).start()
    for case in range(5, 8):
        for copy in outputs(case):
            copy.wait()
    for column in range(4):
        for case in range(2, 6):
            for copy in outputs_up(case, column, grads_own, 0):
                copy.wait()
    for source, target in last:
        pltpu.make_async_copy(source, target, sem_out.at[1]).wait()


def layer(place, heads, tokens, cotangent, embed, vectors, bias_up, out_head, pieces):
    grads = struct((2, 2, PIECE, 256))
    block = struct((256, 256))
    return pl.pallas_call(
        layer_kernel,
        out_shape=(
            struct((256, D)), struct((256, D), jnp.float32), block, block, block, block,
            struct((8, D), jnp.float32), struct((4, 1024), jnp.float32),
            struct((4, 16, 256), jnp.float32),
        ) + (grads,) * 6,
        in_specs=[SMEM] + [VMEM] * 10 + [ANY] * 22,
        out_specs=(VMEM,) * 9 + (ANY,) * 6,
        scratch_shapes=[
            pltpu.VMEM((D, D), jnp.bfloat16),
            pltpu.VMEM((16, 1024, 256), jnp.bfloat16),
            pltpu.VMEM((FF, D), jnp.bfloat16),
            pltpu.VMEM((3, 16, 16, 256), jnp.bfloat16),
            pltpu.VMEM((2, 16, D), jnp.bfloat16),
            pltpu.VMEM((256, FF), jnp.bfloat16),
            pltpu.VMEM((FF, 256), jnp.float32),
            pltpu.VMEM((16, 1024, 256), jnp.bfloat16),
            pltpu.VMEM((FF, D), jnp.bfloat16),
            pltpu.VMEM((D, D), jnp.bfloat16),
            pltpu.VMEM((256, D), jnp.float32),
            pltpu.VMEM((D, 256), jnp.float32),
            pltpu.VMEM((D, 256), jnp.bfloat16),
            pltpu.SemaphoreType.DMA((3,)),
            pltpu.SemaphoreType.DMA((2,)),
        ],
        compiler_params=pltpu.CompilerParams(vmem_limit_bytes=60 << 20),
        cost_estimate=pl.CostEstimate(
            flops=15_000_000_000, bytes_accessed=40_000_000, transcendentals=2_097_152
        ),
        name="layer",
    )(place, *heads, tokens, cotangent, embed, vectors, bias_up, out_head, *pieces)


def product(left, right):
    return jnp.dot(left, right, preferred_element_type=jnp.float32)


def product_inner(left, right):
    return lax.dot_general(
        left, right, (((0,), (0,)), ((), ())), preferred_element_type=jnp.float32
    )


def layer_norm(resid, gain, shift):
    average = jnp.mean(resid, axis=-1, keepdims=True)
    centred = resid - average
    variance = jnp.mean(centred * centred, axis=-1, keepdims=True)
    return centred * lax.rsqrt(variance + NORM_EPS) * gain + shift


def unpack_all(flat_params, dp_count, fsdp_count):
    shapes = [(D, D)] * 4 + [(D, FF), (FF, D)] + [(1, D)] * 4 + [(1, FF)] + [(1, D)] * 6
    blocks = (
        flat_params.reshape(dp_count, fsdp_count, -1).transpose(1, 0, 2).reshape(fsdp_count, -1)
    )
    pieces = []
    offset = 0
    for rows, cols in shapes:
        width = rows * (cols // fsdp_count)
        part = blocks[:, offset : offset + width].reshape(fsdp_count, rows, cols // fsdp_count)
        whole = part.transpose(1, 0, 2).reshape(rows, cols)
        pieces.append(whole.reshape(-1) if rows == 1 else whole)
        offset += width
    return pieces


def split_heads(values):
    return values.reshape(values.shape[0], H, DH).transpose(1, 0, 2)


def merge_heads(values):
    return values.transpose(1, 0, 2).reshape(values.shape[1], H * DH)


def head_forward(head_item):
    query_h, key_h, value_h = head_item
    scores = product(query_h, key_h.T) * DH ** (-0.5)
    highest = jnp.max(scores, axis=1, keepdims=True)
    weights = jnp.exp(scores - highest)
    totals = jnp.sum(weights, axis=1, keepdims=True)
    probabilities = weights / totals
    result = product(probabilities.astype(jnp.bfloat16), value_h)
    return (result, (highest + jnp.log(totals))[:, 0])


def head_query_back(head_item):
    query_h, key_h, value_h, grad_h, logsum = head_item
    score_scale = DH ** (-0.5)
    scores = product(query_h, key_h.T) * score_scale
    probabilities = jnp.exp(scores - logsum[:, None])
    prob_grad = product(grad_h, value_h.T)
    inner_sum = jnp.sum(probabilities * prob_grad, axis=1)
    score_grad = (probabilities * (prob_grad - inner_sum[:, None])).astype(jnp.bfloat16)
    query_grad = product(score_grad, key_h) * score_scale
    return (query_grad, inner_sum)


def head_key_back(head_item):
    key_h, value_h, query_all, grad_all, logsum_all, inner_all = head_item
    score_scale = DH ** (-0.5)
    scores_t = product(key_h, query_all.T) * score_scale
    probs_t = jnp.exp(scores_t - logsum_all[None, :])
    prob_grad_t = product(value_h, grad_all.T)
    score_grad_t = (probs_t * (prob_grad_t - inner_all[None, :])).astype(jnp.bfloat16)
    key_grad = product(score_grad_t, query_all) * score_scale
    value_grad = product(probs_t.astype(jnp.bfloat16), grad_all)
    return (key_grad, value_grad)


def body(
    tokens,
    cotangent,
    master,
    first_moment,
    second_moment,
    average,
    timestep,
    block_length,
    block_start,
):
    dp_count = lax.axis_size("dp")
    fsdp_count = lax.axis_size("fsdp")
    master_low = master.astype(jnp.bfloat16)
    flat_params = lax.all_gather(master_low, ("dp", "fsdp"), axis=0, tiled=True)
    (
        w_query,
        w_key,
        w_value,
        w_out,
        w_up,
        w_down,
        b_query,
        b_value,
        b_out,
        b_down,
        b_up,
        gain_attn,
        shift_attn,
        gain_ffn,
        shift_ffn,
        w_time,
        b_time,
    ) = unpack_all(flat_params, dp_count, fsdp_count)
    gain_a = gain_attn.astype(jnp.float32)
    shift_a = shift_attn.astype(jnp.float32)
    gain_f = gain_ffn.astype(jnp.float32)
    shift_f = shift_ffn.astype(jnp.float32)
    row_count = tokens.shape[0]
    position = lax.axis_index("fsdp") * row_count + jnp.arange(row_count, dtype=jnp.int32)
    block_first = block_start[0]
    inside = ((position >= block_first) & (position < block_first + block_length[0])).astype(
        jnp.float32
    )[:, None]
    time_frac = timestep[0].astype(jnp.float32) / 5000.0
    time_embed = time_frac * w_time.astype(jnp.float32) + b_time.astype(jnp.float32)
    stream = tokens.astype(jnp.float32) + inside * time_embed
    stream_low = stream.astype(jnp.bfloat16)
    queries = (product(stream_low, w_query) + b_query.astype(jnp.float32)).astype(jnp.bfloat16)
    keys_local = product(stream_low, w_key).astype(jnp.bfloat16)
    values_local = (product(stream_low, w_value) + b_value.astype(jnp.float32)).astype(jnp.bfloat16)
    keys_all, values_all = (
        lax.all_gather(keys_local, "fsdp", axis=0, tiled=True),
        lax.all_gather(values_local, "fsdp", axis=0, tiled=True),
    )
    query_heads = split_heads(queries)
    key_heads = split_heads(keys_all)
    value_heads = split_heads(values_all)
    head_out, logsum = lax.map(head_forward, (query_heads, key_heads, value_heads))
    heads_low = merge_heads(head_out).astype(jnp.bfloat16)
    resid_attn = stream + product(heads_low, w_out) + b_out.astype(jnp.float32)
    normed = layer_norm(resid_attn, gain_a, shift_a)
    normed_low = normed.astype(jnp.bfloat16)
    pre_act = product(normed_low, w_up) + b_up.astype(jnp.float32)
    hidden = jax.nn.gelu(pre_act, approximate=False).astype(jnp.bfloat16)
    resid_ffn = normed + product(hidden, w_down) + b_down.astype(jnp.float32)
    block_out = layer_norm(resid_ffn, gain_f, shift_f).astype(jnp.bfloat16)
    stream_all, heads_all, normed_all, hidden_all = (
        lax.all_gather(stream_low, "fsdp", axis=0, tiled=True),
        lax.all_gather(heads_low, "fsdp", axis=0, tiled=True),
        lax.all_gather(normed_low, "fsdp", axis=0, tiled=True),
        lax.all_gather(hidden, "fsdp", axis=0, tiled=True),
    )
    back_params = lax.all_gather(master_low, ("dp", "fsdp"), axis=0, tiled=True)
    back_pieces = unpack_all(back_params, dp_count, fsdp_count)
    w_query_back, w_key_back, w_value_back, w_out_back, w_up_back, w_down_back = back_pieces[:6]
    out_grad = cotangent.astype(jnp.float32)
    _, pull_ffn = jax.vjp(layer_norm, resid_ffn, gain_f, shift_f)
    resid_ffn_grad, grad_gain_ffn, grad_shift_ffn = pull_ffn(out_grad)
    ffn_grad = resid_ffn_grad.astype(jnp.bfloat16)
    hidden_grad = product(ffn_grad, w_down_back.T)
    _, pull_gelu = jax.vjp(partial(jax.nn.gelu, approximate=False), pre_act)
    pre_grad = pull_gelu(hidden_grad)[0].astype(jnp.bfloat16)
    normed_grad = resid_ffn_grad + product(pre_grad, w_up_back.T)
    _, pull_attn = jax.vjp(layer_norm, resid_attn, gain_a, shift_a)
    resid_attn_grad, grad_gain_attn, grad_shift_attn = pull_attn(normed_grad)
    attn_grad = resid_attn_grad.astype(jnp.bfloat16)
    heads_grad = product(attn_grad, w_out_back.T).astype(jnp.bfloat16)
    query_parts, inner_sum = lax.map(
        head_query_back, (query_heads, key_heads, value_heads, split_heads(heads_grad), logsum)
    )
    query_grad = merge_heads(query_parts).astype(jnp.bfloat16)
    queries_all, heads_grad_all = (
        lax.all_gather(queries, "fsdp", axis=0, tiled=True),
        lax.all_gather(heads_grad, "fsdp", axis=0, tiled=True),
    )
    logsum_all, inner_all = (
        lax.all_gather(logsum, "fsdp", axis=1, tiled=True),
        lax.all_gather(inner_sum, "fsdp", axis=1, tiled=True),
    )
    key_parts, value_parts = lax.map(
        head_key_back,
        (
            split_heads(keys_local),
            split_heads(values_local),
            split_heads(queries_all),
            split_heads(heads_grad_all),
            logsum_all,
            inner_all,
        ),
    )
    key_grad = merge_heads(key_parts).astype(jnp.bfloat16)
    value_grad = merge_heads(value_parts).astype(jnp.bfloat16)
    stream_grad = (
        resid_attn_grad
        + product(query_grad, w_query_back.T)
        + product(key_grad, w_key_back.T)
        + product(value_grad, w_value_back.T)
    )
    grad_b_time = jnp.sum(inside * stream_grad, axis=0)
    grad_w_time = time_frac * grad_b_time
    query_cols, key_cols, value_cols, attn_cols, ffn_cols, pre_cols = (
        lax.all_to_all(query_grad, "fsdp", split_axis=1, concat_axis=0, tiled=True),
        lax.all_to_all(key_grad, "fsdp", split_axis=1, concat_axis=0, tiled=True),
        lax.all_to_all(value_grad, "fsdp", split_axis=1, concat_axis=0, tiled=True),
        lax.all_to_all(attn_grad, "fsdp", split_axis=1, concat_axis=0, tiled=True),
        lax.all_to_all(ffn_grad, "fsdp", split_axis=1, concat_axis=0, tiled=True),
        lax.all_to_all(pre_grad, "fsdp", split_axis=1, concat_axis=0, tiled=True),
    )
    grad_w_query = product_inner(stream_all, query_cols)
    grad_w_key = product_inner(stream_all, key_cols)
    grad_w_value = product_inner(stream_all, value_cols)
    grad_w_out = product_inner(heads_all, attn_cols)
    grad_w_up = product_inner(normed_all, pre_cols)
    grad_w_down = product_inner(hidden_all, ffn_cols)
    grad_b_query = jnp.sum(query_cols.astype(jnp.float32), axis=0)
    grad_b_value = jnp.sum(value_cols.astype(jnp.float32), axis=0)
    grad_b_out = jnp.sum(attn_cols.astype(jnp.float32), axis=0)
    grad_b_down = jnp.sum(ffn_cols.astype(jnp.float32), axis=0)
    grad_b_up = jnp.sum(pre_cols.astype(jnp.float32), axis=0)
    vector_terms = jnp.stack(
        [grad_gain_attn, grad_shift_attn, grad_gain_ffn, grad_shift_ffn, grad_w_time, grad_b_time]
    )
    vector_part = lax.psum_scatter(vector_terms, "fsdp", scatter_dimension=1, tiled=True)
    vector_block = jnp.concatenate(
        [grad_b_query, grad_b_value, grad_b_out, grad_b_down, grad_b_up, vector_part.reshape(-1)]
    )
    grad_block = jnp.concatenate(
        [
            piece.reshape(-1)
            for piece in (
                grad_w_query,
                grad_w_key,
                grad_w_value,
                grad_w_out,
                grad_w_up,
                grad_w_down,
            )
        ]
        + [vector_block]
    )
    grad_shard = lax.psum_scatter(grad_block, "dp", scatter_dimension=0, tiled=True)
    vector_grad = lax.psum(vector_block, "dp")
    square_sum = lax.psum(jnp.sum(grad_shard * grad_shard), ("dp", "fsdp"))
    grad_norm = jnp.sqrt(square_sum)
    clip_limit = 4.0 * math.sqrt(PARAMS)
    clipped = grad_shard * (clip_limit / jnp.maximum(grad_norm, clip_limit))
    new_first = 0.9 * first_moment + 0.1 * clipped
    new_second = 0.98 * second_moment + 0.02 * clipped * clipped
    first_hat = new_first / (1.0 - 0.9**STEP)
    second_hat = new_second / (1.0 - 0.98**STEP)
    new_master = master - 0.02 * (first_hat / (jnp.sqrt(second_hat) + 1e-06) + 0.01 * master)
    new_average = 0.99 * average + 0.01 * new_master
    return (
        block_out,
        stream_grad,
        grad_norm,
        vector_grad,
        new_first,
        new_second,
        new_master,
        new_average,
    )


AXES = ("dp", "fsdp")


def send(values, route, name="move"):
    pairs = []
    for n in range(32):
        there = route(n // 8, n // 4 % 2, n // 2 % 2, n % 2)
        if there is not None:
            z, y, x, c = there
            pairs.append((n, z * 8 + y * 4 + x * 2 + c))
    with jax.named_scope(name):
        return lax.ppermute(values, AXES, pairs)


def to_core(z, y, x, c):
    return z, y, x, 1 - c


def to_x(z, y, x, c):
    return z, y, 1 - x, c


def to_y(z, y, x, c):
    return z, 1 - y, x, c


def to_near(z, y, x, c):
    return z ^ 1, y, x, c


def to_far(z, y, x, c):
    return z ^ 2, y, x, c


def only(route, planes):
    return lambda z, y, x, c: route(z, y, x, c) if z in planes else None


def to_opposite(z, y, x, c):
    return 3 - z, y, x, c


def to_relative(r):
    return lambda z, y, x, c: (z, y, x ^ (r // 2), c ^ (r % 2))


def exchange(blocks, name):
    return [blocks[0]] + [send(blocks[r], to_relative(r), name) for r in range(1, 4)]


def after(values, *earlier):
    return lax.optimization_barrier((values, *earlier))[0]


def together(values, routes, *beside):
    near, far, both = (send(values, route, "norm") for route in routes)
    return (values + near) + (far + after(both, *beside))


PLANES = ((1, 2, 3), (0, 1, 3), (0, 2), (0, 1, 2, 3))


def gather_pieces(own, z, y, tokens, run_attend):
    def across(name, values, n):
        return send(values, only(to_x, PLANES[n]), name)

    outer = (z == 0) | (z == 3)
    first = send(own, lambda z, y, x, c: ((2, 0, 3, 1)[z], y, x, c), "first")
    y0 = send(own, to_y, "y0")
    tokens_x = send(tokens, to_x, "tok_x")
    x0 = across("x0", own, 0)
    tokens_c = send(tokens, to_core, "tok_c")
    second = send(after(jnp.where(outer, own, first), tokens_x), to_near, "second")
    crossed = send(
        after(own, first), lambda z, y, x, c: (3 - z, y, x, c) if z in (1, 2) else None, "crossed"
    )
    y1 = send(after(first, y0), to_y, "y1")
    x1 = across("x1", after(first, x0), 1)
    third = send(after(crossed, second), only(to_near, (1, 2)), "third")
    y2 = send(after(second, y1), to_y, "y2")
    x_a = send(jnp.where(z % 2 == 0, second, y0), to_x, "xa")
    last = jnp.where(outer, third, crossed)
    tokens_xc = send(after(tokens_x, third), to_core, "tok_xc")
    y3 = send(after(last, y2), to_y, "y3")
    y_b = send(after(jnp.where(z == 2, x0, x1), y2), to_y, "yb")
    yx2 = across("yx2", after(y2, last), 2)
    x3 = across("x3", after(last, y2), 3)
    tail_0, tail_1, tail_2 = (
        jnp.where(y == 1, mine[TAIL:], other[TAIL:])
        for mine, other in ((own, y0), (first, y1), (second, y2))
    )
    attended = run_attend(
        after(last, y2), (own, y0, first, y1, second, y2, last, x0, x1),
        (tokens, tokens_c, tokens_x, tokens_xc),
        jnp.where(z == 3, tail_0, jnp.where(z == 1, tail_1, tail_2)),
        jnp.where(z == 0, tail_0, jnp.where(z == 2, tail_1, tail_2)),
    )
    attended = lax.optimization_barrier((*attended, x_a, y3, yx2, x3, y_b))[: len(attended)]
    stack = send(attended[-1], to_core, "stack")
    heads = exchange(attended[5:9], "heads")
    yx3 = across("yx3", after(y3, x3, attended[-1]), 3)
    later = [
        send(after(piece, attended[-1]), only(to_core, planes), name)
        for piece, planes, name in (
            (x_a, (0, 1, 2, 3), "cxa"), (y3, (0, 1, 2, 3), "cy3"), (y_b, (0, 1, 2, 3), "cyb"),
            (yx2, PLANES[2], "cyx2"), (x3, (0, 1, 2, 3), "cx3"), (yx3, (0, 1, 2, 3), "cyx3"),
        )
    ]
    mine = [own, first, second, last, y0, y1, y2, x0, x1, x_a, y3, y_b, yx2, x3, yx3]
    return attended[:5], heads, attended[9], [*mine, stack, *later]


def add(left, right):
    return wide(left) + wide(right)


def block_body(
    tokens,
    cotangent,
    master,
    first_moment,
    second_moment,
    average,
    timestep,
    block_length,
    block_start,
):
    shard = lax.axis_index("dp")
    j = lax.axis_index("fsdp")
    z, y = shard // 2, shard % 2
    place = jnp.stack([shard, z, y, j, block_start[0], block_length[0]]).astype(jnp.int32)
    flat = jnp.pad(master, (0, LANE_ROWS * 128 - SHARD)).reshape(LANE_ROWS, 128)
    vec_rows = jnp.pad(master[SHARD - 3584 :].reshape(14, 256), ((0, 2), (0, 0)))
    head_rows = jnp.pad(master[SHARD - 896 :], (0, 3200)).reshape(16, 256)
    tail = low(jnp.where(shard == 7, vec_rows, head_rows))
    tail_x = after(send(tail, to_x, "tail_x"), flat)
    tail_c = send(jnp.concatenate([tail, tail_x]), to_core, "tail_c")
    own = pack(place, flat, jnp.concatenate([tail, tail_c[:16], tail_x, tail_c[16:]]))
    here = (jnp.arange(4) == j)[:, None, None]
    time_frac = timestep[0].astype(jnp.float32) / 5000.0
    vectors = {}

    def absolute(relative):
        blocks = relative.reshape(4, 16, 256)
        blocks = jnp.where(j % 2 == 1, jnp.concatenate([blocks[1:2], blocks[0:1], blocks[3:4], blocks[2:3]]), blocks)
        return jnp.where(j // 2 == 1, jnp.concatenate([blocks[2:4], blocks[0:2]]), blocks)

    def run_attend(ready, held, all_tokens, vec_tail, head_tail):
        vec = wide(absolute(vec_tail))
        full = vec.transpose(1, 0, 2).reshape(16, D)
        vec_own = wide(vec_tail[:16])
        vectors["embed"] = time_frac * full[12:13] + full[13:14]
        vectors["rows"] = jnp.concatenate([full[2:4], full[8:12], jnp.zeros((2, D), jnp.float32)])
        vectors["up"] = vec[:, 4:8].reshape(16, 256)
        vectors["head"] = absolute(head_tail)
        return attend(after(place, ready), all_tokens, vectors["embed"], vec_own[0:8], held)

    attended, heads, lse, pieces = gather_pieces(own, z, y, tokens, run_attend)
    stream, weight, query, key, value = attended

    (block_out, resid_grad, g0, g1, g2, g3, sums, sums_up, head_grad, *grads) = layer(
        place, heads, tokens, cotangent, vectors["embed"],
        vectors["rows"], vectors["up"], vectors["head"], pieces,
    )
    grads_own, grads_other = grads[:3], grads[3:]

    moved = {k: send(grads_other[k - 1], to_core, f"rc{k}") for k in (2, 1)}
    moved[3] = send(after(grads_other[2], moved[2], moved[1]), to_core, "rc3")

    def over_cores(k, a, b):
        return add(grads_own[k - 1][a, b], moved[k][a, b])

    grad_heads = exchange((g0, g1, g2, g3), "heads_grad")
    starts = {
        name: after(low(over_cores(k, 1, b)), *grad_heads)
        for name, k, b in (("d1", 1, 1), ("d2", 2, 1), ("e1", 1, 0), ("e2", 2, 0))
    }
    d1 = send(starts["d1"], to_y, "d1")
    d2 = send(starts["d2"], to_x, "d2")
    e1 = send(starts["e1"], to_y, "e1")
    e2 = send(starts["e2"], to_x, "e2")

    (q_grad, k_grad, v_grad, kept, sent, sums_qkv) = attend_back(
        after(place, *starts.values()),
        query, key, value, lse, weight, grad_heads,
    )

    q_grad, k_grad, v_grad, kept, sent, sums_qkv, d1, d2 = lax.optimization_barrier(
        (q_grad, k_grad, v_grad, kept, sent, sums_qkv, d1, d2)
    )
    sum_1 = low(over_cores(1, 0, 1) + wide(d1))
    sum_2 = low(over_cores(2, 0, 1) + wide(d2))
    sum_3 = low(over_cores(3, 1, 1))
    sum_1, sum_2, sum_3, e1, e2, sent = lax.optimization_barrier(
        (sum_1, sum_2, sum_3, e1, e2, sent)
    )
    from_core = send(sent, to_core, "in_c")
    f1 = send(sum_1, to_x, "f1")
    f2 = send(sum_2, to_y, "f2")
    q_grad, k_grad, v_grad, sum_3, from_core = lax.optimization_barrier(
        (q_grad, k_grad, v_grad, sum_3, from_core)
    )
    d3 = send(sum_3, to_x, "d3")
    e3 = send(after(low(over_cores(3, 1, 0)), f1), to_x, "e3")

    rows = stream.reshape(1024, D)
    w_grads = [low(product_inner(rows, grad)) for grad in (q_grad, k_grad, v_grad)]
    rest = jnp.zeros((PIECE - 1552, 256), jnp.bfloat16)
    piece_0 = jnp.concatenate([w_grads[0], w_grads[1][:528], rest])
    piece_1 = jnp.concatenate([w_grads[1][512:], w_grads[2], rest, rest[:16]])
    low_row = y == 0
    other_row = jnp.where(low_row, piece_1, piece_0)
    ry0 = send(other_row, to_y, "ry0")
    kept_1, sent_1 = combine(
        after(place, other_row, sum_3), (grads_own[1], moved[2], e2, f2), (grads_own[0], moved[1], e1, f1)
    )
    got_inner = send(sent_1, to_near, "rz_inner1")
    inner_part = low(add(kept_1, got_inner))
    inner_last = send(inner_part, only(to_far, (0, 3)), "rz_inner2")
    f3 = send(low(over_cores(3, 0, 1) + wide(after(d3, ry0))), to_y, "f3")
    kept_0, sent_0 = combine(
        after(place, inner_part), (jnp.where(low_row, piece_0, piece_1), ry0), (grads_own[2], moved[3], e3, f3)
    )
    outer_part = low(add(kept_0, send(after(sent_0, inner_last), to_near, "rz_outer1")))
    outer_last = send(outer_part, only(to_far, (1, 2)), "rz_outer2")

    in_x = send(after(low(kept[1] + wide(from_core[1])), e3), to_x, "in_x")
    input_grad = (
        resid_grad
        + kept[0]
        + wide(from_core[0])
        + wide(in_x)
    )

    time_grad = sums[6] + sums_qkv[0]
    rows_of = [sums[0], sums[1]]
    vec_grad = jnp.concatenate(
        [
            jnp.where(here, sums_qkv[1:3, :256][None], 0.0),
            sums[0:2].reshape(2, 4, 256).transpose(1, 0, 2),
            sums_up.reshape(4, 4, 256),
            sums[2:6].reshape(4, 4, 256).transpose(1, 0, 2),
            (time_frac * time_grad).reshape(4, 1, 256),
            time_grad.reshape(4, 1, 256),
            jnp.zeros((4, 2, 256), jnp.float32),
            jnp.where(jnp.arange(4096).reshape(1, 16, 256) < 896, head_grad, 0.0),
        ],
        axis=1,
    )
    vec_grad = vec_grad.reshape(2, 2, 32, 256)
    core_bit, x_bit = j % 2, j // 2
    kept_c = jnp.where(core_bit == 1, vec_grad[:, 1], vec_grad[:, 0])
    sent_c = jnp.where(core_bit == 1, vec_grad[:, 0], vec_grad[:, 1])
    by_x = kept_c + send(sent_c, to_core, "vec_c")
    kept_x = jnp.where(x_bit == 1, by_x[1], by_x[0])
    mine = kept_x + send(jnp.where(x_bit == 1, by_x[0], by_x[1]), to_x, "vec_x")

    grad_flat, square = unpack(after(place, input_grad), inner_part, inner_last, outer_part, outer_last)
    mine = jnp.concatenate([mine, square])
    mine = mine + send(mine, to_y, "norm")
    mine = together(mine, (to_near, to_far, to_opposite))
    vec_sum, head_sum = mine[:14].reshape(-1), mine[16:20].reshape(-1)[:896]
    vector_grad = vec_sum
    is_sum = jnp.arange(40)[:, None] >= 32
    square_sum = jnp.sum(jnp.where(is_sum, mine, mine * mine))
    square_sum = jnp.broadcast_to(square_sum, (8, 128))
    grad_flat = grad_flat.reshape(-1)
    edge = grad_flat[SHARD - 3584 : SHARD]
    edge = jnp.where(
        shard == 7,
        vec_sum,
        jnp.where(shard == 1, jnp.concatenate([edge[: 3584 - 896], head_sum]), edge),
    )
    grad_shard = lax.dynamic_update_slice(grad_flat, edge, (SHARD - 3584,))
    square_sum = together(square_sum, (to_core, to_x, to_relative(3)), grad_shard)
    grad_shard = grad_shard[:SHARD]
    grad_norm = jnp.sqrt(square_sum[0, 0])
    clip_limit = 4.0 * math.sqrt(PARAMS)
    clipped = grad_shard * (clip_limit / jnp.maximum(grad_norm, clip_limit))
    new_first = 0.9 * first_moment + 0.1 * clipped
    new_second = 0.98 * second_moment + 0.02 * clipped * clipped
    first_hat = new_first / (1.0 - 0.9**STEP)
    second_hat = new_second / (1.0 - 0.98**STEP)
    new_master = master - 0.02 * (first_hat / (jnp.sqrt(second_hat) + 1e-06) + 0.01 * master)
    new_average = 0.99 * average + 0.01 * new_master
    return (
        block_out,
        input_grad,
        grad_norm,
        vector_grad,
        new_first,
        new_second,
        new_master,
        new_average,
    )


def solution(mesh):
    return jax.shard_map(
        block_body if mesh.shape["dp"] == 8 and mesh.shape["fsdp"] == 4 else body,
        mesh=mesh,
        in_specs=(
            P(("dp", "fsdp"), None),
            P(("dp", "fsdp"), None),
            P(("dp", "fsdp")),
            P(("dp", "fsdp")),
            P(("dp", "fsdp")),
            P(("dp", "fsdp")),
            P("dp"),
            P("dp"),
            P("dp"),
        ),
        out_specs=(
            P(("dp", "fsdp"), None),
            P(("dp", "fsdp"), None),
            P(),
            P("fsdp"),
            P(("dp", "fsdp")),
            P(("dp", "fsdp")),
            P(("dp", "fsdp")),
            P(("dp", "fsdp")),
        ),
        check_vma=False,
    )
```
